32 devices in a mesh: dp: 8 (over y, x, core), mp: 4 (over z).
Axes of the slice: x: 2, y: 2, z: 4, core: 2. Of those that a mesh axis runs over, the one named last changes fastest.
Arguments:
- layer_in: bfloat16 [8192, 2048], P(('dp', 'mp')), may hold values from -6 to 6
- first_gain: bfloat16 [2048], replicated, may hold values from 0.5 to 1.5
- first_bias: bfloat16 [2048], replicated, may hold values from -1.75 to 1.75
- w_qkv: bfloat16 [2048, 3, 2048], P(None, None, 'mp'), may hold values from -0.125 to 0.125
- a_qkv: bfloat16 [2048, 8, 16], replicated, may hold values from -0.125 to 0.125
- b_qkv: bfloat16 [8, 16, 3, 2048], P(None, None, None, 'mp'), may hold values from -1.5 to 1.5
- w_dense: bfloat16 [2048, 2048], P('mp'), may hold values from -0.375 to 0.375
- a_dense: bfloat16 [2048, 8, 16], P('mp'), may hold values from -0.375 to 0.375
- b_dense: bfloat16 [8, 16, 2048], replicated, may hold values from -1.5 to 1.5
- second_gain: bfloat16 [2048], replicated, may hold values from 0.5 to 1.5
- second_bias: bfloat16 [2048], replicated, may hold values from -1.75 to 1.75
- w_up: bfloat16 [2048, 8192], P(None, 'mp'), may hold values from -0.125 to 0.125
- a_up: bfloat16 [2048, 8, 16], replicated, may hold values from -0.125 to 0.125
- b_up: bfloat16 [8, 16, 8192], P(None, None, 'mp'), may hold values from -1.5 to 1.5
- w_down: bfloat16 [8192, 2048], P('mp'), may hold values from -0.0625 to 0.0625
- a_down: bfloat16 [8192, 8, 16], P('mp'), may hold values from -0.0625 to 0.0625
- b_down: bfloat16 [8, 16, 2048], replicated, may hold values from -1.5 to 1.5
- segment_ids: int32 [8, 1024], P('dp'), may hold values from 0 to 7, never falling along the last dimension, each value on 1 to 512 neighbouring positions
- adapter_ids: int32 [8], P('dp'), may hold values from 0 to 7, as said below
- cotangent: bfloat16 [8192, 2048], P(('dp', 'mp')), may hold values from -6 to 6
Outputs:
- layer_out: bfloat16 [8192, 2048], P(('dp', 'mp'))
- input_grad: bfloat16 [8192, 2048], P(('dp', 'mp'))
- grad_a_qkv: float32 [2048, 8, 16], replicated
- grad_b_qkv: float32 [8, 16, 3, 2048], P(None, None, None, 'mp')
- grad_a_dense: float32 [2048, 8, 16], P('mp')
- grad_b_dense: float32 [8, 16, 2048], replicated
- grad_a_up: float32 [2048, 8, 16], replicated
- grad_b_up: float32 [8, 16, 8192], P(None, None, 'mp')
- grad_a_down: float32 [8192, 8, 16], P('mp')
- grad_b_down: float32 [8, 16, 2048], replicated
The draws below stay inside these ranges and needn't reach their ends.
Inputs may be any that keep to these rules, and one draw needn't show every extreme that they name: `adapter_ids`: every one of the 8 adapters is used by at least one sequence.
All inputs are finite; a program needn't handle non-finite values.
Results may differ from the reference program's by a relative error of at most 0.023.
Values may be sent and summed in bfloat16 or wider, within the bound.
No kernel may reach another device: no remote copies, remote signals or barrier semaphores. Data moves between devices by JAX's collectives and lax.ppermute only.
A program may use at most 256 MiB of HBM per device.

```python
import math
import jax
import jax.numpy as jnp
import numpy as np
from jax import lax

D = 2048
HEADS = 32
HD = 64
FF = 8192
RANK = 16
ADAPTERS = 8
LEN = 1024
NSEQ = 8
TOKENS = 8192
DOCS = 8
MOST = 512


def draw_adapter_ids(key, part):
    first_key = jax.random.fold_in(key, 11)
    extra_key = jax.random.fold_in(key, 12)
    order_key = jax.random.fold_in(key, 13)
    covering = jax.random.permutation(first_key, ADAPTERS).astype(jnp.int32)
    extras = jax.random.randint(extra_key, (NSEQ - ADAPTERS,), 0, ADAPTERS).astype(jnp.int32)
    joined = jnp.concatenate([covering, extras])
    return jax.random.permutation(order_key, joined).astype(jnp.int32)


def level_of(own_key, dims, split, least, largest):
    def one(position, shards_of):
        draws = jax.random.uniform(jax.random.fold_in(jax.random.fold_in(own_key, 6), position), (shards_of,), jnp.float32, least / len(split), largest / len(split))
        return jnp.repeat(jnp.exp(draws), dims[position] // shards_of).reshape((-1,) + (1,) * (len(dims) - position - 1))

    level = one(*split[0])
    for cut in split[1:]:
        level = level * one(*cut)
    return level


def split_up(count, total, reach, skew):
    weights = [(1 << 20) // math.isqrt(grade ** skew) + 1 for grade in range(2, count + 1)]
    spare, holding = total - reach - (count - 1), [1] * (count - 1)
    while spare > 0:
        candidates = [i for i in range(count - 1) if holding[i] < reach]
        pool, remaining = sum([weights[i] for i in candidates]), spare
        for i in candidates:
            addition = min(reach - holding[i], max(1, remaining * weights[i] // pool), spare)
            holding[i] = holding[i] + addition
            spare = spare - addition
    return np.array([reach] + holding)


def ragged(rng, count, total, most, lean):
    if count == 2:
        one = jax.random.randint(rng, (), max(1, total - most), min(most, total - 1) + 1)
        return jnp.stack([one, total - one])
    tallies = jnp.asarray(split_up(count, total, most, lean), jnp.int32)
    twos = (count - 1) // 2
    donor, sink = tallies[1:1 + 2 * twos:2], tallies[2:2 + 2 * twos:2]
    margin = jnp.minimum(donor - 1, most - sink)
    passed = jax.random.randint(jax.random.fold_in(rng, 1), (twos,), 0, 1 << 20) % (margin + 1)
    tallies = tallies.at[1:1 + 2 * twos:2].set(donor - passed).at[2:2 + 2 * twos:2].set(sink + passed)
    return tallies[jax.random.permutation(jax.random.fold_in(rng, 2), count)]


def noise(own_key, extent, scale, most, shards=(), held_as=jnp.bfloat16):
    level = level_of(own_key, extent, shards, -0.22, 0.18) if shards else 1.0
    values = jax.random.normal(own_key, extent, jnp.float32) * scale * level
    return jnp.minimum(jnp.maximum(values, -most), most).astype(held_as)


def setup_inputs(seed: int = 0) -> dict:
    splits = jax.random.split(jax.random.key(seed), 21)
    layer_in = noise(splits[0], (TOKENS, D), 1.0, 6.0, ((0, 32),))
    first_gain = jnp.clip(1.0 + 0.1 * jax.random.normal(splits[1], (D,), jnp.float32), 0.5, 1.5).astype(jnp.bfloat16)
    first_bias = noise(splits[2], (D,), 0.3, 1.75)
    w_qkv = noise(splits[3], (D, 3, D), D ** -0.5, 0.125, ((2, 4),))
    a_qkv = noise(splits[4], (D, ADAPTERS, RANK), D ** -0.5, 0.125)
    b_qkv = noise(splits[5], (ADAPTERS, RANK, 3, D), RANK ** -0.5, 1.5, ((3, 4),))
    w_dense = noise(splits[6], (D, D), (D // 8) ** -0.5, 0.375, ((0, 4),))
    a_dense = noise(splits[7], (D, ADAPTERS, RANK), (D // 8) ** -0.5, 0.375, ((0, 4),))
    b_dense = noise(splits[8], (ADAPTERS, RANK, D), RANK ** -0.5, 1.5)
    second_gain = jnp.clip(1.0 + 0.1 * jax.random.normal(splits[9], (D,), jnp.float32), 0.5, 1.5).astype(jnp.bfloat16)
    second_bias = noise(splits[10], (D,), 0.3, 1.75)
    w_up = noise(splits[11], (D, FF), D ** -0.5, 0.125, ((1, 4),))
    a_up = noise(splits[12], (D, ADAPTERS, RANK), D ** -0.5, 0.125)
    b_up = noise(splits[13], (ADAPTERS, RANK, FF), RANK ** -0.5, 1.5, ((2, 4),))
    w_down = noise(splits[14], (FF, D), FF ** -0.5, 0.0625, ((0, 4),))
    a_down = noise(splits[15], (FF, ADAPTERS, RANK), FF ** -0.5, 0.0625, ((0, 4),))
    b_down = noise(splits[16], (ADAPTERS, RANK, D), RANK ** -0.5, 1.5)
    segment_ids = jax.vmap(lambda own: jnp.searchsorted(jnp.cumsum(ragged(own, DOCS, LEN, MOST, 2)), jnp.arange(LEN), side="right"))(jax.random.split(splits[17], NSEQ)).reshape((NSEQ, LEN)).astype(jnp.int32)
    adapter_ids = draw_adapter_ids(jax.random.fold_in(splits[20], 71), 0)
    cotangent = noise(splits[19], (TOKENS, D), 1.0, 6.0, ((0, 32),))
    return {"layer_in": layer_in, "first_gain": first_gain, "first_bias": first_bias, "w_qkv": w_qkv, "a_qkv": a_qkv, "b_qkv": b_qkv, "w_dense": w_dense, "a_dense": a_dense, "b_dense": b_dense, "second_gain": second_gain, "second_bias": second_bias, "w_up": w_up, "a_up": a_up, "b_up": b_up, "w_down": w_down, "a_down": a_down, "b_down": b_down, "segment_ids": segment_ids, "adapter_ids": adapter_ids, "cotangent": cotangent}


@jax.custom_vjp
def low(v):
    return lax.optimization_barrier(v.astype(jnp.bfloat16)).astype(jnp.float32)

@jax.custom_vjp
def low_back(v):
    return v

def low_keep(v):
    return (low(v), None)

def low_pass(kept, grad):
    return (grad,)

def back_keep(v):
    return (v, None)

def back_low(kept, grad):
    return (low(grad),)
low.defvjp(low_keep, low_pass)
low_back.defvjp(back_keep, back_low)
highest = lax.Precision.HIGHEST
EPSILON = 1e-05

def matmul(left, right):
    return jnp.dot(left, right, precision=highest)

def layer_norm(values, gain, bias):
    center = lax.optimization_barrier(jnp.mean(values, -1, keepdims=True))
    centred = values - center
    variance = lax.optimization_barrier(jnp.mean(centred * centred, -1, keepdims=True))
    return centred * lax.rsqrt(variance + EPSILON) * gain + bias

def attention(queries, key_rows, val_rows, segment_row):
    block = min(512, LEN)
    count = LEN // block
    scale = HD ** (-0.5)
    head_ids = jnp.arange(HEADS, dtype=jnp.float32)
    slopes = jnp.exp2(-8.0 * (head_ids + 1.0) / HEADS)
    positions = jnp.arange(LEN, dtype=jnp.int32)

    def one_block(block_idx):
        start = (block_idx * block).astype(jnp.int32)
        query_block = lax.dynamic_slice_in_dim(queries, start, block, 0)
        query_pos = start + jnp.arange(block, dtype=jnp.int32)
        query_seg = lax.dynamic_slice_in_dim(segment_row, start, block, 0)
        scores = jnp.einsum('qhd,khd->hqk', query_block, key_rows, precision=highest) * scale
        offsets = (positions[None, :] - query_pos[:, None]).astype(jnp.float32)
        scores = scores + slopes[:, None, None] * offsets[None]
        scores = low_back(scores)
        allowed = (positions[None, :] <= query_pos[:, None]) & (segment_row[None, :] == query_seg[:, None])
        scores = jnp.where(allowed[None], scores, -1e+30)
        top = lax.optimization_barrier(jnp.max(scores, -1, keepdims=True))
        weights = jnp.exp(scores - top)
        weights = weights / lax.optimization_barrier(jnp.sum(weights, -1, keepdims=True))
        return jnp.einsum('hqk,khd->qhd', low(weights), val_rows, precision=highest)
    blocks = lax.map(jax.checkpoint(one_block), jnp.arange(count, dtype=jnp.int32))
    return blocks.reshape(LEN, D)

def layer(block_in, adapters, frozen, segment_row, which):
    a_qkv, b_qkv, a_dense, b_dense, a_up, b_up, a_down, b_down = adapters
    first_gain, first_bias, w_qkv, w_dense, second_gain, second_bias, w_up, w_down = frozen
    normed = low(layer_norm(block_in, first_gain, first_bias))
    z_qkv = low(low_back(matmul(normed, a_qkv[:, which, :])))
    merged = matmul(normed, w_qkv.reshape(D, 3 * D)) + matmul(z_qkv, b_qkv[which].reshape(RANK, 3 * D))
    merged = low(low_back(merged)).reshape(LEN, 3, HEADS, HD)
    mixed = attention(merged[:, 0], merged[:, 1], merged[:, 2], segment_row)
    mixed = low(low_back(mixed))
    z_dense = low(low_back(matmul(mixed, a_dense[:, which, :])))
    branch = matmul(mixed, w_dense) + matmul(z_dense, b_dense[which])
    middle = block_in + low_back(branch)
    normed_two = low(layer_norm(middle, second_gain, second_bias))
    z_up = low(low_back(matmul(normed_two, a_up[:, which, :])))
    hidden = low_back(matmul(normed_two, w_up) + matmul(z_up, b_up[which]))
    active = low(jax.nn.gelu(hidden, approximate=False))
    z_down = low(low_back(matmul(active, a_down[:, which, :])))
    return middle + matmul(active, w_down) + matmul(z_down, b_down[which])

def widen(value):
    return value.astype(jnp.float32)

def reference(layer_in, first_gain, first_bias, w_qkv, a_qkv, b_qkv, w_dense, a_dense, b_dense, second_gain, second_bias, w_up, a_up, b_up, w_down, a_down, b_down, segment_ids, adapter_ids, cotangent):
    frozen = (widen(first_gain), widen(first_bias), widen(w_qkv), widen(w_dense), widen(second_gain), widen(second_bias), widen(w_up), widen(w_down))
    adapters = (widen(a_qkv), widen(b_qkv), widen(a_dense), widen(b_dense), widen(a_up), widen(b_up), widen(a_down), widen(b_down))
    inputs = widen(layer_in).reshape(NSEQ, LEN, D)
    cots = widen(cotangent).reshape(NSEQ, LEN, D)

    def one_sequence(totals, item):
        seq_in, seq_cot, segment_row, which = item

        def forward(block_in, adapter_set):
            return layer(block_in, adapter_set, frozen, segment_row, which)
        result, pullback = jax.vjp(forward, seq_in, adapters)
        grad_in, grad_set = pullback(seq_cot)
        totals = jax.tree.map(jnp.add, totals, grad_set)
        return (totals, (result.astype(jnp.bfloat16), grad_in.astype(jnp.bfloat16)))
    zeros = jax.tree.map(jnp.zeros_like, adapters)
    totals, outputs = lax.scan(one_sequence, zeros, (inputs, cots, segment_ids, adapter_ids))
    return (outputs[0].reshape(TOKENS, D), outputs[1].reshape(TOKENS, D), totals[0], totals[1], totals[2], totals[3], totals[4], totals[5], totals[6], totals[7])
```

```python
import functools

import jax
import jax.numpy as jnp
from jax import lax
from jax.experimental import pallas as pl
from jax.experimental.pallas import tpu as pltpu
from jax.sharding import PartitionSpec as P

HEADS = 32
HD = 64
LONGEST = 512
EPSILON = 1e-05
F32 = jnp.float32
BF16 = jnp.bfloat16
MASKED = -1e30


def layer_norm(values, gain, bias):
    center = jnp.mean(values, -1, keepdims=True)
    centred = values - center
    variance = jnp.mean(centred * centred, -1, keepdims=True)
    scaler = lax.rsqrt(variance + EPSILON)
    normal = centred * scaler
    return (normal * gain.astype(F32) + bias.astype(F32), normal, scaler)


def norm_back(grad, normal, scaler, gain):
    scaled = grad * gain.astype(F32)
    first_mean = jnp.mean(scaled, -1, keepdims=True)
    second_mean = jnp.mean(scaled * normal, -1, keepdims=True)
    return (scaled - first_mean - normal * second_mean) * scaler


def dot_nn(left, right):
    return jnp.dot(left, right, preferred_element_type=F32)


def dot_nt(left, right):
    return lax.dot_general(left, right, (((1,), (1,)), ((), ())), preferred_element_type=F32)


def dot_tn(left, right):
    return lax.dot_general(left, right, (((0,), (0,)), ((), ())), preferred_element_type=F32)


def swap(value, axis, bit):
    pairs = [(i, i ^ bit) for i in range(lax.axis_size(axis))]
    return lax.ppermute(value, axis, pairs)


def gather_four(value):
    one = swap(value, "mp", 1)
    two = swap(value, "mp", 2)
    three = swap(two, "mp", 1)
    return [value, one, two, three]


def scatter_four(parts):
    relay = swap(parts[3].astype(BF16), "mp", 1)
    pair = (parts[2].astype(F32) + relay.astype(F32)).astype(BF16)
    far = swap(pair, "mp", 2)
    near = swap(parts[1].astype(BF16), "mp", 1)
    return parts[0].astype(F32) + near.astype(F32) + far.astype(F32)


def place(blocks, index):
    rows = blocks[0].shape[0]
    whole = jnp.zeros((rows * len(blocks),) + blocks[0].shape[1:], blocks[0].dtype)
    for offset, block in enumerate(blocks):
        whole = lax.dynamic_update_slice_in_dim(whole, block, (index ^ offset) * rows, 0)
    return whole


def lane_mask(half):
    return (lax.broadcasted_iota(jnp.int32, (1, 2 * HD), 1) // HD) == half


def pair_scores(keys, query, seg_col, seg_row, slope, apart):
    rows, cols = keys.shape[0], query.shape[0]
    raw = dot_nt(keys, query)
    delta = (
        lax.broadcasted_iota(jnp.int32, (rows, cols), 0)
        - lax.broadcasted_iota(jnp.int32, (rows, cols), 1)
        - apart
    )
    allowed = seg_col == seg_row
    if apart == 0:
        allowed = allowed & (delta <= 0)
    return jnp.where(allowed, raw + slope * delta.astype(F32), MASKED)


def reach_of(block):
    return -(-LONGEST // block)


def forward_kernel(block, seg_ref, slope_ref, col_ref, row_ref, q_ref, k_ref, v_ref, o_ref, stat_ref,
                   turned_ref, top_ref, total_ref, sum_ref):
    head = pl.program_id(0)
    half = lax.rem(head, 2)
    slope = slope_ref[head]
    count = q_ref.shape[0] // block
    mask = lane_mask(half)
    base = half * HD

    @pl.when(half == 0)
    def _():
        turned_ref[...] = v_ref[...].T

    for i in range(count):
        queries = pl.ds(i * block, block)
        scaled = jnp.where(mask, q_ref[queries, :] * HD ** -0.5, 0).astype(BF16)
        row = row_ref[:, queries]

        def one(j, first):
            keys = pl.ds(j * block, block)
            scores = pair_scores(k_ref[keys, :], scaled, col_ref[keys, :1], row, slope, (i - j) * block)
            best = jnp.max(scores, 0, keepdims=True)
            if not first:
                best = jnp.maximum(best, top_ref[...])
            weights = jnp.exp(scores - best)
            total = jnp.sum(weights, 0, keepdims=True)
            rows = pl.ds(pl.multiple_of(base, HD), HD)
            result = dot_nn(turned_ref[rows, keys], weights.astype(BF16))
            if not first:
                fade = jnp.exp(top_ref[...] - best)
                total = total + fade * total_ref[...]
                result = result + fade * sum_ref[...]
            top_ref[...] = best
            total_ref[...] = total
            sum_ref[...] = result

        one(i, True)
        for back in range(1, min(i, reach_of(block)) + 1):
            j = i - back

            @pl.when(seg_ref[j * block + block - 1] == seg_ref[i * block])
            def _(j=j):
                one(j, False)

        stat_ref[0, :, queries] = jnp.broadcast_to(top_ref[...] + jnp.log(total_ref[...]), (8, block))
        done = (sum_ref[...] / total_ref[...]).T
        both = jnp.concatenate([done, done], 1)
        kept = o_ref[queries, :]
        o_ref[queries, :] = jnp.where(mask, both, kept.astype(F32)).astype(BF16)


def attention_forward(query, key, val, seg, slopes):
    rows, width = query.shape
    block = min(256, rows)
    wide = pl.BlockSpec((rows, 2 * HD), lambda h, *_: (0, h // 2))
    col = jnp.broadcast_to(seg[:, None], (rows, 128))
    return pl.pallas_call(
        functools.partial(forward_kernel, block),
        out_shape=(
            jax.ShapeDtypeStruct((rows, width), BF16),
            jax.ShapeDtypeStruct((width // HD, 8, rows), F32),
        ),
        grid_spec=pltpu.PrefetchScalarGridSpec(
            num_scalar_prefetch=2,
            grid=(width // HD,),
            in_specs=[
                pl.BlockSpec((rows, 128), lambda h, *_: (0, 0)),
                pl.BlockSpec((1, rows), lambda h, *_: (0, 0)),
                wide, wide, wide,
            ],
            out_specs=(wide, pl.BlockSpec((1, 8, rows), lambda h, *_: (h, 0, 0))),
            scratch_shapes=[
                pltpu.VMEM((2 * HD, rows), BF16),
                pltpu.VMEM((1, block), F32),
                pltpu.VMEM((1, block), F32),
                pltpu.VMEM((HD, block), F32),
            ],
        ),
        name="attention_forward",
    )(seg, slopes, col, seg[None, :], query, key, val)


def backward_kernel(block, seg_ref, slope_ref, col_ref, row_ref, stat_ref, center_ref, q_ref, k_ref, v_ref, g_ref,
                    dq_ref, dk_ref, dv_ref, turned_ref, qsum_ref, ksum_ref, vsum_ref):
    head = pl.program_id(0)
    half = lax.rem(head, 2)
    slope = slope_ref[head]
    count = q_ref.shape[0] // block
    mask = lane_mask(half)
    base = half * HD
    rows = pl.ds(pl.multiple_of(base, HD), HD)

    @pl.when(half == 0)
    def _():
        turned_ref[...] = k_ref[...].T
        qsum_ref[...] = jnp.zeros_like(qsum_ref)
        ksum_ref[...] = jnp.zeros_like(ksum_ref)
        vsum_ref[...] = jnp.zeros_like(vsum_ref)

    for i in range(count):
        queries = pl.ds(i * block, block)
        scaled = jnp.where(mask, q_ref[queries, :] * HD ** -0.5, 0).astype(BF16)
        grads = jnp.where(mask, g_ref[queries, :], 0).astype(BF16)
        row = row_ref[:, queries]

        def one(j):
            keys = pl.ds(j * block, block)
            scores = pair_scores(k_ref[keys, :], scaled, col_ref[keys, :1], row, slope, (i - j) * block)
            probs = jnp.exp(scores - stat_ref[0, :1, queries])
            d_probs = dot_nt(v_ref[keys, :], grads)
            d_scores = (probs * (d_probs - center_ref[0, :1, queries])).astype(BF16)
            vsum_ref[keys, :] += dot_nn(probs.astype(BF16), grads)
            ksum_ref[keys, :] += dot_nn(d_scores, scaled)
            qsum_ref[rows, queries] += dot_nn(turned_ref[rows, keys], d_scores)

        one(i)
        for back in range(1, min(i, reach_of(block)) + 1):
            j = i - back

            @pl.when(seg_ref[j * block + block - 1] == seg_ref[i * block])
            def _(j=j):
                one(j)

    @pl.when(half == 1)
    def _():
        dq_ref[...] = (qsum_ref[...] * HD ** -0.5).T.astype(BF16)
        dk_ref[...] = ksum_ref[...].astype(BF16)
        dv_ref[...] = vsum_ref[...].astype(BF16)


def attention_backward(query, key, val, grad, stat, center, seg, slopes):
    rows, width = query.shape
    block = min(256, rows)
    wide = pl.BlockSpec((rows, 2 * HD), lambda h, *_: (0, h // 2))
    thin = pl.BlockSpec((1, 8, rows), lambda h, *_: (h, 0, 0))
    col = jnp.broadcast_to(seg[:, None], (rows, 128))
    return pl.pallas_call(
        functools.partial(backward_kernel, block),
        out_shape=(jax.ShapeDtypeStruct((rows, width), BF16),) * 3,
        grid_spec=pltpu.PrefetchScalarGridSpec(
            num_scalar_prefetch=2,
            grid=(width // HD,),
            in_specs=[
                pl.BlockSpec((rows, 128), lambda h, *_: (0, 0)),
                pl.BlockSpec((1, rows), lambda h, *_: (0, 0)),
                thin, thin, wide, wide, wide, wide,
            ],
            out_specs=(wide, wide, wide),
            scratch_shapes=[
                pltpu.VMEM((2 * HD, rows), BF16),
                pltpu.VMEM((2 * HD, rows), F32),
                pltpu.VMEM((rows, 2 * HD), F32),
                pltpu.VMEM((rows, 2 * HD), F32),
            ],
        ),
        name="attention_backward",
    )(seg, slopes, col, seg[None, :], stat, center, query, key, val, grad)


def gelu_pair(values):
    below = 0.5 * (1.0 + lax.erf(values * 0.5 ** 0.5))
    density = jnp.exp(values * values * -0.5) * 0.3989422804014327
    return values * below, below + values * density


def turned(factor, which):
    return lax.dynamic_index_in_dim(factor.transpose(1, 2, 0), which, 0, False)


def local(
    layer_in, first_gain, first_bias, w_qkv, a_qkv, b_qkv, w_dense, a_dense, b_dense, second_gain, second_bias,
    w_up, a_up, b_up, w_down, a_down, b_down, segment_ids, adapter_ids, cotangent,
):
    own_rows, width = layer_in.shape
    kinds = a_qkv.shape[1]
    rank = a_qkv.shape[2]
    local_width = w_dense.shape[0]
    local_ff = w_up.shape[1]
    local_heads = local_width // HD
    index = lax.axis_index("mp")
    spot = lax.axis_index("dp")
    copies = lax.axis_size("dp")
    pair_rows = 2 * own_rows
    low, high = index & 1, index >> 1
    which = adapter_ids[0]
    seg = segment_ids[0]
    head_ids = (index * local_heads + lax.iota(jnp.int32, local_heads)).astype(F32)
    slopes = jnp.exp2(-8.0 * (head_ids + 1.0) / HEADS)

    aq, ad, au, an = (turned(a, which) for a in (a_qkv, a_dense, a_up, a_down))
    bq = lax.dynamic_index_in_dim(b_qkv.transpose(0, 2, 1, 3), which, 0, False)
    bd, bu, bn = (lax.dynamic_index_in_dim(b, which, 0, False) for b in (b_dense, b_up, b_down))

    blocks = gather_four(layer_in)
    ad_parts = gather_four(ad)
    bu_far, an_far = swap(bu, "mp", 2), swap(an, "mp", 2)

    def slice_of(weight):
        size = weight.shape[0] // copies
        return lax.dynamic_slice_in_dim(weight, spot * size, size, 0)

    wd_slices = gather_four(slice_of(w_dense))
    wd = [w_dense] + [lax.all_gather(s, "dp", axis=0, tiled=True) for s in wd_slices[1:]]
    wu_far = lax.all_gather(swap(slice_of(w_up), "mp", 2), "dp", axis=0, tiled=True)
    wn_far = lax.all_gather(swap(slice_of(w_down), "mp", 2), "dp", axis=0, tiled=True)

    rows_all = place(blocks, index)
    normed_all = layer_norm(rows_all.astype(F32), first_gain, first_bias)[0].astype(BF16)
    wq = w_qkv.transpose(1, 0, 2)
    z_qkv = dot_nt(normed_all, aq).astype(BF16)
    query, key, val = (
        (dot_nn(normed_all, wq[i]) + dot_nn(z_qkv, bq[i])).astype(BF16) for i in range(3)
    )
    mixed, stat = attention_forward(query, key, val, seg, slopes)

    mine = lax.dynamic_slice_in_dim(mixed, high * pair_rows, pair_rows, 0)
    other = lax.dynamic_slice_in_dim(mixed, (1 - high) * pair_rows, pair_rows, 0)
    m_one = swap(mine, "mp", 1)
    m_two = swap(other, "mp", 2)
    m_three = swap(m_two, "mp", 1)
    m_parts = [mine, m_one, m_two, m_three]
    z_dense = sum(dot_nt(m, a) for m, a in zip(m_parts, ad_parts)).astype(BF16)
    branch = sum(dot_nn(m, w) for m, w in zip(m_parts, wd)) + dot_nn(z_dense, bd)
    rows_pair = lax.dynamic_slice_in_dim(rows_all, high * pair_rows, pair_rows, 0)
    middle = rows_pair.astype(F32) + branch
    second, normal_two, scaler_two = layer_norm(middle, second_gain, second_bias)
    second = second.astype(BF16)

    def own(value):
        return lax.dynamic_slice_in_dim(value, low * own_rows, own_rows, 0)

    def partner(value):
        return lax.dynamic_slice_in_dim(value, (1 - low) * own_rows, own_rows, 0)

    cot_pair = place([cotangent, swap(cotangent, "mp", 1)], low)
    z_up = dot_nt(second, au).astype(BF16)
    dz_down = dot_nt(cot_pair, bn).astype(BF16)
    down_part, d_second_part, z_down, dz_up, ga_down, gb_up = 0.0, 0.0, 0.0, 0.0, [], []
    for up, bup, down, adown in ((w_up, bu, w_down, an), (wu_far, bu_far, wn_far, an_far)):
        hidden = dot_nn(second, up) + dot_nn(z_up, bup)
        active, slope = gelu_pair(hidden)
        active = active.astype(BF16)
        d_active = dot_nt(cot_pair, down) + dot_nn(dz_down, adown)
        d_hidden = (d_active * slope).astype(BF16)
        d_second_part += dot_nt(d_hidden, up)
        dz_up += dot_nt(d_hidden, bup)
        down_part += dot_nn(active, down)
        z_down += dot_nt(active, adown)
        ga_down.append(dot_tn(dz_down, active))
        gb_up.append(dot_tn(z_up, d_hidden))
    dz_up, z_down = dz_up.astype(BF16), z_down.astype(BF16)
    d_second_part = d_second_part + dot_nn(dz_up, au)
    down_part = down_part + dot_nn(z_down, bn)
    d_second = own(d_second_part) + swap(partner(d_second_part).astype(BF16), "mp", 1).astype(F32)
    mlp = own(down_part) + swap(partner(down_part).astype(BF16), "mp", 1).astype(F32)
    layer_out = (own(middle) + mlp).astype(BF16)
    ga_up = dot_tn(dz_up, second)
    gb_down = dot_tn(z_down, cot_pair)
    ga_down = ga_down[0] + swap(ga_down[1].astype(BF16), "mp", 2).astype(F32)
    gb_up = gb_up[0] + swap(gb_up[1].astype(BF16), "mp", 2).astype(F32)

    d_middle = cotangent.astype(F32) + norm_back(d_second, own(normal_two), own(scaler_two), second_gain)
    middle_low = d_middle.astype(BF16)
    gb_dense = dot_tn(own(z_dense), middle_low)
    dz_dense = dot_nt(middle_low, bd).astype(BF16)
    ga_dense = [dot_tn(dz_dense, own(m)) for m in m_parts]
    d_mixed = [
        (dot_nt(middle_low, w) + dot_nn(dz_dense, a)).astype(BF16) for w, a in zip(wd, ad_parts)
    ]
    d_mixed = place([d_mixed[0]] + [swap(d_mixed[r], "mp", r) for r in (1, 2, 3)], index)

    center = jnp.einsum(
        "thd,thd->ht",
        d_mixed.astype(F32).reshape(-1, local_heads, HD),
        mixed.astype(F32).reshape(-1, local_heads, HD),
    )
    center = jnp.broadcast_to(center[:, None, :], stat.shape)
    d_parts = attention_backward(query, key, val, d_mixed, stat, center, seg, slopes)
    gb_qkv = [dot_tn(z_qkv, d) for d in d_parts]
    dz_qkv = sum(dot_nt(d, b) for d, b in zip(d_parts, (bq[0], bq[1], bq[2]))).astype(BF16)
    ga_qkv = dot_tn(dz_qkv, normed_all)
    d_first_part = sum(dot_nt(d, wq[i]) for i, d in enumerate(d_parts)) + dot_nn(dz_qkv, aq)
    d_first = scatter_four([
        lax.dynamic_slice_in_dim(d_first_part, (index ^ r) * own_rows, own_rows, 0) for r in range(4)
    ])
    normal_one, scaler_one = layer_norm(layer_in.astype(F32), first_gain, first_bias)[1:]
    input_grad = (d_middle + norm_back(d_first, normal_one, scaler_one, first_gain)).astype(BF16)

    quarter = width // 4
    full = jnp.concatenate([ga_qkv, gb_dense, ga_up, gb_down], 0)
    full = scatter_four([
        lax.dynamic_slice_in_dim(full, (index ^ r) * quarter, quarter, 1) for r in range(4)
    ])
    full = place(gather_four(full.astype(BF16)[None]), index)
    ga_dense = scatter_four(ga_dense)
    shard = jnp.concatenate([*gb_qkv, ga_dense, gb_up, ga_down], 1)
    packed = jnp.concatenate([
        full.reshape(-1, 128), shard.astype(BF16).reshape(-1, 128),
        jnp.full((16, 128), which, BF16),
    ], 0)
    packed = lax.all_gather(packed, "dp", axis=0)
    ids = packed[:, -1, 0]
    choice = (ids[None, :] == lax.iota(jnp.int32, kinds).astype(BF16)[:, None]).astype(BF16)

    def spread(first, count, *shape):
        part = lax.slice_in_dim(packed, first // 128, (first + count) // 128, axis=1).reshape(copies, -1)
        return dot_nn(choice, part).reshape(kinds, *shape)

    size = 4 * rank * width
    full = spread(0, size, 4, 4, rank, quarter)
    ga_qkv, gb_dense, ga_up, gb_down = (
        full[:, :, i].transpose(0, 2, 1, 3).reshape(kinds, rank, width) for i in range(4)
    )
    shard = spread(size, rank * (4 * local_width + 2 * local_ff), rank, -1)
    gb_qkv = shard[:, :, : 3 * local_width].reshape(kinds, rank, 3, local_width)
    ga_dense = shard[:, :, 3 * local_width : 4 * local_width]
    gb_up = shard[:, :, 4 * local_width : 4 * local_width + local_ff]
    ga_down = shard[:, :, 4 * local_width + local_ff :]
    return (
        layer_out,
        input_grad,
        ga_qkv.transpose(2, 0, 1),
        gb_qkv,
        ga_dense.transpose(2, 0, 1),
        gb_dense,
        ga_up.transpose(2, 0, 1),
        gb_up,
        ga_down.transpose(2, 0, 1),
        gb_down,
    )


def solution(mesh):
    return jax.shard_map(
        local,
        mesh=mesh,
        in_specs=(
            P(("dp", "mp"), None), P(), P(), P(None, None, "mp"), P(), P(None, None, None, "mp"), P("mp", None),
            P("mp", None, None), P(), P(), P(), P(None, "mp"), P(), P(None, None, "mp"), P("mp", None),
            P("mp", None, None), P(), P("dp", None), P("dp"), P(("dp", "mp"), None),
        ),
        out_specs=(
            P(("dp", "mp"), None), P(("dp", "mp"), None), P(), P(None, None, None, "mp"), P("mp", None, None), P(),
            P(), P(None, None, "mp"), P("mp", None, None), P(),
        ),
        check_vma=False,
    )
```

```python
import functools

import jax
import jax.numpy as jnp
from jax import lax
from jax.experimental import pallas as pl
from jax.experimental.pallas import tpu as pltpu
from jax.sharding import PartitionSpec as P

HEADS = 32
HD = 64
LONGEST = 512
EPSILON = 1e-05
F32 = jnp.float32
BF16 = jnp.bfloat16
MASKED = -1e30
WHOLE = pl.BlockSpec(memory_space=pltpu.VMEM)
REMOTE = pl.BlockSpec(memory_space=pl.ANY)


def shape(dims, kind=BF16):
    return jax.ShapeDtypeStruct(dims, kind)


def statistics(values):
    center = jnp.mean(values, -1, keepdims=True)
    centred = values - center
    variance = jnp.mean(centred * centred, -1, keepdims=True)
    scaler = lax.rsqrt(variance + EPSILON)
    return centred * scaler, scaler


def layer_norm(values, gain, bias):
    return statistics(values)[0] * gain.astype(F32) + bias.astype(F32)


def norm_back(grad, values, gain):
    normal, scaler = statistics(values)
    scaled = grad * gain.astype(F32)
    first_mean = jnp.mean(scaled, -1, keepdims=True)
    second_mean = jnp.mean(scaled * normal, -1, keepdims=True)
    return (scaled - first_mean - normal * second_mean) * scaler


def by_rows(count, body, chunk=32):
    for i in range(count // chunk):
        body(slice(i * chunk, (i + 1) * chunk))


def dot_nn(left, right):
    return jnp.dot(left, right, preferred_element_type=F32)


def dot_nt(left, right):
    return lax.dot_general(left, right, (((1,), (1,)), ((), ())), preferred_element_type=F32)


def dot_tn(left, right):
    return lax.dot_general(left, right, (((0,), (0,)), ((), ())), preferred_element_type=F32)


def swap(value, axis, bit):
    pairs = [(i, i ^ bit) for i in range(lax.axis_size(axis))]
    return lax.ppermute(value, axis, pairs)


def after(value, *others):
    return lax.optimization_barrier((value, *others))[0]


def gelu_pair(values):
    below = 0.5 * (1.0 + lax.erf(values * 0.5 ** 0.5))
    density = jnp.exp(values * values * -0.5) * 0.3989422804014327
    return values * below, below + values * density


def project_kernel(kept, at_ref, x_ref, gain_ref, bias_ref, aq_ref, bq_ref, wq_ref, *refs):
    merged_ref, normed_ref, z_ref, w_ref, out_ref, low_ref, thin_ref, sems, loads = refs[kept:]
    count = x_ref.shape[0]
    weights = [pltpu.make_async_copy(wq_ref.at[i], w_ref.at[i], loads.at[i]) for i in range(wq_ref.shape[0])]
    for copy in weights:
        copy.start()
    rows = pl.ds(pl.multiple_of(at_ref[0] * count, count), count)

    def norm(part):
        low_ref[part, :] = layer_norm(x_ref[part, :].astype(F32), gain_ref[...], bias_ref[...]).astype(BF16)

    by_rows(count, norm)
    normed = low_ref[...]
    copies = [pltpu.make_async_copy(low_ref, normed_ref.at[rows, :], sems.at[0])]
    copies[0].start()
    inner = dot_nt(normed, aq_ref[...]).astype(BF16)
    thin_ref[...] = inner
    copies.append(pltpu.make_async_copy(thin_ref, z_ref.at[rows, :], sems.at[1]))
    copies[1].start()
    for i in range(wq_ref.shape[0]):
        weights[i].wait()
        out_ref[i] = (dot_nn(normed, w_ref[i]) + dot_nn(inner, bq_ref[i])).astype(BF16)
        copies.append(pltpu.make_async_copy(out_ref.at[i], merged_ref.at[i, rows, :], sems.at[2 + i]))
        copies[-1].start()
    for copy in copies:
        copy.wait()


def project(at, rows, gain, bias, aq, bq, wq, total, earlier):
    count, width = rows.shape
    parts, _, local_width = wq.shape
    rank = aq.shape[0]
    kept = len(earlier)
    return pl.pallas_call(
        functools.partial(project_kernel, kept),
        out_shape=(shape((parts, total, local_width)), shape((total, width)), shape((total, rank))),
        grid_spec=pltpu.PrefetchScalarGridSpec(
            num_scalar_prefetch=1,
            grid=(),
            in_specs=[WHOLE] * 5 + [REMOTE] * (1 + kept),
            out_specs=(REMOTE,) * 3,
            scratch_shapes=[
                pltpu.VMEM(wq.shape, BF16),
                pltpu.VMEM((parts, count, local_width), BF16),
                pltpu.VMEM((count, width), BF16),
                pltpu.VMEM((count, rank), BF16),
                pltpu.SemaphoreType.DMA((2 + parts,)),
                pltpu.SemaphoreType.DMA((parts,)),
            ],
        ),
        input_output_aliases={7 + i: i for i in range(kept)},
        name="project",
    )(at.reshape(1), rows, gain, bias, aq, bq, wq, *earlier)


def lane_mask(half):
    return (lax.broadcasted_iota(jnp.int32, (1, 2 * HD), 1) // HD) == half


def pair_scores(keys, query, seg_col, seg_row, slope, apart):
    rows, cols = keys.shape[0], query.shape[0]
    raw = dot_nt(keys, query)
    delta = (
        lax.broadcasted_iota(jnp.int32, (rows, cols), 0)
        - lax.broadcasted_iota(jnp.int32, (rows, cols), 1)
        - apart
    )
    allowed = seg_col == seg_row
    if apart == 0:
        allowed = allowed & (delta <= 0)
    return jnp.where(allowed, raw + slope * delta.astype(F32), MASKED)


def reach_of(block):
    return -(-LONGEST // block)


def attend_kernel(block, count, first_ref, seg_ref, slope_ref, col_ref, row_ref, q_ref, k_ref, v_ref,
                  o_ref, stat_ref, turned_ref, top_ref, total_ref, sum_ref):
    head = pl.program_id(0)
    half = lax.rem(head, 2)
    slope = slope_ref[head]
    mask = lane_mask(half)
    heads_rows = pl.ds(pl.multiple_of(half * HD, HD), HD)

    @pl.when(half == 0)
    def _():
        turned_ref[...] = v_ref[0].T

    for own in range(count):
        i = first_ref[0] + own
        start = pl.multiple_of(i * block, block)
        here = pl.ds(own * block, block)
        scaled = jnp.where(mask, q_ref[0, pl.ds(start, block), :] * HD ** -0.5, 0).astype(BF16)
        row = row_ref[:, pl.ds(start, block)]

        def one(back):
            at = pl.multiple_of(start - back * block, block)
            keys = pl.ds(at, block)
            scores = pair_scores(k_ref[0, keys, :], scaled, col_ref[keys, :1], row, slope, back * block)
            best = jnp.max(scores, 0, keepdims=True)
            if back:
                best = jnp.maximum(best, top_ref[...])
            weights = jnp.exp(scores - best)
            total = jnp.sum(weights, 0, keepdims=True)
            result = dot_nn(turned_ref[heads_rows, keys], weights.astype(BF16))
            if back:
                fade = jnp.exp(top_ref[...] - best)
                total = total + fade * total_ref[...]
                result = result + fade * sum_ref[...]
            top_ref[...] = best
            total_ref[...] = total
            sum_ref[...] = result

        one(0)
        for back in range(1, reach_of(block) + 1):
            last = jnp.maximum(start - (back - 1) * block - 1, 0)

            @pl.when((i >= back) & (seg_ref[last] == seg_ref[start]))
            def _(back=back):
                one(back)

        stat_ref[0, :, here] = top_ref[...] + jnp.log(total_ref[...])
        done = (sum_ref[...] / total_ref[...]).T
        both = jnp.concatenate([done, done], 1)
        o_ref[here, :] = jnp.where(mask, both, o_ref[here, :].astype(F32)).astype(BF16)


def attend(first, merged, seg, slopes, count):
    _, rows, width = merged.shape
    block = min(256, rows)
    heads = width // HD
    col = jnp.broadcast_to(seg[:, None], (rows, 128))

    def part(i):
        return pl.BlockSpec((1, rows, 2 * HD), lambda h, *_: (i, 0, h // 2))

    return pl.pallas_call(
        functools.partial(attend_kernel, block, count),
        out_shape=(shape((count * block, width)), shape((heads, 1, count * block), F32)),
        grid_spec=pltpu.PrefetchScalarGridSpec(
            num_scalar_prefetch=3,
            grid=(heads,),
            in_specs=[
                pl.BlockSpec((rows, 128), lambda h, *_: (0, 0)),
                pl.BlockSpec((1, rows), lambda h, *_: (0, 0)),
                part(0), part(1), part(2),
            ],
            out_specs=(
                pl.BlockSpec((count * block, 2 * HD), lambda h, *_: (0, h // 2)),
                pl.BlockSpec((1, 1, count * block), lambda h, *_: (h, 0, 0)),
            ),
            scratch_shapes=[
                pltpu.VMEM((2 * HD, rows), BF16),
                pltpu.VMEM((1, block), F32),
                pltpu.VMEM((1, block), F32),
                pltpu.VMEM((HD, block), F32),
            ],
        ),
        name="attend",
    )(first.reshape(1), seg, slopes, col, seg[None, :], merged, merged, merged)


def attend_back_kernel(block, seg_ref, slope_ref, col_ref, row_ref, stat_ref, m_ref, g_ref, q_ref, k_ref, v_ref,
                       d_ref, turned_ref, center_ref, qsum_ref, ksum_ref, vsum_ref):
    head = pl.program_id(0)
    half = lax.rem(head, 2)
    slope = slope_ref[head]
    count = g_ref.shape[0] // block
    mask = lane_mask(half)
    rows = pl.ds(pl.multiple_of(half * HD, HD), HD)

    @pl.when(half == 0)
    def _():
        turned_ref[...] = k_ref[0].T
        product = (g_ref[...].astype(F32) * m_ref[...].astype(F32)).T
        center_ref[0:1] = jnp.sum(product[:HD], 0, keepdims=True)
        center_ref[1:2] = jnp.sum(product[HD:], 0, keepdims=True)
        qsum_ref[...] = jnp.zeros_like(qsum_ref)
        ksum_ref[...] = jnp.zeros_like(ksum_ref)
        vsum_ref[...] = jnp.zeros_like(vsum_ref)

    for i in range(count):
        queries = pl.ds(i * block, block)
        scaled = jnp.where(mask, q_ref[0, queries, :] * HD ** -0.5, 0).astype(BF16)
        grads = jnp.where(mask, g_ref[queries, :], 0).astype(BF16)
        row = row_ref[:, queries]

        def one(j):
            keys = pl.ds(j * block, block)
            scores = pair_scores(k_ref[0, keys, :], scaled, col_ref[keys, :1], row, slope, (i - j) * block)
            probs = jnp.exp(scores - stat_ref[0, :, queries])
            d_probs = dot_nt(v_ref[0, keys, :], grads)
            d_scores = (probs * (d_probs - center_ref[pl.ds(half, 1), queries])).astype(BF16)
            vsum_ref[keys, :] += dot_nn(probs.astype(BF16), grads)
            ksum_ref[keys, :] += dot_nn(d_scores, scaled)
            qsum_ref[rows, queries] += dot_nn(turned_ref[rows, keys], d_scores)

        one(i)
        for back in range(1, min(i, reach_of(block)) + 1):
            j = i - back

            @pl.when(seg_ref[j * block + block - 1] == seg_ref[i * block])
            def _(j=j):
                one(j)

    @pl.when(half == 1)
    def _():
        d_ref[0] = (qsum_ref[...] * HD ** -0.5).T.astype(BF16)
        d_ref[1] = ksum_ref[...].astype(BF16)
        d_ref[2] = vsum_ref[...].astype(BF16)


def attend_back(merged, mixed, grad, stat, seg, slopes):
    parts, rows, width = merged.shape
    block = min(256, rows)
    wide = pl.BlockSpec((rows, 2 * HD), lambda h, *_: (0, h // 2))
    col = jnp.broadcast_to(seg[:, None], (rows, 128))

    def part(i):
        return pl.BlockSpec((1, rows, 2 * HD), lambda h, *_: (i, 0, h // 2))

    return pl.pallas_call(
        functools.partial(attend_back_kernel, block),
        out_shape=shape(merged.shape),
        grid_spec=pltpu.PrefetchScalarGridSpec(
            num_scalar_prefetch=2,
            grid=(width // HD,),
            in_specs=[
                pl.BlockSpec((rows, 128), lambda h, *_: (0, 0)),
                pl.BlockSpec((1, rows), lambda h, *_: (0, 0)),
                pl.BlockSpec((1, 1, rows), lambda h, *_: (h, 0, 0)),
                wide, wide, part(0), part(1), part(2),
            ],
            out_specs=pl.BlockSpec((parts, rows, 2 * HD), lambda h, *_: (0, 0, h // 2)),
            scratch_shapes=[
                pltpu.VMEM((2 * HD, rows), BF16),
                pltpu.VMEM((2, rows), F32),
                pltpu.VMEM((2 * HD, rows), F32),
                pltpu.VMEM((rows, 2 * HD), F32),
                pltpu.VMEM((rows, 2 * HD), F32),
            ],
        ),
        name="attend_back",
    )(seg, slopes, col, seg[None, :], stat, mixed, grad, merged, merged, merged)


def dense_kernel(at_ref, x0_ref, x1_ref, m0_ref, m1_ref, m2_ref, m3_ref, a_ref, bd_ref, gain_ref, bias_ref, au_ref,
                 own_ref, far_ref, middle_ref, second_ref, zd_ref, zu_ref, w_ref, m_ref, loads):
    size = m0_ref.shape[1]
    count = x0_ref.shape[0]
    width = x0_ref.shape[1]
    pieces, _, thick, _ = far_ref.shape
    copies = [pltpu.make_async_copy(own_ref.reshape(pieces, thick, width), w_ref.at[0], loads.at[0])]
    copies += [pltpu.make_async_copy(far_ref.at[:, r], w_ref.at[1 + r], loads.at[1 + r]) for r in range(3)]
    for copy in copies:
        copy.start()
    for r, m in enumerate((m0_ref, m1_ref, m2_ref, m3_ref)):
        m_ref[:, r * size:(r + 1) * size] = m[...]
    inner = dot_nt(m_ref[...], a_ref[...]).astype(BF16)
    zd_ref[...] = inner
    for copy in copies:
        copy.wait()
    weights = w_ref[...].reshape(4 * size, width)
    swapped = at_ref[0] == 1
    tile = min(512, width)
    for i in range(2):
        rows = slice(i * count, (i + 1) * count)
        near, away = (x0_ref, x1_ref) if i == 0 else (x1_ref, x0_ref)
        for j in range(width // tile):
            cols = slice(j * tile, (j + 1) * tile)
            x = jnp.where(swapped, away[:, cols], near[:, cols]).astype(F32)
            middle_ref[rows, cols] = x + dot_nn(m_ref[rows, :], weights[:, cols]) + dot_nn(inner[rows], bd_ref[:, cols])

    def norm(part):
        second_ref[part, :] = layer_norm(middle_ref[part, :], gain_ref[...], bias_ref[...]).astype(BF16)

    by_rows(2 * count, norm)
    zu_ref[...] = dot_nt(second_ref[...], au_ref[...]).astype(BF16)


def dense(low, x_own, x_far, m_parts, ad, bd, gain, bias, au, w_own, w_far):
    count, width = x_own.shape
    rank = ad.shape[0]
    return pl.pallas_call(
        dense_kernel,
        out_shape=(
            shape((2 * count, width), F32), shape((2 * count, width)), shape((2 * count, rank)),
            shape((2 * count, rank)),
        ),
        in_specs=[pl.BlockSpec(memory_space=pltpu.SMEM)] + [WHOLE] * 11 + [REMOTE] * 2,
        out_specs=(WHOLE,) * 4,
        scratch_shapes=[
            pltpu.VMEM((4, w_far.shape[0]) + w_far.shape[2:], BF16), pltpu.VMEM((2 * count, width), BF16),
            pltpu.SemaphoreType.DMA((4,)),
        ],
        name="dense",
    )(low.reshape(1), x_own, x_far, *m_parts, ad, bd, gain, bias, au, w_own, w_far)


def feed_kernel(earlier, at_ref, x_ref, g_ref, up_ref, down_ref, zu_ref, dz_ref, bu_ref, an_ref, au_ref, *refs):
    step = pl.program_id(0)
    total_ref, inner_ref = refs[-2:]
    if earlier:
        before_ref, active_ref, hidden_ref, dz_out_ref, out_ref = refs[:-2]
    else:
        active_ref, hidden_ref, dz_out_ref, out_ref = refs[:-2]

    @pl.when(step == 0)
    def _():
        total_ref[...] = before_ref[...] if earlier else jnp.zeros_like(total_ref)
        inner_ref[...] = jnp.zeros_like(inner_ref)

    hidden = dot_nn(x_ref[...], up_ref[...]) + dot_nn(zu_ref[...], bu_ref[...])
    d_active = dot_nt(g_ref[...], down_ref[...]) + dot_nn(dz_ref[...], an_ref[...])
    active, slope = gelu_pair(hidden)
    active_ref[...] = active.astype(BF16)
    d_hidden = (d_active * slope).astype(BF16)
    hidden_ref[...] = d_hidden
    total_ref[...] += dot_nt(d_hidden, up_ref[...])
    inner_ref[...] += dot_nt(d_hidden, bu_ref[...])

    @pl.when(step == pl.num_programs(0) - 1)
    def _():
        inner = inner_ref[...].astype(BF16)
        dz_out_ref[...] = inner
        out_ref[...] = (total_ref[...] + dot_nn(inner, au_ref[...])).astype(out_ref.dtype)


def feed(at, count, x, g, up, down, zu, dz, bu, an, au, before, kind):
    width = x.shape[1]
    ff = up.shape[1]
    tile = min(512, ff)
    rank = bu.shape[0]
    earlier = before is not None
    once = pl.Buffered(1)
    rows = pl.BlockSpec((count, width), lambda t, at: (at[0], 0), pipeline_mode=once)
    thin = pl.BlockSpec((count, rank), lambda t, at: (at[0], 0))
    cols = pl.BlockSpec((count, tile), lambda t, at: (0, t))
    row = pl.BlockSpec((rank, tile), lambda t, at: (0, t))
    return pl.pallas_call(
        functools.partial(feed_kernel, earlier),
        out_shape=(shape((count, ff)), shape((count, ff)), shape((count, rank)), shape((count, width), kind)),
        grid_spec=pltpu.PrefetchScalarGridSpec(
            num_scalar_prefetch=1,
            grid=(ff // tile,),
            in_specs=[
                rows, rows, pl.BlockSpec((width, tile), lambda t, at: (0, t)),
                pl.BlockSpec((tile, width), lambda t, at: (t, 0)), thin, thin, row, row,
                pl.BlockSpec((rank, width), lambda t, at: (0, 0)),
            ] + [rows] * earlier,
            out_specs=(
                cols, cols, pl.BlockSpec((count, rank), lambda t, at: (0, 0)),
                pl.BlockSpec((count, width), lambda t, at: (0, 0), pipeline_mode=once),
            ),
            scratch_shapes=[pltpu.VMEM((count, width), F32), pltpu.VMEM((count, rank), F32)],
        ),
        name="feed",
    )(at.reshape(1), x, g, up, down, zu, dz, bu, an, au, *((before,) if earlier else ()))


def emit_kernel(earlier, at_ref, *refs):
    parts = 2 if earlier else 1
    step = pl.program_id(0)
    total_ref, inner_ref = refs[-2:]
    actives, hiddens, zs, ds = (refs[i * parts:(i + 1) * parts] for i in range(4))
    down_ref, an_ref, bn_ref = refs[4 * parts:4 * parts + 3]
    outs = refs[4 * parts + 3:-2]
    if earlier:
        befores, outs = outs[:2], outs[2:]
    gn_ref, gu_ref, z_ref = outs[:3]
    count = actives[0].shape[0]
    gn, gu = 0.0, 0.0
    for i in range(parts):
        rows = slice(i * count, (i + 1) * count)

        @pl.when(step == 0)
        def _():
            total_ref[rows] = befores[i][...] if earlier else jnp.zeros((count, total_ref.shape[1]), F32)
            inner_ref[rows] = jnp.zeros((count, inner_ref.shape[1]), F32)

        active = actives[i][...]
        total_ref[rows] += dot_nn(active, down_ref[...])
        inner_ref[rows] += dot_nt(active, an_ref[...])
        gn = gn + dot_tn(ds[i][...], active)
        gu = gu + dot_tn(zs[i][...], hiddens[i][...])
    gn_ref[...] = gn.astype(BF16)
    gu_ref[...] = gu.astype(BF16)

    @pl.when(step == pl.num_programs(0) - 1)
    def _():
        inner = inner_ref[...].astype(BF16)
        z_ref[...] = inner
        for i in range(parts):
            rows = slice(i * count, (i + 1) * count)
            out = outs[3 + i]
            out[...] = (total_ref[rows] + dot_nn(inner[rows], bn_ref[...])).astype(out.dtype)


def emit(low, actives, hiddens, down, an, bn, zu, dz, before):
    parts = len(actives)
    count, ff = actives[0].shape
    width = down.shape[1]
    tile = min(512, ff)
    rank = an.shape[0]
    earlier = before is not None
    once = pl.Buffered(1)
    places = (lambda at: 1 - at[0], lambda at: at[0]) if earlier else (lambda at: 0,)
    cols = pl.BlockSpec((count, tile), lambda t, at: (0, t))
    row = pl.BlockSpec((rank, tile), lambda t, at: (0, t))
    thin = [pl.BlockSpec((count, rank), lambda t, at, p=p: (p(at), 0)) for p in places]
    wide = [pl.BlockSpec((count, width), lambda t, at, p=p: (p(at), 0), pipeline_mode=once) for p in places]
    kinds = (BF16, F32) if earlier else (F32,)
    return pl.pallas_call(
        functools.partial(emit_kernel, earlier),
        out_shape=(
            shape((rank, ff)), shape((rank, ff)), shape((parts * count, rank)),
        ) + tuple(shape((count, width), k) for k in kinds),
        grid_spec=pltpu.PrefetchScalarGridSpec(
            num_scalar_prefetch=1,
            grid=(ff // tile,),
            in_specs=[cols] * (2 * parts) + thin * 2 + [
                pl.BlockSpec((tile, width), lambda t, at: (t, 0)), row,
                pl.BlockSpec((rank, width), lambda t, at: (0, 0)),
            ] + wide * earlier,
            out_specs=(
                row, row, pl.BlockSpec((parts * count, rank), lambda t, at: (0, 0)),
            ) + (pl.BlockSpec((count, width), lambda t, at: (0, 0), pipeline_mode=once),) * parts,
            scratch_shapes=[pltpu.VMEM((parts * count, width), F32), pltpu.VMEM((parts * count, rank), F32)],
        ),
        name="emit",
    )(low.reshape(1), *actives, *hiddens, *([zu] * parts), *([dz] * parts), down, an, bn, *([before] * parts * earlier))


def dense_back_kernel(low_ref, own_ref, far_ref, cot_ref, gain_ref, bd_ref, ad_ref, middle_ref, w0_ref, w1_ref,
                      d_ref, low_out_ref, dz_ref, mixed_ref, mid_ref, w_ref, loads):
    count, width = own_ref.shape
    size = mixed_ref.shape[2]
    pieces, _, thick, _ = w1_ref.shape
    rows = pl.ds(pl.multiple_of(low_ref[0] * count, count), count)
    first = pltpu.make_async_copy(middle_ref.at[rows, :], mid_ref, loads.at[4])
    first.start()
    copies = [pltpu.make_async_copy(w0_ref.reshape(pieces, thick, width), w_ref.at[0], loads.at[0])]
    copies += [pltpu.make_async_copy(w1_ref.at[:, r], w_ref.at[1 + r], loads.at[1 + r]) for r in range(3)]
    order = (3, 2, 1, 0)
    for r in order:
        copies[r].start()
    first.wait()

    def norm(part):
        grad = own_ref[part, :] + far_ref[part, :].astype(F32)
        d_middle = cot_ref[part, :].astype(F32) + norm_back(grad, mid_ref[part, :], gain_ref[...])
        d_ref[part, :] = d_middle
        low_out_ref[part, :] = d_middle.astype(BF16)

    by_rows(count, norm)
    low = low_out_ref[...]
    inner = dot_nt(low, bd_ref[...]).astype(BF16)
    dz_ref[...] = inner
    for r in order:
        copies[r].wait()
        cols = slice(r * size, (r + 1) * size)
        weights = w_ref[r].reshape(size, width)
        mixed_ref[r] = (dot_nt(low, weights) + dot_nn(inner, ad_ref[:, cols])).astype(BF16)


def dense_back(low, own, far, middle, cot, gain, bd, ad, w_own, w_far):
    count, width = own.shape
    rank = bd.shape[0]
    return pl.pallas_call(
        dense_back_kernel,
        out_shape=(shape((count, width), F32), shape((count, width)), shape((count, rank)), shape((4, count, width // 4))),
        in_specs=[pl.BlockSpec(memory_space=pltpu.SMEM)] + [WHOLE] * 6 + [REMOTE] * 3,
        out_specs=(WHOLE,) * 4,
        scratch_shapes=[
            pltpu.VMEM((count, width), F32), pltpu.VMEM((4, w_far.shape[0]) + w_far.shape[2:], BF16),
            pltpu.SemaphoreType.DMA((5,)),
        ],
        name="dense_back",
    )(low.reshape(1), own, far, cot, gain, bd, ad, middle, w_own, w_far)


def project_back_kernel(order, at_ref, aq_ref, bq_ref, d_ref, wq_ref, *refs):
    outs, part_ref, w_ref, sems, loads = refs[:-4], *refs[-4:]
    count = outs[0].shape[0]

    def fetch(place):
        rows = pl.ds(pl.multiple_of((at_ref[0] ^ order[place]) * count, count), count)
        return pltpu.make_async_copy(d_ref.at[:, rows, :], part_ref.at[place], sems.at[place])

    blocks = [fetch(place) for place in range(len(order))]
    weights = [pltpu.make_async_copy(wq_ref.at[i], w_ref.at[i], loads.at[i]) for i in range(3)]
    blocks[0].start()
    for copy in weights + blocks[1:]:
        copy.start()
    for place, out in enumerate(outs):
        blocks[place].wait()
        parts = [part_ref[place, i] for i in range(3)]
        inner = sum(dot_nt(d, bq_ref[i]) for i, d in enumerate(parts)).astype(BF16)
        total = dot_nn(inner, aq_ref[...])
        for i in range(3):
            if place == 0:
                weights[i].wait()
            total = total + dot_nt(parts[i], w_ref[i])
        out[...] = total.astype(out.dtype)


def project_back(at, d_merged, wq, aq, bq, order, kinds):
    parts, total, local_width = d_merged.shape
    width = wq.shape[1]
    count = total // 4
    return pl.pallas_call(
        functools.partial(project_back_kernel, order),
        out_shape=tuple(shape((count, width), k) for k in kinds),
        in_specs=[pl.BlockSpec(memory_space=pltpu.SMEM)] + [WHOLE] * 2 + [REMOTE] * 2,
        out_specs=(WHOLE,) * len(order),
        scratch_shapes=[
            pltpu.VMEM((len(order), parts, count, local_width), BF16), pltpu.VMEM(wq.shape, BF16),
            pltpu.SemaphoreType.DMA((len(order),)), pltpu.SemaphoreType.DMA((3,)),
        ],
        name="project_back",
    )(at.reshape(1), aq, bq, d_merged, wq)


def inner_kernel(d_ref, z_ref, n_ref, bq_ref, ga_ref, gb_ref):
    step = pl.program_id(0)

    @pl.when(step == 0)
    def _():
        ga_ref[...] = jnp.zeros_like(ga_ref)
        gb_ref[...] = jnp.zeros_like(gb_ref)

    inner = sum(dot_nt(d_ref[i], bq_ref[i]) for i in range(3)).astype(BF16)
    ga_ref[...] += dot_tn(inner, n_ref[...])
    width = d_ref.shape[2]
    for i in range(3):
        gb_ref[:, i * width:(i + 1) * width] += dot_tn(z_ref[...], d_ref[i])


def inner_grads(d_merged, z_qkv, normed, bq):
    parts, total, local_width = d_merged.shape
    width = normed.shape[1]
    rank = z_qkv.shape[1]
    count = total // 2
    return pl.pallas_call(
        inner_kernel,
        out_shape=(shape((rank, width), F32), shape((rank, parts * local_width), F32)),
        grid=(2,),
        in_specs=[
            pl.BlockSpec((parts, count, local_width), lambda i: (0, i, 0)),
            pl.BlockSpec((count, rank), lambda i: (i, 0)),
            pl.BlockSpec((count, width), lambda i: (i, 0)),
            pl.BlockSpec(bq.shape, lambda i: (0, 0, 0)),
        ],
        out_specs=(
            pl.BlockSpec((rank, width), lambda i: (0, 0)),
            pl.BlockSpec((rank, parts * local_width), lambda i: (0, 0)),
        ),
        name="inner_grads",
    )(d_merged, z_qkv, normed, bq)


def spread_kernel(ids_ref, first_ref, second_ref, *outs):
    step = pl.program_id(0)

    @pl.when(step == 0)
    def _():
        for out in outs:
            out[...] = jnp.zeros_like(out)

    which = ids_ref[step]
    ga_up, gb_down, gb_dense, gb_up, ga_down, ga_dense, ga_qkv, gb_qkv = outs
    at = 0
    for out in (ga_up, gb_down, gb_dense, gb_up, ga_down, ga_dense):
        size = out.shape[2]
        out[which] += first_ref[0, :, at:at + size].astype(F32)
        at += size
    size = ga_qkv.shape[2]
    ga_qkv[which] += second_ref[0, :, :size].astype(F32)
    local_width = gb_qkv.shape[3]
    for i in range(3):
        gb_qkv[which, i] += second_ref[0, :, size + i * local_width:size + (i + 1) * local_width].astype(F32)


def spread(ids, first, second, kinds, width, local_width, local_ff):
    copies, rank, _ = first.shape
    dims = [(kinds, rank, n) for n in (width, width, width, local_ff, local_ff, local_width, width)]
    dims.append((kinds, 3, rank, local_width))
    return pl.pallas_call(
        spread_kernel,
        out_shape=tuple(shape(d, F32) for d in dims),
        grid_spec=pltpu.PrefetchScalarGridSpec(
            num_scalar_prefetch=1,
            grid=(copies,),
            in_specs=[
                pl.BlockSpec((1,) + first.shape[1:], lambda s, _: (s, 0, 0)),
                pl.BlockSpec((1,) + second.shape[1:], lambda s, _: (s, 0, 0)),
            ],
            out_specs=tuple(
                pl.BlockSpec(d, lambda s, _, n=len(d): (0,) * n, pipeline_mode=pl.Buffered(1)) for d in dims
            ),
        ),
        name="spread",
    )(ids, first, second)


def turned(factor, which):
    return lax.dynamic_index_in_dim(factor.transpose(1, 2, 0), which, 0, False)


def local(
    layer_in, first_gain, first_bias, w_qkv, a_qkv, b_qkv, w_dense, a_dense, b_dense, second_gain, second_bias,
    w_up, a_up, b_up, w_down, a_down, b_down, segment_ids, adapter_ids, cotangent,
):
    own_rows, width = layer_in.shape
    kinds = a_qkv.shape[1]
    rank = a_qkv.shape[2]
    local_width = w_dense.shape[0]
    local_ff = w_up.shape[1]
    local_heads = local_width // HD
    index = lax.axis_index("mp")
    spot = lax.axis_index("dp")
    copies = lax.axis_size("dp")
    total_rows = 4 * own_rows
    low, high = index & 1, index >> 1
    which = adapter_ids[0]
    seg = segment_ids[0]
    head_ids = (index * local_heads + lax.iota(jnp.int32, local_heads)).astype(F32)
    slopes = jnp.exp2(-8.0 * (head_ids + 1.0) / HEADS)
    first_gain, first_bias, second_gain, second_bias = (
        v[None, :] for v in (first_gain, first_bias, second_gain, second_bias)
    )

    aq, ad, au, an = (turned(a, which) for a in (a_qkv, a_dense, a_up, a_down))
    bq = lax.dynamic_index_in_dim(b_qkv.transpose(0, 2, 1, 3), which, 0, False)
    bd, bu, bn = (lax.dynamic_index_in_dim(b, which, 0, False) for b in (b_dense, b_up, b_down))
    wq = w_qkv.transpose(1, 0, 2)

    def slice_of(weight):
        size = weight.shape[0] // copies
        return lax.dynamic_slice_in_dim(weight, spot * size, size, 0)

    x_one = swap(layer_in, "mp", 1)
    x_two = swap(layer_in, "mp", 2)
    wd_slice = slice_of(w_dense)
    size = wd_slice.shape[0]
    ad_flat = ad.reshape(-1, width)
    last = size + ad_flat.shape[0]
    tail = jnp.concatenate([wd_slice, ad_flat], 0)

    def step_in(r, block, held):
        return project(index ^ r, block, first_gain, first_bias, aq, bq, wq, total_rows, held)

    held = step_in(0, layer_in, ())
    wu_halves = jnp.split(slice_of(w_up), 2, axis=0)
    x_one, x_two, *held = lax.optimization_barrier((x_one, x_two, *held))

    x_three = swap(x_two, "mp", 1)
    pack_two = swap(after(jnp.concatenate([tail, bu, an], 0), x_one), "mp", 2)
    wu_first = swap(after(wu_halves[0], x_one), "mp", 2)
    held = step_in(1, x_one, held)
    held = step_in(2, x_two, held)
    x_three, pack_two, wu_first, *held = lax.optimization_barrier((x_three, pack_two, wu_first, *held))

    pack_one = swap(jnp.concatenate([tail, pack_two[:last]], 0), "mp", 1)
    wu_second = swap(after(wu_halves[1], x_three), "mp", 2)
    held = step_in(3, x_three, held)
    merged, normed, z_qkv = held
    other, stat_other = attend(2 * (1 - high), merged, seg, slopes, 2)
    other, pack_one, pack_two, wu_first, wu_second, merged = lax.optimization_barrier(
        (other, pack_one, pack_two, wu_first, wu_second, merged)
    )

    m_two = swap(other, "mp", 2)
    bu_far, an_far = pack_two[last:last + rank], pack_two[last + rank:]
    packs = (pack_one[:last], pack_two, pack_one[last:])
    wd_slices = jnp.concatenate([p[:size] for p in packs], 0)
    wd_far = lax.all_gather(wd_slices, "dp", axis=0).reshape(copies, 3, size, width)
    ad = jnp.concatenate([ad] + [p[size:last].reshape(rank, local_width) for p in packs], 1)
    wu_slice = after(jnp.concatenate([wu_first, wu_second], 0), wd_slices)
    wu_far = lax.all_gather(wu_slice, "dp", axis=0, tiled=True)
    mine, stat_mine = attend(2 * high, merged, seg, slopes, 2)
    m_two, mine = lax.optimization_barrier((m_two, mine))

    m_one = swap(mine, "mp", 1)
    m_three = swap(m_two, "mp", 1)
    wn_halves = jnp.split(after(slice_of(w_down), m_two), 2, axis=0)
    wn_first = swap(wn_halves[0], "mp", 2)
    m_one, m_three, wn_first = lax.optimization_barrier((m_one, m_three, wn_first))

    m_parts = [mine, m_one, m_two, m_three]
    cot_far = swap(after(cotangent, m_one), "mp", 1)
    wn_second = swap(after(wn_halves[1], m_one), "mp", 2)

    def pair(own, far):
        return jnp.where(low == 0, jnp.concatenate([own, far], 0), jnp.concatenate([far, own], 0))

    middle, second, z_dense, z_up = dense(
        low, layer_in, x_one, m_parts, ad, bd, second_gain, second_bias, au, w_dense, wd_far
    )
    wn_second, second, cot_far = lax.optimization_barrier((wn_second, second, cot_far))
    wn_far = lax.all_gather(jnp.concatenate([wn_first, wn_second], 0), "dp", axis=0, tiled=True)

    cot_pair = pair(cotangent, cot_far)
    dz_down = dot_nt(cot_pair, bn).astype(BF16)
    zero = jnp.zeros((), jnp.int32)
    act, dh, dzu, so_far = feed(
        zero, 2 * own_rows, second, cot_pair, w_up, w_down, z_up, dz_down, bu, an, au, None, F32
    )
    gn_own, gu_own, zn, out_so_far = emit(zero, (act,), (dh,), w_down, an, bn, z_up, dz_down, None)
    out_so_far, so_far = lax.optimization_barrier((out_so_far, so_far))
    far_args = (second, cot_pair, wu_far, wn_far, z_up, dz_down, bu_far, an_far, au, so_far)
    act_a, dh_a, dzu_a, d_send = feed(1 - low, own_rows, *far_args, BF16)
    low_late, d_send = lax.optimization_barrier((low, d_send))

    d_near = swap(d_send, "mp", 1)
    act_b, dh_b, dzu_b, d_own = feed(low_late, own_rows, *far_args, F32)
    gn_far, gu_far, zn_far, out_send, out_own = emit(
        low, (act_a, act_b), (dh_a, dh_b), wn_far, an_far, bn, z_up, dz_down, out_so_far
    )

    def halves(own, far, axis):
        return jnp.where(high == 0, jnp.concatenate([own, far], axis), jnp.concatenate([far, own], axis))

    def own(value):
        return lax.dynamic_slice_in_dim(value, low * own_rows, own_rows, 0)

    def join(value, first, second):
        return (value.astype(F32) + pair(second, first).astype(F32)).astype(BF16)

    mixed = halves(mine, other, 0)
    stat = halves(stat_mine, stat_other, 2)
    d_near, out_send, mixed, stat = lax.optimization_barrier((d_near, out_send, mixed, stat))

    d_middle, d_low, dz_dense, d_mixed = dense_back(
        low, d_own, d_near, middle, cotangent, second_gain, bd, ad, w_dense, wd_far
    )
    d_mixed, d_low, dz_dense = lax.optimization_barrier((d_mixed, d_low, dz_dense))
    g_blocks = [d_mixed[0]] + [swap(d_mixed[r], "mp", r) for r in (1, 2, 3)]
    ga_up = dot_tn(join(dzu, dzu_a, dzu_b), second)
    gb_down = dot_tn(join(zn, zn_far[:own_rows], zn_far[own_rows:]), cot_pair)
    gb_dense = dot_tn(own(z_dense), d_low)
    gd = [dot_tn(dz_dense, own(m)) for m in m_parts]
    sums = jnp.concatenate([ga_up, gb_down, gb_dense], 1)
    near_in = jnp.concatenate([sums, gd[1], gd[3]], 1).astype(BF16)
    *g_blocks, near_in = lax.optimization_barrier((*g_blocks, near_in))

    near = swap(near_in, "mp", 1)
    out_near = swap(after(out_send, near_in), "mp", 1)
    grad = jnp.zeros((total_rows, local_width), BF16)
    for r, block in enumerate(g_blocks):
        grad = lax.dynamic_update_slice_in_dim(grad, block, (index ^ r) * own_rows, 0)
    d_merged = attend_back(merged, mixed, grad, stat, seg, slopes)
    (send,) = project_back(index, d_merged, wq, aq, bq, (3,), (BF16,))
    send, d_merged, near, out_near = lax.optimization_barrier((send, d_merged, near, out_near))

    relay = swap(send, "mp", 1)
    ga_qkv, gb_qkv = inner_grads(d_merged, z_qkv, normed, bq)
    ga_low = ga_qkv.astype(BF16)
    near = near.astype(F32)
    sums = sums + near[:, :3 * width]
    gd_own = gd[0] + near[:, 3 * width:3 * width + local_width]
    gd_far = gd[2] + near[:, 3 * width + local_width:]
    mate_in = jnp.concatenate([sums.astype(BF16), gu_far, gn_far, gd_far.astype(BF16)], 1)
    ga_low, mate_in, d_merged = lax.optimization_barrier((ga_low, mate_in, d_merged))
    ga_others = [swap(ga_low, "mp", r) for r in (1, 2, 3)]
    mate = swap(mate_in, "mp", 2)
    send_two, send_one, kept = project_back(index, d_merged, wq, aq, bq, (2, 1, 0), (F32, BF16, F32))
    relay, kept, send_one, send_two, mate, *ga_others = lax.optimization_barrier(
        (relay, kept, send_one, send_two, mate, *ga_others)
    )

    d_two = swap((send_two + relay.astype(F32)).astype(BF16), "mp", 2)
    d_one = swap(send_one, "mp", 1)
    layer_out = (own(middle) + out_own + out_near.astype(F32)).astype(BF16)
    first_pack = jnp.concatenate([sums, gu_own, gn_own, gd_own], 1) + mate.astype(F32)
    first_pack = jnp.concatenate([first_pack.astype(BF16), jnp.full((rank, 128), which, BF16)], 1)
    first_pack = lax.all_gather(first_pack, "dp", axis=0)
    ga_qkv = ga_qkv + sum(g.astype(F32) for g in ga_others)
    second_pack = jnp.concatenate([ga_qkv, gb_qkv], 1).astype(BF16)
    second_pack = lax.all_gather(second_pack, "dp", axis=0)
    ids = first_pack[:, 0, -1].astype(jnp.int32)
    ga_up, gb_down, gb_dense, gb_up, ga_down, ga_dense, ga_qkv, gb_qkv = spread(
        ids, first_pack, second_pack, kinds, width, local_width, local_ff
    )
    d_one, d_two = lax.optimization_barrier((d_one, d_two, gb_qkv))[:2]
    d_first = kept + d_one.astype(F32) + d_two.astype(F32)
    input_grad = (d_middle + norm_back(d_first, layer_in.astype(F32), first_gain)).astype(BF16)
    return (
        layer_out,
        input_grad,
        ga_qkv.transpose(2, 0, 1),
        gb_qkv.transpose(0, 2, 1, 3),
        ga_dense.transpose(2, 0, 1),
        gb_dense,
        ga_up.transpose(2, 0, 1),
        gb_up,
        ga_down.transpose(2, 0, 1),
        gb_down,
    )


def solution(mesh):
    return jax.shard_map(
        local,
        mesh=mesh,
        in_specs=(
            P(("dp", "mp"), None), P(), P(), P(None, None, "mp"), P(), P(None, None, None, "mp"), P("mp", None),
            P("mp", None, None), P(), P(), P(), P(None, "mp"), P(), P(None, None, "mp"), P("mp", None),
            P("mp", None, None), P(), P("dp", None), P("dp"), P(("dp", "mp"), None),
        ),
        out_specs=(
            P(("dp", "mp"), None), P(("dp", "mp"), None), P(), P(None, None, None, "mp"), P("mp", None, None), P(),
            P(), P(None, None, "mp"), P("mp", None, None), P(),
        ),
        check_vma=False,
    )
```

```python
import functools

import jax
import jax.numpy as jnp
from jax import lax
from jax.experimental import pallas as pl
from jax.experimental.pallas import tpu as pltpu
from jax.sharding import PartitionSpec as P

HEADS = 32
HD = 64
LONGEST = 512
EPSILON = 1e-05
F32 = jnp.float32
BF16 = jnp.bfloat16
MASKED = -1e30
WHOLE = pl.BlockSpec(memory_space=pltpu.VMEM)
REMOTE = pl.BlockSpec(memory_space=pl.ANY)


def shape(dims, kind=BF16):
    return jax.ShapeDtypeStruct(dims, kind)


def statistics(values):
    center = jnp.mean(values, -1, keepdims=True)
    centred = values - center
    variance = jnp.mean(centred * centred, -1, keepdims=True)
    scaler = lax.rsqrt(variance + EPSILON)
    return centred * scaler, scaler


def layer_norm(values, gain, bias):
    return statistics(values)[0] * gain.astype(F32) + bias.astype(F32)


def norm_back(grad, values, gain):
    normal, scaler = statistics(values)
    scaled = grad * gain.astype(F32)
    first_mean = jnp.mean(scaled, -1, keepdims=True)
    second_mean = jnp.mean(scaled * normal, -1, keepdims=True)
    return (scaled - first_mean - normal * second_mean) * scaler


def by_rows(count, body, chunk=32):
    for i in range(count // chunk):
        body(slice(i * chunk, (i + 1) * chunk))


def dot_nn(left, right):
    return jnp.dot(left, right, preferred_element_type=F32)


def dot_nt(left, right):
    return lax.dot_general(left, right, (((1,), (1,)), ((), ())), preferred_element_type=F32)


def dot_tn(left, right):
    return lax.dot_general(left, right, (((0,), (0,)), ((), ())), preferred_element_type=F32)


def swap(value, axis, bit):
    pairs = [(i, i ^ bit) for i in range(lax.axis_size(axis))]
    return lax.ppermute(value, axis, pairs)


def after(value, *others):
    return lax.optimization_barrier((value, *others))[0]


def gelu_pair(values):
    below = 0.5 * (1.0 + lax.erf(values * 0.5 ** 0.5))
    density = jnp.exp(values * values * -0.5) * 0.3989422804014327
    return values * below, below + values * density


def project_kernel(kept, at_ref, x_ref, gain_ref, bias_ref, aq_ref, bq_ref, wq_ref, *refs):
    merged_ref, normed_ref, z_ref, w_ref, out_ref, low_ref, thin_ref, sems, loads = refs[kept:]
    count = x_ref.shape[0]
    rows = pl.ds(pl.multiple_of(at_ref[0] * count, count), count)
    parts = wq_ref.shape[0]

    def load(i):
        return pltpu.make_async_copy(wq_ref.at[i], w_ref.at[i], loads.at[i])

    def save(i):
        return pltpu.make_async_copy(out_ref.at[i], merged_ref.at[i, rows, :], sems.at[2 + i])

    for i in range(parts):
        load(i).start()

    chunk = min(64, count)

    def norm(i, carry):
        part = pl.ds(pl.multiple_of(i * chunk, chunk), chunk)
        low_ref[part, :] = layer_norm(x_ref[part, :].astype(F32), gain_ref[...], bias_ref[...]).astype(BF16)
        return carry

    lax.fori_loop(0, count // chunk, norm, 0)
    copies = [pltpu.make_async_copy(low_ref, normed_ref.at[rows, :], sems.at[0])]
    copies[0].start()
    thin_ref[...] = dot_nt(low_ref[...], aq_ref[...]).astype(BF16)
    copies.append(pltpu.make_async_copy(thin_ref, z_ref.at[rows, :], sems.at[1]))
    copies[1].start()

    def one(i, carry):
        load(i).wait()
        out_ref[i] = (dot_nn(low_ref[...], w_ref[i]) + dot_nn(thin_ref[...], bq_ref[i])).astype(BF16)
        save(i).start()
        return carry

    lax.fori_loop(0, parts, one, 0)
    for copy in copies + [save(i) for i in range(parts)]:
        copy.wait()


def project(at, rows, gain, bias, aq, bq, wq, total, earlier):
    count, width = rows.shape
    parts, _, local_width = wq.shape
    rank = aq.shape[0]
    kept = len(earlier)
    return pl.pallas_call(
        functools.partial(project_kernel, kept),
        out_shape=(shape((parts, total, local_width)), shape((total, width)), shape((total, rank))),
        grid_spec=pltpu.PrefetchScalarGridSpec(
            num_scalar_prefetch=1,
            grid=(),
            in_specs=[WHOLE] * 5 + [REMOTE] * (1 + kept),
            out_specs=(REMOTE,) * 3,
            scratch_shapes=[
                pltpu.VMEM(wq.shape, BF16),
                pltpu.VMEM((parts, count, local_width), BF16),
                pltpu.VMEM((count, width), BF16),
                pltpu.VMEM((count, rank), BF16),
                pltpu.SemaphoreType.DMA((2 + parts,)),
                pltpu.SemaphoreType.DMA((parts,)),
            ],
        ),
        input_output_aliases={7 + i: i for i in range(kept)},
        name="project",
    )(at.reshape(1), rows, gain, bias, aq, bq, wq, *earlier)


def lane_mask(half):
    return (lax.broadcasted_iota(jnp.int32, (1, 2 * HD), 1) // HD) == half


def allowed_pairs(seg_col, seg_row, causal):
    dims = (seg_col.shape[0], seg_row.shape[1])
    allowed = seg_col == seg_row
    if causal:
        allowed = allowed & (lax.broadcasted_iota(jnp.int32, dims, 0) <= lax.broadcasted_iota(jnp.int32, dims, 1))
    return allowed


def reach_of(block):
    return -(-LONGEST // block)


def attend_kernel(block, count, first_ref, seg_ref, slope_ref, col_ref, row_ref, q_ref, k_ref, v_ref,
                  o_ref, stat_ref, turned_ref, top_ref, total_ref, sum_ref):
    pair = pl.program_id(0)
    turned_ref[...] = v_ref[0].T

    for own in range(count):
        i = first_ref[0] + own
        start = pl.multiple_of(i * block, block)
        here = pl.ds(own * block, block)
        query = q_ref[0, pl.ds(start, block), :] * HD ** -0.5
        scaled = [jnp.where(lane_mask(half), query, 0).astype(BF16) for half in range(2)]

        def one(back):
            at = pl.multiple_of(start - back * block, block)
            keys = pl.ds(at, block)
            allowed = allowed_pairs(col_ref[keys, :1], row_ref[:, pl.ds(start, block)], back == 0)
            place = lax.broadcasted_iota(jnp.int32, (block, block), 0).astype(F32)
            for half in range(2):
                slope = slope_ref[2 * pair + half]
                shift = slope * at.astype(F32)
                scores = jnp.where(allowed, dot_nt(k_ref[0, keys, :], scaled[half]) + slope * place, MASKED)
                best = jnp.max(scores, 0, keepdims=True) + shift
                if back:
                    before = top_ref[half]
                    best = jnp.maximum(best, before)
                weights = jnp.exp(scores - (best - shift))
                total = jnp.sum(weights, 0, keepdims=True)
                result = dot_nn(turned_ref[half * HD:(half + 1) * HD, keys], weights.astype(BF16))
                if back:
                    fade = jnp.exp(before - best)
                    total = total + fade * total_ref[half]
                    result = result + fade * sum_ref[half]
                top_ref[half] = best
                total_ref[half] = total
                sum_ref[half] = result

        one(0)
        for back in range(1, reach_of(block) + 1):
            last = jnp.maximum(start - (back - 1) * block - 1, 0)

            @pl.when((i >= back) & (seg_ref[last] == seg_ref[start]))
            def _(back=back):
                one(back)

        for half in range(2):
            stat_ref[half, :, here] = top_ref[half] + jnp.log(total_ref[half])
        done = jnp.concatenate([sum_ref[half] / total_ref[half] for half in range(2)], 0)
        o_ref[here, :] = done.T.astype(BF16)


def attend(first, merged, seg, slopes, count):
    _, rows, width = merged.shape
    block = min(256, rows)
    heads = width // HD
    col = jnp.broadcast_to(seg[:, None], (rows, 128))

    def part(i):
        return pl.BlockSpec((1, rows, 2 * HD), lambda h, *_: (i, 0, h))

    return pl.pallas_call(
        functools.partial(attend_kernel, block, count),
        out_shape=(shape((count * block, width)), shape((heads, 1, count * block), F32)),
        grid_spec=pltpu.PrefetchScalarGridSpec(
            num_scalar_prefetch=3,
            grid=(heads // 2,),
            in_specs=[
                pl.BlockSpec((rows, 128), lambda h, *_: (0, 0)),
                pl.BlockSpec((1, rows), lambda h, *_: (0, 0)),
                part(0), part(1), part(2),
            ],
            out_specs=(
                pl.BlockSpec((count * block, 2 * HD), lambda h, *_: (0, h)),
                pl.BlockSpec((2, 1, count * block), lambda h, *_: (h, 0, 0)),
            ),
            scratch_shapes=[
                pltpu.VMEM((2 * HD, rows), BF16),
                pltpu.VMEM((2, 1, block), F32),
                pltpu.VMEM((2, 1, block), F32),
                pltpu.VMEM((2, HD, block), F32),
            ],
        ),
        name="attend",
    )(first.reshape(1), seg, slopes, col, seg[None, :], merged, merged, merged)


def attend_back_kernel(block, seg_ref, slope_ref, col_ref, row_ref, stat_ref, m_ref, g_ref, q_ref, k_ref, v_ref,
                       d_ref, turned_ref, center_ref, qsum_ref, ksum_ref, vsum_ref):
    pair = pl.program_id(0)
    count = g_ref.shape[0] // block
    turned_ref[...] = k_ref[0].T
    product = (g_ref[...].astype(F32) * m_ref[...].astype(F32)).T
    for half in range(2):
        center_ref[half:half + 1] = jnp.sum(product[half * HD:(half + 1) * HD], 0, keepdims=True)
    qsum_ref[...] = jnp.zeros_like(qsum_ref)
    ksum_ref[...] = jnp.zeros_like(ksum_ref)
    vsum_ref[...] = jnp.zeros_like(vsum_ref)

    for i in range(count):
        queries = pl.ds(i * block, block)
        query = q_ref[0, queries, :] * HD ** -0.5
        scaled = [jnp.where(lane_mask(half), query, 0).astype(BF16) for half in range(2)]
        grads = [jnp.where(lane_mask(half), g_ref[queries, :], 0).astype(BF16) for half in range(2)]

        def one(j):
            keys = pl.ds(j * block, block)
            allowed = allowed_pairs(col_ref[keys, :1], row_ref[:, queries], i == j)
            place = lax.broadcasted_iota(jnp.int32, (block, block), 0).astype(F32)
            val_part, key_part = 0.0, 0.0
            for half in range(2):
                slope = slope_ref[2 * pair + half]
                shift = slope * float(j * block)
                scores = jnp.where(allowed, dot_nt(k_ref[0, keys, :], scaled[half]) + slope * place, MASKED)
                probs = jnp.exp(scores - (stat_ref[half, :, queries] - shift))
                d_probs = dot_nt(v_ref[0, keys, :], grads[half])
                d_scores = (probs * (d_probs - center_ref[half:half + 1, queries])).astype(BF16)
                val_part = val_part + dot_nn(probs.astype(BF16), grads[half])
                key_part = key_part + dot_nn(d_scores, scaled[half])
                rows = slice(half * HD, (half + 1) * HD)
                qsum_ref[rows, queries] += dot_nn(turned_ref[rows, keys], d_scores)
            vsum_ref[keys, :] += val_part
            ksum_ref[keys, :] += key_part

        one(i)
        for back in range(1, min(i, reach_of(block)) + 1):
            j = i - back

            @pl.when(seg_ref[j * block + block - 1] == seg_ref[i * block])
            def _(j=j):
                one(j)

    d_ref[0] = (qsum_ref[...] * HD ** -0.5).T.astype(BF16)
    d_ref[1] = ksum_ref[...].astype(BF16)
    d_ref[2] = vsum_ref[...].astype(BF16)


def attend_back(merged, mixed, grad, stat, seg, slopes):
    parts, rows, width = merged.shape
    block = min(256, rows)
    wide = pl.BlockSpec((rows, 2 * HD), lambda h, *_: (0, h))
    col = jnp.broadcast_to(seg[:, None], (rows, 128))

    def part(i):
        return pl.BlockSpec((1, rows, 2 * HD), lambda h, *_: (i, 0, h))

    return pl.pallas_call(
        functools.partial(attend_back_kernel, block),
        out_shape=shape(merged.shape),
        grid_spec=pltpu.PrefetchScalarGridSpec(
            num_scalar_prefetch=2,
            grid=(width // (2 * HD),),
            in_specs=[
                pl.BlockSpec((rows, 128), lambda h, *_: (0, 0)),
                pl.BlockSpec((1, rows), lambda h, *_: (0, 0)),
                pl.BlockSpec((2, 1, rows), lambda h, *_: (h, 0, 0)),
                wide, wide, part(0), part(1), part(2),
            ],
            out_specs=pl.BlockSpec((parts, rows, 2 * HD), lambda h, *_: (0, 0, h)),
            scratch_shapes=[
                pltpu.VMEM((2 * HD, rows), BF16),
                pltpu.VMEM((2, rows), F32),
                pltpu.VMEM((2 * HD, rows), F32),
                pltpu.VMEM((rows, 2 * HD), F32),
                pltpu.VMEM((rows, 2 * HD), F32),
            ],
        ),
        name="attend_back",
    )(seg, slopes, col, seg[None, :], stat, mixed, grad, merged, merged, merged)


def dense_kernel(at_ref, x0_ref, x1_ref, m0_ref, m1_ref, m2_ref, m3_ref, a_ref, bd_ref, gain_ref, bias_ref, au_ref,
                 own_ref, far_ref, middle_ref, second_ref, zd_ref, zu_ref, w_ref, m_ref, sum_ref, loads):
    size = m0_ref.shape[1]
    count = x0_ref.shape[0]
    tiles, pieces, _, thick, tile = w_ref.shape
    near = at_ref[0] * count
    away = (1 - at_ref[0]) * count

    def columns(t):
        return pl.ds(pl.multiple_of(t * tile, tile), tile)

    def load(t):
        cols = columns(t)
        own = own_ref.reshape(pieces, thick, own_ref.shape[1]).at[:, :, cols]
        far = far_ref.at[:, pl.ds(4, 3), :, cols]
        return (
            pltpu.make_async_copy(own, w_ref.at[t, :, 0], loads.at[0, t]),
            pltpu.make_async_copy(far, w_ref.at[t, :, pl.ds(1, 3)], loads.at[1, t]),
        )

    def start(t, carry):
        for copy in load(t):
            copy.start()
        return carry

    lax.fori_loop(0, tiles, start, 0)
    for r, m in enumerate((m0_ref, m1_ref, m2_ref, m3_ref)):
        m_ref[:, r * size:(r + 1) * size] = m[...]
    zd_ref[...] = dot_nt(m_ref[...], a_ref[...]).astype(BF16)

    def one(t, carry):
        cols = columns(t)
        for copy in load(t):
            copy.wait()
        total = dot_nn(zd_ref[...], bd_ref[:, cols])
        for r in range(4):
            weights = w_ref[t, :, r].reshape(pieces * thick, tile)
            total = total + dot_nn(m_ref[:, r * size:(r + 1) * size], weights)
        sum_ref[:, cols] = total
        for x_ref, start in ((x0_ref, near), (x1_ref, away)):
            rows = pl.ds(pl.multiple_of(start, count), count)
            sum_ref[rows, cols] += x_ref[:, cols].astype(F32)
        return carry

    lax.fori_loop(0, tiles, one, 0)
    chunk = min(64, count)

    def norm(i, carry):
        part = pl.ds(pl.multiple_of(i * chunk, chunk), chunk)
        values = sum_ref[part, :]
        middle_ref[part, :] = values.astype(BF16)
        second_ref[part, :] = layer_norm(values, gain_ref[...], bias_ref[...]).astype(BF16)
        return carry

    lax.fori_loop(0, 2 * count // chunk, norm, 0)
    zu_ref[...] = dot_nt(second_ref[...], au_ref[...]).astype(BF16)


def dense(low, x_own, x_far, m_parts, ad, bd, gain, bias, au, w_own, w_far):
    count, width = x_own.shape
    rank = ad.shape[0]
    tile = min(512, width)
    pieces, _, thick, _ = w_far.shape
    return pl.pallas_call(
        dense_kernel,
        out_shape=(
            shape((2 * count, width)), shape((2 * count, width)), shape((2 * count, rank)),
            shape((2 * count, rank)),
        ),
        in_specs=[pl.BlockSpec(memory_space=pltpu.SMEM)] + [WHOLE] * 11 + [REMOTE] * 2,
        out_specs=(WHOLE,) * 4,
        scratch_shapes=[
            pltpu.VMEM((width // tile, pieces, 4, thick, tile), BF16), pltpu.VMEM((2 * count, width), BF16),
            pltpu.VMEM((2 * count, width), F32), pltpu.SemaphoreType.DMA((2, width // tile)),
        ],
        name="dense",
    )(low.reshape(1), x_own, x_far, *m_parts, ad, bd, gain, bias, au, w_own, w_far)


def feed_kernel(earlier, at_ref, x_ref, g_ref, up_ref, down_ref, zu_ref, dz_ref, bu_ref, an_ref, au_ref, *refs):
    step = pl.program_id(0)
    if earlier:
        before_ref, active_ref, hidden_ref, dz_out_ref, out_ref, total_ref, inner_ref, held_ref, sem = refs
        count = held_ref.shape[0]
        rows = pl.ds(pl.multiple_of(at_ref[0] * count, count), count)
    else:
        active_ref, hidden_ref, dz_out_ref, out_ref, total_ref, inner_ref = refs

    @pl.when(step == 0)
    def _():
        if earlier:
            pltpu.make_async_copy(before_ref.at[rows, :], held_ref, sem).start()
        total_ref[...] = jnp.zeros_like(total_ref)
        inner_ref[...] = jnp.zeros_like(inner_ref)

    up = up_ref[...].reshape(x_ref.shape[1], hidden_ref.shape[1])
    hidden = dot_nn(x_ref[...], up) + dot_nn(zu_ref[...], bu_ref[...])
    d_active = dot_nt(g_ref[...], down_ref[...]) + dot_nn(dz_ref[...], an_ref[...])
    active, slope = gelu_pair(hidden)
    active_ref[...] = active.astype(BF16)
    d_hidden = (d_active * slope).astype(BF16)
    hidden_ref[...] = d_hidden
    total_ref[...] += dot_nt(d_hidden, up)
    inner_ref[...] += dot_nt(d_hidden, bu_ref[...])

    @pl.when(step == pl.num_programs(0) - 1)
    def _():
        inner = inner_ref[...].astype(BF16)
        dz_out_ref[...] = inner
        total = total_ref[...] + dot_nn(inner, au_ref[...])
        if earlier:
            pltpu.make_async_copy(before_ref.at[rows, :], held_ref, sem).wait()
            total = total + held_ref[...]
        out_ref[...] = total.astype(out_ref.dtype)


def feed(at, count, x, g, up, down, zu, dz, bu, an, au, before, kind):
    width = x.shape[1]
    ff = up.shape[3]
    tile = min(512, ff)
    rank = bu.shape[0]
    earlier = before is not None
    once = pl.Buffered(1)
    rows = pl.BlockSpec((count, width), lambda t, at: (at[0], 0), pipeline_mode=once)
    thin = pl.BlockSpec((count, rank), lambda t, at: (at[0], 0))
    cols = pl.BlockSpec((count, tile), lambda t, at: (0, t))
    row = pl.BlockSpec((rank, tile), lambda t, at: (0, t))
    return pl.pallas_call(
        functools.partial(feed_kernel, earlier),
        out_shape=(shape((count, ff)), shape((count, ff)), shape((count, rank)), shape((count, width), kind)),
        grid_spec=pltpu.PrefetchScalarGridSpec(
            num_scalar_prefetch=1,
            grid=(ff // tile,),
            in_specs=[
                rows, rows, pl.BlockSpec((up.shape[0], 4, up.shape[2], tile), lambda t, at: (0, 0, 0, t)),
                pl.BlockSpec((tile, width), lambda t, at: (t, 0)), thin, thin, row, row,
                pl.BlockSpec((rank, width), lambda t, at: (0, 0)),
            ] + [REMOTE] * earlier,
            out_specs=(
                cols, cols, pl.BlockSpec((count, rank), lambda t, at: (0, 0)),
                pl.BlockSpec((count, width), lambda t, at: (0, 0), pipeline_mode=once),
            ),
            scratch_shapes=[pltpu.VMEM((count, width), F32), pltpu.VMEM((count, rank), F32)] + [
                pltpu.VMEM((count, width), F32), pltpu.SemaphoreType.DMA(()),
            ] * earlier,
        ),
        name="feed",
    )(at.reshape(1), x, g, up, down, zu, dz, bu, an, au, *((before,) if earlier else ()))


def emit_kernel(earlier, at_ref, *refs):
    parts = 2 if earlier else 1
    step = pl.program_id(0)
    total_ref, inner_ref = refs[-2:]
    actives, hiddens, zs, ds = (refs[i * parts:(i + 1) * parts] for i in range(4))
    down_ref, an_ref, bn_ref = refs[4 * parts:4 * parts + 3]
    outs = refs[4 * parts + 3:-2]
    if earlier:
        befores, outs = outs[:2], outs[2:]
    gn_ref, gu_ref, z_ref = outs[:3]
    count = actives[0].shape[0]
    gn, gu = 0.0, 0.0
    for i in range(parts):
        rows = slice(i * count, (i + 1) * count)

        @pl.when(step == 0)
        def _():
            total_ref[rows] = befores[i][...] if earlier else jnp.zeros((count, total_ref.shape[1]), F32)
            inner_ref[rows] = jnp.zeros((count, inner_ref.shape[1]), F32)

        active = actives[i][...]
        total_ref[rows] += dot_nn(active, down_ref[...])
        inner_ref[rows] += dot_nt(active, an_ref[...])
        gn = gn + dot_tn(ds[i][...], active)
        gu = gu + dot_tn(zs[i][...], hiddens[i][...])
    gn_ref[...] = gn.astype(BF16)
    gu_ref[...] = gu.astype(BF16)

    @pl.when(step == pl.num_programs(0) - 1)
    def _():
        inner = inner_ref[...].astype(BF16)
        z_ref[...] = inner
        for i in range(parts):
            rows = slice(i * count, (i + 1) * count)
            out = outs[3 + i]
            out[...] = (total_ref[rows] + dot_nn(inner[rows], bn_ref[...])).astype(out.dtype)


def emit(low, actives, hiddens, down, an, bn, zu, dz, before):
    parts = len(actives)
    count, ff = actives[0].shape
    width = down.shape[1]
    tile = min(512, ff)
    rank = an.shape[0]
    earlier = before is not None
    once = pl.Buffered(1)
    places = (lambda at: 1 - at[0], lambda at: at[0]) if earlier else (lambda at: 0,)
    cols = pl.BlockSpec((count, tile), lambda t, at: (0, t))
    row = pl.BlockSpec((rank, tile), lambda t, at: (0, t))
    thin = [pl.BlockSpec((count, rank), lambda t, at, p=p: (p(at), 0)) for p in places]
    wide = [pl.BlockSpec((count, width), lambda t, at, p=p: (p(at), 0), pipeline_mode=once) for p in places]
    kinds = (BF16, F32) if earlier else (F32,)
    return pl.pallas_call(
        functools.partial(emit_kernel, earlier),
        out_shape=(
            shape((rank, ff)), shape((rank, ff)), shape((parts * count, rank)),
        ) + tuple(shape((count, width), k) for k in kinds),
        grid_spec=pltpu.PrefetchScalarGridSpec(
            num_scalar_prefetch=1,
            grid=(ff // tile,),
            in_specs=[cols] * (2 * parts) + thin * 2 + [
                pl.BlockSpec((tile, width), lambda t, at: (t, 0)), row,
                pl.BlockSpec((rank, width), lambda t, at: (0, 0)),
            ] + wide * earlier,
            out_specs=(
                row, row, pl.BlockSpec((parts * count, rank), lambda t, at: (0, 0)),
            ) + (pl.BlockSpec((count, width), lambda t, at: (0, 0), pipeline_mode=once),) * parts,
            scratch_shapes=[pltpu.VMEM((parts * count, width), F32), pltpu.VMEM((parts * count, rank), F32)],
        ),
        name="emit",
    )(low.reshape(1), *actives, *hiddens, *([zu] * parts), *([dz] * parts), down, an, bn, *([before] * parts * earlier))


def dense_back_kernel(low_ref, own_ref, far_ref, cot_ref, gain_ref, bd_ref, ad_ref, middle_ref, w0_ref, w1_ref,
                      low_out_ref, dz_ref, mixed_ref, mid_ref, w_ref, loads):
    count, width = own_ref.shape
    size = mixed_ref.shape[2]
    pieces, _, thick, _ = w1_ref.shape
    rows = pl.ds(pl.multiple_of(low_ref[0] * count, count), count)
    first = pltpu.make_async_copy(middle_ref.at[rows, :], mid_ref, loads.at[4])
    first.start()
    pltpu.make_async_copy(w0_ref.reshape(pieces, thick, width), w_ref.at[0], loads.at[0]).start()

    def start(r, carry):
        pltpu.make_async_copy(w1_ref.at[:, r + 3], w_ref.at[r], loads.at[r]).start()
        return carry

    lax.fori_loop(1, 4, start, 0)
    first.wait()
    chunk = min(64, count)

    def norm(i, carry):
        part = pl.ds(pl.multiple_of(i * chunk, chunk), chunk)
        grad = own_ref[part, :].astype(F32) + far_ref[part, :].astype(F32)
        change = norm_back(grad, mid_ref[part, :].astype(F32), gain_ref[...])
        low_out_ref[part, :] = (cot_ref[part, :].astype(F32) + change).astype(BF16)
        return carry

    lax.fori_loop(0, count // chunk, norm, 0)
    dz_ref[...] = dot_nt(low_out_ref[...], bd_ref[...]).astype(BF16)

    def one(r, carry):
        pltpu.make_async_copy(w1_ref.at[:, 0], w_ref.at[r], loads.at[r]).wait()
        weights = w_ref[r].reshape(size, width)
        cols = pl.ds(pl.multiple_of(r * size, size), size)
        mixed_ref[r] = (dot_nt(low_out_ref[...], weights) + dot_nn(dz_ref[...], ad_ref[:, cols])).astype(BF16)
        return carry

    lax.fori_loop(0, 4, one, 0)


def dense_back(low, own, far, middle, cot, gain, bd, ad, w_own, w_far):
    count, width = own.shape
    rank = bd.shape[0]
    return pl.pallas_call(
        dense_back_kernel,
        out_shape=(shape((count, width)), shape((count, rank)), shape((4, count, width // 4))),
        in_specs=[pl.BlockSpec(memory_space=pltpu.SMEM)] + [WHOLE] * 6 + [REMOTE] * 3,
        out_specs=(WHOLE,) * 3,
        scratch_shapes=[
            pltpu.VMEM((count, width), BF16), pltpu.VMEM((4, w_far.shape[0]) + w_far.shape[2:], BF16),
            pltpu.SemaphoreType.DMA((5,)),
        ],
        name="dense_back",
    )(low.reshape(1), own, far, cot, gain, bd, ad, middle, w_own, w_far)


def project_back_kernel(order, at_ref, aq_ref, bq_ref, d_ref, wq_ref, *refs):
    outs = refs[:len(order)]
    part_ref, w_ref, inner_ref, sems, loads = refs[len(order):]
    count = outs[0].shape[0]
    tiles, _, tile, _ = w_ref.shape

    def columns(t):
        return pl.ds(pl.multiple_of(t * tile, tile), tile)

    def fetch(place):
        rows = pl.ds(pl.multiple_of((at_ref[0] ^ order[place]) * count, count), count)
        here = pl.ds(place * count, count)
        return pltpu.make_async_copy(d_ref.at[:, rows, :], part_ref.at[:, here, :], sems.at[place])

    def load(t):
        return pltpu.make_async_copy(wq_ref.at[:, columns(t), :], w_ref.at[t], loads.at[t])

    def start(t, carry):
        load(t).start()
        return carry

    blocks = [fetch(place) for place in range(len(order))]
    for copy in blocks:
        copy.start()
    lax.fori_loop(0, tiles, start, 0)
    for copy in blocks:
        copy.wait()
    inner_ref[...] = sum(dot_nt(part_ref[i], bq_ref[i]) for i in range(3)).astype(BF16)

    def one(t, carry):
        load(t).wait()
        cols = columns(t)
        total = dot_nn(inner_ref[...], aq_ref[:, cols])
        for i in range(3):
            total = total + dot_nt(part_ref[i], w_ref[t, i])
        for place, out in enumerate(outs):
            out[:, cols] = total[place * count:(place + 1) * count].astype(BF16)
        return carry

    lax.fori_loop(0, tiles, one, 0)


def project_back(at, d_merged, wq, aq, bq, order):
    parts, total, local_width = d_merged.shape
    width = wq.shape[1]
    count = total // 4
    tile = min(512, width)
    rows = len(order) * count
    return pl.pallas_call(
        functools.partial(project_back_kernel, order),
        out_shape=(shape((count, width)),) * len(order),
        in_specs=[pl.BlockSpec(memory_space=pltpu.SMEM)] + [WHOLE] * 2 + [REMOTE] * 2,
        out_specs=(WHOLE,) * len(order),
        scratch_shapes=[
            pltpu.VMEM((parts, rows, local_width), BF16), pltpu.VMEM((width // tile, parts, tile, local_width), BF16),
            pltpu.VMEM((rows, aq.shape[0]), BF16),
            pltpu.SemaphoreType.DMA((len(order),)), pltpu.SemaphoreType.DMA((width // tile,)),
        ],
        name="project_back",
    )(at.reshape(1), aq, bq, d_merged, wq)


def inner_kernel(d_ref, z_ref, n_ref, bq_ref, ga_ref, gb_ref):
    step = pl.program_id(0)

    @pl.when(step == 0)
    def _():
        ga_ref[...] = jnp.zeros_like(ga_ref)
        gb_ref[...] = jnp.zeros_like(gb_ref)

    inner = sum(dot_nt(d_ref[i], bq_ref[i]) for i in range(3)).astype(BF16)
    ga_ref[...] += dot_tn(inner, n_ref[...])
    width = d_ref.shape[2]
    for i in range(3):
        gb_ref[:, i * width:(i + 1) * width] += dot_tn(z_ref[...], d_ref[i])


def inner_grads(d_merged, z_qkv, normed, bq):
    parts, total, local_width = d_merged.shape
    width = normed.shape[1]
    rank = z_qkv.shape[1]
    count = total // 2
    return pl.pallas_call(
        inner_kernel,
        out_shape=(shape((rank, width), F32), shape((rank, parts * local_width), F32)),
        grid=(2,),
        in_specs=[
            pl.BlockSpec((parts, count, local_width), lambda i: (0, i, 0)),
            pl.BlockSpec((count, rank), lambda i: (i, 0)),
            pl.BlockSpec((count, width), lambda i: (i, 0)),
            pl.BlockSpec(bq.shape, lambda i: (0, 0, 0)),
        ],
        out_specs=(
            pl.BlockSpec((rank, width), lambda i: (0, 0)),
            pl.BlockSpec((rank, parts * local_width), lambda i: (0, 0)),
        ),
        name="inner_grads",
    )(d_merged, z_qkv, normed, bq)


def spread_kernel(ids_ref, first_ref, second_ref, *outs):
    step = pl.program_id(0)

    @pl.when(step == 0)
    def _():
        for out in outs:
            out[...] = jnp.zeros_like(out)

    which = ids_ref[step]
    ga_up, gb_down, gb_dense, gb_up, ga_down, ga_dense, ga_qkv, gb_qkv = outs
    at = 0
    for out in (ga_up, gb_down, gb_dense, gb_up, ga_down, ga_dense):
        size = out.shape[2]
        out[which] += first_ref[0, :, at:at + size].astype(F32)
        at += size
    size = ga_qkv.shape[2]
    ga_qkv[which] += second_ref[0, :, :size].astype(F32)
    local_width = gb_qkv.shape[3]
    for i in range(3):
        gb_qkv[which, i] += second_ref[0, :, size + i * local_width:size + (i + 1) * local_width].astype(F32)


def spread(ids, first, second, kinds, width, local_width, local_ff):
    copies, rank, _ = first.shape
    dims = [(kinds, rank, n) for n in (width, width, width, local_ff, local_ff, local_width, width)]
    dims.append((kinds, 3, rank, local_width))
    return pl.pallas_call(
        spread_kernel,
        out_shape=tuple(shape(d, F32) for d in dims),
        grid_spec=pltpu.PrefetchScalarGridSpec(
            num_scalar_prefetch=1,
            grid=(copies,),
            in_specs=[
                pl.BlockSpec((1,) + first.shape[1:], lambda s, _: (s, 0, 0)),
                pl.BlockSpec((1,) + second.shape[1:], lambda s, _: (s, 0, 0)),
            ],
            out_specs=tuple(
                pl.BlockSpec(d, lambda s, _, n=len(d): (0,) * n, pipeline_mode=pl.Buffered(1)) for d in dims
            ),
        ),
        name="spread",
    )(ids, first, second)


def last_kernel(kept_ref, one_ref, two_ref, x_ref, d_ref, gain_ref, out_ref):
    grad = kept_ref[...].astype(F32) + one_ref[...].astype(F32) + two_ref[...].astype(F32)
    change = norm_back(grad, x_ref[...].astype(F32), gain_ref[...])
    out_ref[...] = (d_ref[...].astype(F32) + change).astype(BF16)


def last_norm(kept, one, two, x, d, gain):
    count, width = x.shape
    chunk = min(64, count)
    rows = pl.BlockSpec((chunk, width), lambda i: (i, 0))
    return pl.pallas_call(
        last_kernel,
        out_shape=shape((count, width)),
        grid=(count // chunk,),
        in_specs=[rows] * 5 + [pl.BlockSpec((1, width), lambda i: (0, 0))],
        out_specs=rows,
        name="last_norm",
    )(kept, one, two, x, d, gain)


def turned(factor, which):
    return lax.dynamic_index_in_dim(factor.transpose(1, 2, 0), which, 0, False)


def local(
    layer_in, first_gain, first_bias, w_qkv, a_qkv, b_qkv, w_dense, a_dense, b_dense, second_gain, second_bias,
    w_up, a_up, b_up, w_down, a_down, b_down, segment_ids, adapter_ids, cotangent,
):
    own_rows, width = layer_in.shape
    kinds = a_qkv.shape[1]
    rank = a_qkv.shape[2]
    local_width = w_dense.shape[0]
    local_ff = w_up.shape[1]
    local_heads = local_width // HD
    index = lax.axis_index("mp")
    spot = lax.axis_index("dp")
    copies = lax.axis_size("dp")
    total_rows = 4 * own_rows
    low, high = index & 1, index >> 1
    which = adapter_ids[0]
    seg = segment_ids[0]
    head_ids = (index * local_heads + lax.iota(jnp.int32, local_heads)).astype(F32)
    slopes = jnp.exp2(-8.0 * (head_ids + 1.0) / HEADS)
    first_gain, first_bias, second_gain, second_bias = (
        v[None, :] for v in (first_gain, first_bias, second_gain, second_bias)
    )

    aq, ad, au, an = (turned(a, which) for a in (a_qkv, a_dense, a_up, a_down))
    bq = lax.dynamic_index_in_dim(b_qkv.transpose(0, 2, 1, 3), which, 0, False)
    bd, bu, bn = (lax.dynamic_index_in_dim(b, which, 0, False) for b in (b_dense, b_up, b_down))
    wq = w_qkv.transpose(1, 0, 2)

    def slice_of(weight):
        size = weight.shape[0] // copies
        return lax.dynamic_slice_in_dim(weight, spot * size, size, 0)

    x_one = swap(layer_in, "mp", 1)
    x_two = swap(layer_in, "mp", 2)
    wd_slice = slice_of(w_dense)
    size = wd_slice.shape[0]
    ad_flat = ad.reshape(-1, width)
    last = size + ad_flat.shape[0]
    tail = jnp.concatenate([wd_slice, ad_flat], 0)

    def step_in(r, block, held):
        return project(index ^ r, block, first_gain, first_bias, aq, bq, wq, total_rows, held)

    held = step_in(0, layer_in, ())
    wu_halves = jnp.split(slice_of(w_up), 2, axis=0)
    x_one, x_two, *held = lax.optimization_barrier((x_one, x_two, *held))

    x_three = swap(x_two, "mp", 1)
    pack_two = swap(after(jnp.concatenate([tail, bu, an], 0), x_one), "mp", 2)
    wu_first = swap(after(wu_halves[0], x_one), "mp", 2)
    held = step_in(1, x_one, held)
    held = step_in(2, x_two, held)
    x_three, pack_two, wu_first, *held = lax.optimization_barrier((x_three, pack_two, wu_first, *held))

    pack_one = swap(jnp.concatenate([tail, pack_two[:last]], 0), "mp", 1)
    wu_second = swap(after(wu_halves[1], x_three), "mp", 2)
    held = step_in(3, x_three, held)
    merged, normed, z_qkv = held
    other, stat_other = attend(2 * (1 - high), merged, seg, slopes, 2)
    other, pack_one, pack_two, wu_first, wu_second, merged = lax.optimization_barrier(
        (other, pack_one, pack_two, wu_first, wu_second, merged)
    )

    m_two = swap(other, "mp", 2)
    bu_far, an_far = pack_two[last:last + rank], pack_two[last + rank:]
    packs = (pack_one[:last], pack_two, pack_one[last:])
    slices = jnp.concatenate([wu_first, wu_second, *(p[:size] for p in packs)], 0)
    shared = lax.all_gather(slices, "dp", axis=0).reshape(copies, 7, size, width)
    ad = jnp.concatenate([ad] + [p[size:last].reshape(rank, local_width) for p in packs], 1)
    mine, stat_mine = attend(2 * high, merged, seg, slopes, 2)
    m_two, mine = lax.optimization_barrier((m_two, mine))

    m_one = swap(mine, "mp", 1)
    m_three = swap(m_two, "mp", 1)
    wn_halves = jnp.split(after(slice_of(w_down), m_two), 2, axis=0)
    wn_first = swap(wn_halves[0], "mp", 2)
    m_one, m_three, wn_first = lax.optimization_barrier((m_one, m_three, wn_first))

    m_parts = [mine, m_one, m_two, m_three]
    cot_far = swap(after(cotangent, m_one), "mp", 1)
    wn_second = swap(after(wn_halves[1], m_one), "mp", 2)

    def pair(own, far):
        return jnp.where(low == 0, jnp.concatenate([own, far], 0), jnp.concatenate([far, own], 0))

    middle, second, z_dense, z_up = dense(
        low, layer_in, x_one, m_parts, ad, bd, second_gain, second_bias, au, w_dense, shared
    )
    wn_second, second, cot_far = lax.optimization_barrier((wn_second, second, cot_far))
    wn_far = lax.all_gather(jnp.concatenate([wn_first, wn_second], 0), "dp", axis=0, tiled=True)

    cot_pair = pair(cotangent, cot_far)
    dz_down = dot_nt(cot_pair, bn).astype(BF16)
    zero = jnp.zeros((), jnp.int32)
    act, dh, dzu, so_far = feed(
        zero, 2 * own_rows, second, cot_pair, w_up.reshape(copies, 4, size, width), w_down, z_up, dz_down, bu, an, au, None, F32
    )
    gn_own, gu_own, zn, out_so_far = emit(zero, (act,), (dh,), w_down, an, bn, z_up, dz_down, None)
    out_so_far, so_far = lax.optimization_barrier((out_so_far, so_far))
    far_args = (second, cot_pair, shared, wn_far, z_up, dz_down, bu_far, an_far, au, so_far)
    act_a, dh_a, dzu_a, d_send = feed(1 - low, own_rows, *far_args, BF16)
    low_late, d_send = lax.optimization_barrier((low, d_send))

    d_near = swap(d_send, "mp", 1)
    act_b, dh_b, dzu_b, d_own = feed(low_late, own_rows, *far_args, BF16)
    gn_far, gu_far, zn_far, out_send, out_own = emit(
        low, (act_a, act_b), (dh_a, dh_b), wn_far, an_far, bn, z_up, dz_down, out_so_far
    )

    def halves(own, far, axis):
        return jnp.where(high == 0, jnp.concatenate([own, far], axis), jnp.concatenate([far, own], axis))

    def own(value):
        return lax.dynamic_slice_in_dim(value, low * own_rows, own_rows, 0)

    def join(value, first, second):
        return (value.astype(F32) + pair(second, first).astype(F32)).astype(BF16)

    mixed = halves(mine, other, 0)
    stat = halves(stat_mine, stat_other, 2)
    d_near, out_send, mixed, stat = lax.optimization_barrier((d_near, out_send, mixed, stat))

    d_low, dz_dense, d_mixed = dense_back(
        low, d_own, d_near, middle, cotangent, second_gain, bd, ad, w_dense, shared
    )
    d_mixed, d_low, dz_dense = lax.optimization_barrier((d_mixed, d_low, dz_dense))
    g_blocks = [d_mixed[0]] + [swap(d_mixed[r], "mp", r) for r in (1, 2, 3)]
    ga_up = dot_tn(join(dzu, dzu_a, dzu_b), second)
    gb_down = dot_tn(join(zn, zn_far[:own_rows], zn_far[own_rows:]), cot_pair)
    gb_dense = dot_tn(own(z_dense), d_low)
    gd = [dot_tn(dz_dense, own(m)) for m in m_parts]
    sums = jnp.concatenate([ga_up, gb_down, gb_dense], 1)
    near = swap(jnp.concatenate([sums, gd[1], gd[3]], 1).astype(BF16), "mp", 1)
    *g_blocks, near = lax.optimization_barrier((*g_blocks, near))

    near = near.astype(F32)
    sums = sums + near[:, :3 * width]
    gd_own = gd[0] + near[:, 3 * width:3 * width + local_width]
    gd_far = gd[2] + near[:, 3 * width + local_width:]
    mate = swap(jnp.concatenate([sums.astype(BF16), gu_far, gn_far, gd_far.astype(BF16)], 1), "mp", 2)
    out_near = swap(after(out_send, near), "mp", 1)
    grad = jnp.zeros((total_rows, local_width), BF16)
    for r, block in enumerate(g_blocks):
        grad = lax.dynamic_update_slice_in_dim(grad, block, (index ^ r) * own_rows, 0)
    d_merged = attend_back(merged, mixed, grad, stat, seg, slopes)
    (send,) = project_back(index, d_merged, wq, aq, bq, (3,))
    send, d_merged, mate, out_near = lax.optimization_barrier((send, d_merged, mate, out_near))

    relay = swap(send, "mp", 1)
    first_pack = jnp.concatenate([sums, gu_own, gn_own, gd_own], 1) + mate.astype(F32)
    first_pack = jnp.concatenate([first_pack.astype(BF16), jnp.full((rank, 128), which, BF16)], 1)
    first_pack = lax.all_gather(first_pack, "dp", axis=0)
    ga_qkv, gb_qkv = inner_grads(d_merged, z_qkv, normed, bq)
    ga_low, d_merged = lax.optimization_barrier((ga_qkv.astype(BF16), d_merged))
    ga_others = [swap(ga_low, "mp", r) for r in (1, 2, 3)]
    send_two, send_one, kept = project_back(index, d_merged, wq, aq, bq, (2, 1, 0))
    relay, send_one, send_two, kept, *ga_others = lax.optimization_barrier(
        (relay, send_one, send_two, kept, *ga_others)
    )

    d_two = swap((send_two.astype(F32) + relay.astype(F32)).astype(BF16), "mp", 2)
    d_one = swap(send_one, "mp", 1)
    layer_out = (own(middle).astype(F32) + out_own + out_near.astype(F32)).astype(BF16)
    ga_qkv = ga_qkv + sum(g.astype(F32) for g in ga_others)
    second_pack = jnp.concatenate([ga_qkv, gb_qkv], 1).astype(BF16)
    second_pack = lax.all_gather(second_pack, "dp", axis=0)
    ids = first_pack[:, 0, -1].astype(jnp.int32)
    ga_up, gb_down, gb_dense, gb_up, ga_down, ga_dense, ga_qkv, gb_qkv = spread(
        ids, first_pack, second_pack, kinds, width, local_width, local_ff
    )
    d_one, d_two = lax.optimization_barrier((d_one, d_two, gb_qkv))[:2]
    input_grad = last_norm(kept, d_one, d_two, layer_in, d_low, first_gain)
    return (
        layer_out,
        input_grad,
        ga_qkv.transpose(2, 0, 1),
        gb_qkv.transpose(0, 2, 1, 3),
        ga_dense.transpose(2, 0, 1),
        gb_dense,
        ga_up.transpose(2, 0, 1),
        gb_up,
        ga_down.transpose(2, 0, 1),
        gb_down,
    )


def solution(mesh):
    return jax.shard_map(
        local,
        mesh=mesh,
        in_specs=(
            P(("dp", "mp"), None), P(), P(), P(None, None, "mp"), P(), P(None, None, None, "mp"), P("mp", None),
            P("mp", None, None), P(), P(), P(), P(None, "mp"), P(), P(None, None, "mp"), P("mp", None),
            P("mp", None, None), P(), P("dp", None), P("dp"), P(("dp", "mp"), None),
        ),
        out_specs=(
            P(("dp", "mp"), None), P(("dp", "mp"), None), P(), P(None, None, None, "mp"), P("mp", None, None), P(),
            P(), P(None, None, "mp"), P("mp", None, None), P(),
        ),
        check_vma=False,
    )
```

```python
import functools

import jax
import jax.numpy as jnp
from jax import lax
from jax.experimental import pallas as pl
from jax.experimental.pallas import tpu as pltpu
from jax.sharding import PartitionSpec as P

HEADS = 32
HD = 64
LONGEST = 512
EPSILON = 1e-05
F32 = jnp.float32
BF16 = jnp.bfloat16
MASKED = -1e30
WHOLE = pl.BlockSpec(memory_space=pltpu.VMEM)
REMOTE = pl.BlockSpec(memory_space=pl.ANY)


def shape(dims, kind=BF16):
    return jax.ShapeDtypeStruct(dims, kind)


def statistics(values):
    center = jnp.mean(values, -1, keepdims=True)
    centred = values - center
    variance = jnp.mean(centred * centred, -1, keepdims=True)
    scaler = lax.rsqrt(variance + EPSILON)
    return centred * scaler, scaler


def layer_norm(values, gain, bias):
    return statistics(values)[0] * gain.astype(F32) + bias.astype(F32)


def norm_back(grad, values, gain):
    normal, scaler = statistics(values)
    scaled = grad * gain.astype(F32)
    first_mean = jnp.mean(scaled, -1, keepdims=True)
    second_mean = jnp.mean(scaled * normal, -1, keepdims=True)
    return (scaled - first_mean - normal * second_mean) * scaler


def by_rows(count, body, chunk=32):
    for i in range(count // chunk):
        body(slice(i * chunk, (i + 1) * chunk))


def dot_nn(left, right):
    return jnp.dot(left, right, preferred_element_type=F32)


def dot_nt(left, right):
    return lax.dot_general(left, right, (((1,), (1,)), ((), ())), preferred_element_type=F32)


def dot_tn(left, right):
    return lax.dot_general(left, right, (((0,), (0,)), ((), ())), preferred_element_type=F32)


def swap(value, axis, bit):
    pairs = [(i, i ^ bit) for i in range(lax.axis_size(axis))]
    return lax.ppermute(value, axis, pairs)


def after(value, *others):
    return lax.optimization_barrier((value, *others))[0]


def gelu_pair(values):
    below = 0.5 * (1.0 + lax.erf(values * 0.5 ** 0.5))
    density = jnp.exp(values * values * -0.5) * 0.3989422804014327
    return values * below, below + values * density


def project_kernel(kept, at_ref, x_ref, gain_ref, bias_ref, aq_ref, bq_ref, wq_ref, *refs):
    merged_ref, normed_ref, z_ref, w_ref, out_ref, low_ref, thin_ref, sems, loads = refs[kept:]
    count = x_ref.shape[0]
    rows = pl.ds(pl.multiple_of(at_ref[0] * count, count), count)
    parts = wq_ref.shape[0]

    def load(i):
        return pltpu.make_async_copy(wq_ref.at[i], w_ref.at[i], loads.at[i])

    def save(i):
        return pltpu.make_async_copy(out_ref.at[i], merged_ref.at[i, rows, :], sems.at[2 + i])

    for i in range(parts):
        load(i).start()

    chunk = min(64, count)

    def norm(i, carry):
        part = pl.ds(pl.multiple_of(i * chunk, chunk), chunk)
        low_ref[part, :] = layer_norm(x_ref[part, :].astype(F32), gain_ref[...], bias_ref[...]).astype(BF16)
        return carry

    lax.fori_loop(0, count // chunk, norm, 0)
    copies = [pltpu.make_async_copy(low_ref, normed_ref.at[rows, :], sems.at[0])]
    copies[0].start()
    thin_ref[...] = dot_nt(low_ref[...], aq_ref[...]).astype(BF16)
    copies.append(pltpu.make_async_copy(thin_ref, z_ref.at[rows, :], sems.at[1]))
    copies[1].start()

    def one(i, carry):
        load(i).wait()
        out_ref[i] = (dot_nn(low_ref[...], w_ref[i]) + dot_nn(thin_ref[...], bq_ref[i])).astype(BF16)
        save(i).start()
        return carry

    lax.fori_loop(0, parts, one, 0)
    for copy in copies + [save(i) for i in range(parts)]:
        copy.wait()


def project(at, rows, gain, bias, aq, bq, wq, total, earlier):
    count, width = rows.shape
    parts, _, local_width = wq.shape
    rank = aq.shape[0]
    kept = len(earlier)
    return pl.pallas_call(
        functools.partial(project_kernel, kept),
        out_shape=(shape((parts, total, local_width)), shape((total, width)), shape((total, rank))),
        grid_spec=pltpu.PrefetchScalarGridSpec(
            num_scalar_prefetch=1,
            grid=(),
            in_specs=[WHOLE] * 5 + [REMOTE] * (1 + kept),
            out_specs=(REMOTE,) * 3,
            scratch_shapes=[
                pltpu.VMEM(wq.shape, BF16),
                pltpu.VMEM((parts, count, local_width), BF16),
                pltpu.VMEM((count, width), BF16),
                pltpu.VMEM((count, rank), BF16),
                pltpu.SemaphoreType.DMA((2 + parts,)),
                pltpu.SemaphoreType.DMA((parts,)),
            ],
        ),
        input_output_aliases={7 + i: i for i in range(kept)},
        name="project",
    )(at.reshape(1), rows, gain, bias, aq, bq, wq, *earlier)


def lane_mask(half):
    return (lax.broadcasted_iota(jnp.int32, (1, 2 * HD), 1) // HD) == half


def allowed_pairs(seg_col, seg_row, causal):
    dims = (seg_col.shape[0], seg_row.shape[1])
    allowed = seg_col == seg_row
    if causal:
        allowed = allowed & (lax.broadcasted_iota(jnp.int32, dims, 0) <= lax.broadcasted_iota(jnp.int32, dims, 1))
    return allowed


def reach_of(block):
    return -(-LONGEST // block)


def attend_kernel(block, count, first_ref, seg_ref, slope_ref, col_ref, row_ref, q_ref, k_ref, v_ref,
                  o_ref, stat_ref, turned_ref, top_ref, total_ref, sum_ref):
    pair = pl.program_id(0)
    turned_ref[...] = v_ref[0].T

    for own in range(count):
        i = first_ref[0] ^ own
        start = pl.multiple_of(i * block, block)
        here = pl.ds(own * block, block)
        query = q_ref[0, pl.ds(start, block), :] * HD ** -0.5
        scaled = [jnp.where(lane_mask(half), query, 0).astype(BF16) for half in range(2)]

        def one(back):
            at = pl.multiple_of(start - back * block, block)
            keys = pl.ds(at, block)
            allowed = allowed_pairs(col_ref[keys, :1], row_ref[:, pl.ds(start, block)], back == 0)
            place = lax.broadcasted_iota(jnp.int32, (block, block), 0).astype(F32)
            for half in range(2):
                slope = slope_ref[2 * pair + half]
                shift = slope * at.astype(F32)
                scores = jnp.where(allowed, dot_nt(k_ref[0, keys, :], scaled[half]) + slope * place, MASKED)
                best = jnp.max(scores, 0, keepdims=True) + shift
                if back:
                    before = top_ref[half]
                    best = jnp.maximum(best, before)
                weights = jnp.exp(scores - (best - shift))
                total = jnp.sum(weights, 0, keepdims=True)
                result = dot_nn(turned_ref[half * HD:(half + 1) * HD, keys], weights.astype(BF16))
                if back:
                    fade = jnp.exp(before - best)
                    total = total + fade * total_ref[half]
                    result = result + fade * sum_ref[half]
                top_ref[half] = best
                total_ref[half] = total
                sum_ref[half] = result

        one(0)
        for back in range(1, reach_of(block) + 1):
            last = jnp.maximum(start - (back - 1) * block - 1, 0)

            @pl.when((i >= back) & (seg_ref[last] == seg_ref[start]))
            def _(back=back):
                one(back)

        for half in range(2):
            stat_ref[half, :, here] = top_ref[half] + jnp.log(total_ref[half])
        done = jnp.concatenate([sum_ref[half] / total_ref[half] for half in range(2)], 0)
        o_ref[here, :] = done.T.astype(BF16)


def attend(first, merged, seg, slopes, count):
    _, rows, width = merged.shape
    block = min(256, rows)
    heads = width // HD
    col = jnp.broadcast_to(seg[:, None], (rows, 128))

    def part(i):
        return pl.BlockSpec((1, rows, 2 * HD), lambda h, *_: (i, 0, h))

    return pl.pallas_call(
        functools.partial(attend_kernel, block, count),
        out_shape=(shape((count * block, width)), shape((heads, 1, count * block), F32)),
        grid_spec=pltpu.PrefetchScalarGridSpec(
            num_scalar_prefetch=3,
            grid=(heads // 2,),
            in_specs=[
                pl.BlockSpec((rows, 128), lambda h, *_: (0, 0)),
                pl.BlockSpec((1, rows), lambda h, *_: (0, 0)),
                part(0), part(1), part(2),
            ],
            out_specs=(
                pl.BlockSpec((count * block, 2 * HD), lambda h, *_: (0, h)),
                pl.BlockSpec((2, 1, count * block), lambda h, *_: (h, 0, 0)),
            ),
            scratch_shapes=[
                pltpu.VMEM((2 * HD, rows), BF16),
                pltpu.VMEM((2, 1, block), F32),
                pltpu.VMEM((2, 1, block), F32),
                pltpu.VMEM((2, HD, block), F32),
            ],
        ),
        name="attend",
    )(first.reshape(1), seg, slopes, col, seg[None, :], merged, merged, merged)


def attend_back_kernel(block, at_ref, seg_ref, slope_ref, col_ref, row_ref, *refs):
    stats, mixed, grads_in = refs[:2], refs[2:4], refs[4:8]
    q_ref, k_ref, v_ref, d_ref, stat_ref, m_ref, g_ref, turned_ref, center_ref, qsum_ref, ksum_ref, vsum_ref = refs[8:]
    pair = pl.program_id(0)
    count = g_ref.shape[0] // block
    size = grads_in[0].shape[0]
    for r, ref in enumerate(grads_in):
        rows = pl.ds(pl.multiple_of((at_ref[0] ^ r) * size, size), size)
        part = slice((r % 2) * size, (r % 2 + 1) * size)
        g_ref[rows, :] = ref[...]
        m_ref[rows, :] = mixed[r // 2][part, :]
        stat_ref[:, :, rows] = stats[r // 2][:, :, part]
    turned_ref[...] = k_ref[0].T
    product = (g_ref[...].astype(F32) * m_ref[...].astype(F32)).T
    for half in range(2):
        center_ref[half:half + 1] = jnp.sum(product[half * HD:(half + 1) * HD], 0, keepdims=True)
    qsum_ref[...] = jnp.zeros_like(qsum_ref)
    ksum_ref[...] = jnp.zeros_like(ksum_ref)
    vsum_ref[...] = jnp.zeros_like(vsum_ref)

    for i in range(count):
        queries = pl.ds(i * block, block)
        query = q_ref[0, queries, :] * HD ** -0.5
        scaled = [jnp.where(lane_mask(half), query, 0).astype(BF16) for half in range(2)]
        grads = [jnp.where(lane_mask(half), g_ref[queries, :], 0).astype(BF16) for half in range(2)]

        def one(j):
            keys = pl.ds(j * block, block)
            allowed = allowed_pairs(col_ref[keys, :1], row_ref[:, queries], i == j)
            place = lax.broadcasted_iota(jnp.int32, (block, block), 0).astype(F32)
            val_part, key_part = 0.0, 0.0
            for half in range(2):
                slope = slope_ref[2 * pair + half]
                shift = slope * float(j * block)
                scores = jnp.where(allowed, dot_nt(k_ref[0, keys, :], scaled[half]) + slope * place, MASKED)
                probs = jnp.exp(scores - (stat_ref[half, :, queries] - shift))
                d_probs = dot_nt(v_ref[0, keys, :], grads[half])
                d_scores = (probs * (d_probs - center_ref[half:half + 1, queries])).astype(BF16)
                val_part = val_part + dot_nn(probs.astype(BF16), grads[half])
                key_part = key_part + dot_nn(d_scores, scaled[half])
                rows = slice(half * HD, (half + 1) * HD)
                qsum_ref[rows, queries] += dot_nn(turned_ref[rows, keys], d_scores)
            vsum_ref[keys, :] += val_part
            ksum_ref[keys, :] += key_part

        one(i)
        for back in range(1, min(i, reach_of(block)) + 1):
            j = i - back

            @pl.when(seg_ref[j * block + block - 1] == seg_ref[i * block])
            def _(j=j):
                one(j)

    d_ref[0] = (qsum_ref[...] * HD ** -0.5).T.astype(BF16)
    d_ref[1] = ksum_ref[...].astype(BF16)
    d_ref[2] = vsum_ref[...].astype(BF16)


def attend_back(at, merged, mixed, grads, stats, seg, slopes):
    parts, rows, width = merged.shape
    block = min(256, rows)
    half = rows // 2
    col = jnp.broadcast_to(seg[:, None], (rows, 128))

    def wide(count):
        return pl.BlockSpec((count, 2 * HD), lambda h, *_: (0, h))

    def part(i):
        return pl.BlockSpec((1, rows, 2 * HD), lambda h, *_: (i, 0, h))

    return pl.pallas_call(
        functools.partial(attend_back_kernel, block),
        out_shape=shape(merged.shape),
        grid_spec=pltpu.PrefetchScalarGridSpec(
            num_scalar_prefetch=3,
            grid=(width // (2 * HD),),
            in_specs=[
                pl.BlockSpec((rows, 128), lambda h, *_: (0, 0)),
                pl.BlockSpec((1, rows), lambda h, *_: (0, 0)),
            ] + [pl.BlockSpec((2, 1, half), lambda h, *_: (h, 0, 0))] * 2 + [wide(half)] * 2 + [wide(rows // 4)] * 4 + [
                part(0), part(1), part(2),
            ],
            out_specs=pl.BlockSpec((parts, rows, 2 * HD), lambda h, *_: (0, 0, h)),
            scratch_shapes=[
                pltpu.VMEM((2, 1, rows), F32),
                pltpu.VMEM((rows, 2 * HD), BF16),
                pltpu.VMEM((rows, 2 * HD), BF16),
                pltpu.VMEM((2 * HD, rows), BF16),
                pltpu.VMEM((2, rows), F32),
                pltpu.VMEM((2 * HD, rows), F32),
                pltpu.VMEM((rows, 2 * HD), F32),
                pltpu.VMEM((rows, 2 * HD), F32),
            ],
        ),
        name="attend_back",
    )(at.reshape(1), seg, slopes, col, seg[None, :], *stats, *mixed, *grads, merged, merged, merged)


def dense_kernel(x0_ref, x1_ref, m0_ref, m1_ref, m2_ref, m3_ref, a_ref, bd_ref, gain_ref, bias_ref, au_ref,
                 own_ref, far_ref, middle_ref, second_ref, zd_ref, zu_ref, w_ref, m_ref, sum_ref, loads):
    size = m0_ref.shape[1]
    count = x0_ref.shape[0]
    tiles, pieces, _, thick, tile = w_ref.shape

    def columns(t):
        return pl.ds(pl.multiple_of(t * tile, tile), tile)

    def load(t):
        cols = columns(t)
        own = own_ref.reshape(pieces, thick, own_ref.shape[1]).at[:, :, cols]
        far = far_ref.at[:, pl.ds(4, 3), :, cols]
        return (
            pltpu.make_async_copy(own, w_ref.at[t, :, 0], loads.at[0, t]),
            pltpu.make_async_copy(far, w_ref.at[t, :, pl.ds(1, 3)], loads.at[1, t]),
        )

    def start(t, carry):
        for copy in load(t):
            copy.start()
        return carry

    lax.fori_loop(0, tiles, start, 0)
    for r, m in enumerate((m0_ref, m1_ref, m2_ref, m3_ref)):
        cols = slice(r * size, (r + 1) * size)
        m_ref[:count, cols] = m[(r % 2) * count:(r % 2 + 1) * count, :]
        m_ref[count:, cols] = m[(1 - r % 2) * count:(2 - r % 2) * count, :]
    zd_ref[...] = dot_nt(m_ref[...], a_ref[...]).astype(BF16)

    def one(t, carry):
        cols = columns(t)
        for copy in load(t):
            copy.wait()
        total = dot_nn(zd_ref[...], bd_ref[:, cols])
        for r in range(4):
            weights = w_ref[t, :, r].reshape(pieces * thick, tile)
            total = total + dot_nn(m_ref[:, r * size:(r + 1) * size], weights)
        sum_ref[:count, cols] = total[:count] + x0_ref[:, cols].astype(F32)
        sum_ref[count:, cols] = total[count:] + x1_ref[:, cols].astype(F32)
        return carry

    lax.fori_loop(0, tiles, one, 0)
    chunk = min(64, count)

    def norm(i, carry):
        part = pl.ds(pl.multiple_of(i * chunk, chunk), chunk)
        values = sum_ref[part, :]
        middle_ref[part, :] = values.astype(BF16)
        second_ref[part, :] = layer_norm(values, gain_ref[...], bias_ref[...]).astype(BF16)
        return carry

    lax.fori_loop(0, 2 * count // chunk, norm, 0)
    zu_ref[...] = dot_nt(second_ref[...], au_ref[...]).astype(BF16)


def dense(x_own, x_far, m_parts, ad, bd, gain, bias, au, w_own, w_far):
    count, width = x_own.shape
    rank = ad.shape[0]
    tile = min(512, width)
    pieces, _, thick, _ = w_far.shape
    return pl.pallas_call(
        dense_kernel,
        out_shape=(
            shape((2 * count, width)), shape((2 * count, width)), shape((2 * count, rank)),
            shape((2 * count, rank)),
        ),
        in_specs=[WHOLE] * 11 + [REMOTE] * 2,
        out_specs=(WHOLE,) * 4,
        scratch_shapes=[
            pltpu.VMEM((width // tile, pieces, 4, thick, tile), BF16), pltpu.VMEM((2 * count, width), BF16),
            pltpu.VMEM((2 * count, width), F32), pltpu.SemaphoreType.DMA((2, width // tile)),
        ],
        name="dense",
    )(x_own, x_far, *m_parts, ad, bd, gain, bias, au, w_own, w_far)


def feed_kernel(earlier, at_ref, x_ref, up_ref, down_ref, zu_ref, dz_ref, bu_ref, an_ref, au_ref, *refs):
    blocks = 1 if earlier else 2
    g_refs, refs = refs[:blocks], refs[blocks:]
    step = pl.program_id(0)
    if earlier:
        before_ref, active_ref, hidden_ref, dz_out_ref, out_ref, total_ref, inner_ref, held_ref, sem = refs
        count = held_ref.shape[0]
        rows = pl.ds(pl.multiple_of(at_ref[0] * count, count), count)
    else:
        active_ref, hidden_ref, dz_out_ref, out_ref, total_ref, inner_ref = refs

    @pl.when(step == 0)
    def _():
        if earlier:
            pltpu.make_async_copy(before_ref.at[rows, :], held_ref, sem).start()
        total_ref[...] = jnp.zeros_like(total_ref)
        inner_ref[...] = jnp.zeros_like(inner_ref)

    up = up_ref[...].reshape(x_ref.shape[1], hidden_ref.shape[1])
    hidden = dot_nn(x_ref[...], up) + dot_nn(zu_ref[...], bu_ref[...])
    d_active = jnp.concatenate([dot_nt(g[...], down_ref[...]) for g in g_refs], 0) + dot_nn(dz_ref[...], an_ref[...])
    active, slope = gelu_pair(hidden)
    active_ref[...] = active.astype(BF16)
    d_hidden = (d_active * slope).astype(BF16)
    hidden_ref[...] = d_hidden
    total_ref[...] += dot_nt(d_hidden, up)
    inner_ref[...] += dot_nt(d_hidden, bu_ref[...])

    @pl.when(step == pl.num_programs(0) - 1)
    def _():
        inner = inner_ref[...].astype(BF16)
        dz_out_ref[...] = inner
        total = total_ref[...] + dot_nn(inner, au_ref[...])
        if earlier:
            pltpu.make_async_copy(before_ref.at[rows, :], held_ref, sem).wait()
            total = total + held_ref[...]
        out_ref[...] = total.astype(out_ref.dtype)


def feed(at, count, x, g, up, down, zu, dz, bu, an, au, before, kind):
    width = x.shape[1]
    ff = up.shape[3]
    tile = min(512, ff)
    rank = bu.shape[0]
    earlier = before is not None
    once = pl.Buffered(1)
    rows = pl.BlockSpec((count, width), lambda t, at: (at[0], 0), pipeline_mode=once)
    thin = pl.BlockSpec((count, rank), lambda t, at: (at[0], 0))
    cols = pl.BlockSpec((count, tile), lambda t, at: (0, t))
    row = pl.BlockSpec((rank, tile), lambda t, at: (0, t))
    return pl.pallas_call(
        functools.partial(feed_kernel, earlier),
        out_shape=(shape((count, ff)), shape((count, ff)), shape((count, rank)), shape((count, width), kind)),
        grid_spec=pltpu.PrefetchScalarGridSpec(
            num_scalar_prefetch=1,
            grid=(ff // tile,),
            in_specs=[
                rows, pl.BlockSpec((up.shape[0], 4, up.shape[2], tile), lambda t, at: (0, 0, 0, t)),
                pl.BlockSpec((tile, width), lambda t, at: (t, 0)), thin, thin, row, row,
                pl.BlockSpec((rank, width), lambda t, at: (0, 0)),
            ] + [pl.BlockSpec(b.shape, lambda t, at: (0, 0), pipeline_mode=once) for b in g] + [REMOTE] * earlier,
            out_specs=(
                cols, cols, pl.BlockSpec((count, rank), lambda t, at: (0, 0)),
                pl.BlockSpec((count, width), lambda t, at: (0, 0), pipeline_mode=once),
            ),
            scratch_shapes=[pltpu.VMEM((count, width), F32), pltpu.VMEM((count, rank), F32)] + [
                pltpu.VMEM((count, width), F32), pltpu.SemaphoreType.DMA(()),
            ] * earlier,
        ),
        name="feed",
    )(jnp.full((1,), at, jnp.int32), x, up, down, zu, dz, bu, an, au, *g, *((before,) if earlier else ()))


def emit_kernel(earlier, at_ref, active_ref, hidden_ref, down_ref, an_ref, bn_ref, z_in_ref, d_in_ref, *refs):
    step = pl.program_id(0)
    if earlier:
        before_ref, gn_ref, gu_ref, z_ref, out_ref, total_ref, inner_ref, held_ref, sem = refs
        count = held_ref.shape[0]
        copy = pltpu.make_async_copy(before_ref.at[pl.ds(at_ref[0] * count, count), :], held_ref, sem)
    else:
        gn_ref, gu_ref, z_ref, out_ref, total_ref, inner_ref = refs

    @pl.when(step == 0)
    def _():
        if earlier:
            copy.start()
        total_ref[...] = jnp.zeros_like(total_ref)
        inner_ref[...] = jnp.zeros_like(inner_ref)

    active = active_ref[...]
    total_ref[...] += dot_nn(active, down_ref[...])
    inner_ref[...] += dot_nt(active, an_ref[...])
    gn_ref[...] = dot_tn(d_in_ref[...], active).astype(BF16)
    gu_ref[...] = dot_tn(z_in_ref[...], hidden_ref[...]).astype(BF16)

    @pl.when(step == pl.num_programs(0) - 1)
    def _():
        inner = inner_ref[...].astype(BF16)
        z_ref[...] = inner
        total = total_ref[...] + dot_nn(inner, bn_ref[...])
        if earlier:
            copy.wait()
            total = total + held_ref[...]
        out_ref[...] = total.astype(out_ref.dtype)


def emit(at, active, hidden, down, an, bn, zu, dz, before, kind):
    count, ff = active.shape
    width = down.shape[1]
    tile = min(512, ff)
    rank = an.shape[0]
    earlier = before is not None
    cols = pl.BlockSpec((count, tile), lambda t, at: (0, t))
    row = pl.BlockSpec((rank, tile), lambda t, at: (0, t))
    thin = pl.BlockSpec((count, rank), lambda t, at: (at[0], 0))
    return pl.pallas_call(
        functools.partial(emit_kernel, earlier),
        out_shape=(shape((rank, ff)), shape((rank, ff)), shape((count, rank)), shape((count, width), kind)),
        grid_spec=pltpu.PrefetchScalarGridSpec(
            num_scalar_prefetch=1,
            grid=(ff // tile,),
            in_specs=[
                cols, cols, pl.BlockSpec((tile, width), lambda t, at: (t, 0)), row,
                pl.BlockSpec((rank, width), lambda t, at: (0, 0)), thin, thin,
            ] + [REMOTE] * earlier,
            out_specs=(
                row, row, pl.BlockSpec((count, rank), lambda t, at: (0, 0)),
                pl.BlockSpec((count, width), lambda t, at: (0, 0), pipeline_mode=pl.Buffered(1)),
            ),
            scratch_shapes=[pltpu.VMEM((count, width), F32), pltpu.VMEM((count, rank), F32)] + [
                pltpu.VMEM((count, width), F32), pltpu.SemaphoreType.DMA(()),
            ] * earlier,
        ),
        name="emit",
    )(jnp.full((1,), at, jnp.int32), active, hidden, down, an, bn, zu, dz, *((before,) if earlier else ()))


def dense_back_kernel(own_ref, far_ref, cot_ref, gain_ref, bd_ref, ad_ref, middle_ref, w0_ref, w1_ref,
                      low_out_ref, dz_ref, *refs):
    outs = refs[:4]
    mid_ref, w_ref, loads = refs[4:]
    count, width = own_ref.shape
    size = outs[0].shape[1]
    pieces, _, thick, _ = w1_ref.shape
    first = pltpu.make_async_copy(middle_ref.at[pl.ds(0, count), :], mid_ref, loads.at[4])
    first.start()
    pltpu.make_async_copy(w0_ref.reshape(pieces, thick, width), w_ref.at[0], loads.at[0]).start()

    def start(r, carry):
        pltpu.make_async_copy(w1_ref.at[:, r + 3], w_ref.at[r], loads.at[r]).start()
        return carry

    lax.fori_loop(1, 4, start, 0)
    first.wait()
    chunk = min(64, count)

    def norm(i, carry):
        part = pl.ds(pl.multiple_of(i * chunk, chunk), chunk)
        grad = own_ref[part, :].astype(F32) + far_ref[part, :].astype(F32)
        change = norm_back(grad, mid_ref[part, :].astype(F32), gain_ref[...])
        low_out_ref[part, :] = (cot_ref[part, :].astype(F32) + change).astype(BF16)
        return carry

    lax.fori_loop(0, count // chunk, norm, 0)
    dz_ref[...] = dot_nt(low_out_ref[...], bd_ref[...]).astype(BF16)

    def one(r, carry):
        pltpu.make_async_copy(w1_ref.at[:, 0], w_ref.at[r], loads.at[r]).wait()
        weights = w_ref[r].reshape(size, width)
        cols = pl.ds(pl.multiple_of(r * size, size), size)
        value = (dot_nt(low_out_ref[...], weights) + dot_nn(dz_ref[...], ad_ref[:, cols])).astype(BF16)
        for n, out in enumerate(outs):

            @pl.when(r == n)
            def _(out=out):
                out[...] = value

        return carry

    lax.fori_loop(0, 4, one, 0)


def dense_back(own, far, middle, cot, gain, bd, ad, w_own, w_far):
    count, width = own.shape
    rank = bd.shape[0]
    return pl.pallas_call(
        dense_back_kernel,
        out_shape=(shape((count, width)), shape((count, rank))) + (shape((count, width // 4)),) * 4,
        in_specs=[WHOLE] * 6 + [REMOTE] * 3,
        out_specs=(WHOLE,) * 6,
        scratch_shapes=[
            pltpu.VMEM((count, width), BF16), pltpu.VMEM((4, w_far.shape[0]) + w_far.shape[2:], BF16),
            pltpu.SemaphoreType.DMA((5,)),
        ],
        name="dense_back",
    )(own, far, cot, gain, bd, ad, middle, w_own, w_far)


def project_back_kernel(order, at_ref, aq_ref, bq_ref, d_ref, wq_ref, *refs):
    outs = refs[:len(order)]
    part_ref, w_ref, inner_ref, sems, loads = refs[len(order):]
    count = outs[0].shape[0]
    tiles, _, tile, _ = w_ref.shape

    def columns(t):
        return pl.ds(pl.multiple_of(t * tile, tile), tile)

    def fetch(place):
        rows = pl.ds(pl.multiple_of((at_ref[0] ^ order[place]) * count, count), count)
        here = pl.ds(place * count, count)
        return pltpu.make_async_copy(d_ref.at[:, rows, :], part_ref.at[:, here, :], sems.at[place])

    def load(t):
        return pltpu.make_async_copy(wq_ref.at[:, columns(t), :], w_ref.at[t], loads.at[t])

    def start(t, carry):
        load(t).start()
        return carry

    blocks = [fetch(place) for place in range(len(order))]
    for copy in blocks:
        copy.start()
    lax.fori_loop(0, tiles, start, 0)
    for copy in blocks:
        copy.wait()
    inner_ref[...] = sum(dot_nt(part_ref[i], bq_ref[i]) for i in range(3)).astype(BF16)

    def one(t, carry):
        load(t).wait()
        cols = columns(t)
        total = dot_nn(inner_ref[...], aq_ref[:, cols])
        for i in range(3):
            total = total + dot_nt(part_ref[i], w_ref[t, i])
        for place, out in enumerate(outs):
            out[:, cols] = total[place * count:(place + 1) * count].astype(BF16)
        return carry

    lax.fori_loop(0, tiles, one, 0)


def project_back(at, d_merged, wq, aq, bq, order):
    parts, total, local_width = d_merged.shape
    width = wq.shape[1]
    count = total // 4
    tile = min(512, width)
    rows = len(order) * count
    return pl.pallas_call(
        functools.partial(project_back_kernel, order),
        out_shape=(shape((count, width)),) * len(order),
        in_specs=[pl.BlockSpec(memory_space=pltpu.SMEM)] + [WHOLE] * 2 + [REMOTE] * 2,
        out_specs=(WHOLE,) * len(order),
        scratch_shapes=[
            pltpu.VMEM((parts, rows, local_width), BF16), pltpu.VMEM((width // tile, parts, tile, local_width), BF16),
            pltpu.VMEM((rows, aq.shape[0]), BF16),
            pltpu.SemaphoreType.DMA((len(order),)), pltpu.SemaphoreType.DMA((width // tile,)),
        ],
        name="project_back",
    )(at.reshape(1), aq, bq, d_merged, wq)


def inner_kernel(d_ref, z_ref, n_ref, bq_ref, ga_ref, gb_ref):
    step = pl.program_id(0)

    @pl.when(step == 0)
    def _():
        ga_ref[...] = jnp.zeros_like(ga_ref)
        gb_ref[...] = jnp.zeros_like(gb_ref)

    inner = sum(dot_nt(d_ref[i], bq_ref[i]) for i in range(3)).astype(BF16)
    ga_ref[...] += dot_tn(inner, n_ref[...])
    width = d_ref.shape[2]
    for i in range(3):
        gb_ref[:, i * width:(i + 1) * width] += dot_tn(z_ref[...], d_ref[i])


def inner_grads(d_merged, z_qkv, normed, bq):
    parts, total, local_width = d_merged.shape
    width = normed.shape[1]
    rank = z_qkv.shape[1]
    count = total // 2
    return pl.pallas_call(
        inner_kernel,
        out_shape=(shape((rank, width), F32), shape((rank, parts * local_width), F32)),
        grid=(2,),
        in_specs=[
            pl.BlockSpec((parts, count, local_width), lambda i: (0, i, 0)),
            pl.BlockSpec((count, rank), lambda i: (i, 0)),
            pl.BlockSpec((count, width), lambda i: (i, 0)),
            pl.BlockSpec(bq.shape, lambda i: (0, 0, 0)),
        ],
        out_specs=(
            pl.BlockSpec((rank, width), lambda i: (0, 0)),
            pl.BlockSpec((rank, parts * local_width), lambda i: (0, 0)),
        ),
        name="inner_grads",
    )(d_merged, z_qkv, normed, bq)


def spread_kernel(ids_ref, first_ref, second_ref, *outs):
    step = pl.program_id(0)

    @pl.when(step == 0)
    def _():
        for out in outs:
            out[...] = jnp.zeros_like(out)

    which = ids_ref[step]
    ga_up, gb_down, gb_dense, gb_up, ga_down, ga_dense, ga_qkv, gb_qkv = outs
    at = 0
    for out in (ga_up, gb_down, gb_dense, gb_up, ga_down, ga_dense):
        size = out.shape[2]
        out[which] += first_ref[0, :, at:at + size].astype(F32)
        at += size
    size = ga_qkv.shape[2]
    ga_qkv[which] += second_ref[0, :, :size].astype(F32)
    local_width = gb_qkv.shape[3]
    for i in range(3):
        gb_qkv[which, i] += second_ref[0, :, size + i * local_width:size + (i + 1) * local_width].astype(F32)


def spread(ids, first, second, kinds, width, local_width, local_ff):
    copies, rank, _ = first.shape
    dims = [(kinds, rank, n) for n in (width, width, width, local_ff, local_ff, local_width, width)]
    dims.append((kinds, 3, rank, local_width))
    return pl.pallas_call(
        spread_kernel,
        out_shape=tuple(shape(d, F32) for d in dims),
        grid_spec=pltpu.PrefetchScalarGridSpec(
            num_scalar_prefetch=1,
            grid=(copies,),
            in_specs=[
                pl.BlockSpec((1,) + first.shape[1:], lambda s, _: (s, 0, 0)),
                pl.BlockSpec((1,) + second.shape[1:], lambda s, _: (s, 0, 0)),
            ],
            out_specs=tuple(
                pl.BlockSpec(d, lambda s, _, n=len(d): (0,) * n, pipeline_mode=pl.Buffered(1)) for d in dims
            ),
        ),
        name="spread",
    )(ids, first, second)


def last_kernel(kept_ref, one_ref, two_ref, x_ref, d_ref, gain_ref, out_ref):
    grad = kept_ref[...].astype(F32) + one_ref[...].astype(F32) + two_ref[...].astype(F32)
    change = norm_back(grad, x_ref[...].astype(F32), gain_ref[...])
    out_ref[...] = (d_ref[...].astype(F32) + change).astype(BF16)


def last_norm(kept, one, two, x, d, gain):
    count, width = x.shape
    chunk = min(64, count)
    rows = pl.BlockSpec((chunk, width), lambda i: (i, 0))
    return pl.pallas_call(
        last_kernel,
        out_shape=shape((count, width)),
        grid=(count // chunk,),
        in_specs=[rows] * 5 + [pl.BlockSpec((1, width), lambda i: (0, 0))],
        out_specs=rows,
        name="last_norm",
    )(kept, one, two, x, d, gain)


def turned(factor, which):
    return lax.dynamic_index_in_dim(factor.transpose(1, 2, 0), which, 0, False)


def local(
    layer_in, first_gain, first_bias, w_qkv, a_qkv, b_qkv, w_dense, a_dense, b_dense, second_gain, second_bias,
    w_up, a_up, b_up, w_down, a_down, b_down, segment_ids, adapter_ids, cotangent,
):
    own_rows, width = layer_in.shape
    kinds = a_qkv.shape[1]
    rank = a_qkv.shape[2]
    local_width = w_dense.shape[0]
    local_ff = w_up.shape[1]
    local_heads = local_width // HD
    index = lax.axis_index("mp")
    spot = lax.axis_index("dp")
    copies = lax.axis_size("dp")
    total_rows = 4 * own_rows
    low, high = index & 1, index >> 1
    which = adapter_ids[0]
    seg = segment_ids[0]
    head_ids = (index * local_heads + lax.iota(jnp.int32, local_heads)).astype(F32)
    slopes = jnp.exp2(-8.0 * (head_ids + 1.0) / HEADS)
    first_gain, first_bias, second_gain, second_bias = (
        v[None, :] for v in (first_gain, first_bias, second_gain, second_bias)
    )

    aq, ad, au, an = (turned(a, which) for a in (a_qkv, a_dense, a_up, a_down))
    bq = lax.dynamic_index_in_dim(b_qkv.transpose(0, 2, 1, 3), which, 0, False)
    bd, bu, bn = (lax.dynamic_index_in_dim(b, which, 0, False) for b in (b_dense, b_up, b_down))
    wq = w_qkv.transpose(1, 0, 2)

    def slice_of(weight):
        size = weight.shape[0] // copies
        return lax.dynamic_slice_in_dim(weight, spot * size, size, 0)

    x_one = swap(layer_in, "mp", 1)
    x_two = swap(layer_in, "mp", 2)
    wd_slice = slice_of(w_dense)
    size = wd_slice.shape[0]
    ad_flat = ad.reshape(-1, width)
    last = size + ad_flat.shape[0]
    tail = jnp.concatenate([wd_slice, ad_flat], 0)

    def step_in(r, block, held):
        return project(index ^ r, block, first_gain, first_bias, aq, bq, wq, total_rows, held)

    held = step_in(0, layer_in, ())
    wu_halves = jnp.split(slice_of(w_up), 2, axis=0)
    x_one, x_two, *held = lax.optimization_barrier((x_one, x_two, *held))

    x_three = swap(x_two, "mp", 1)
    pack_two = swap(after(jnp.concatenate([tail, bu, an], 0), x_one), "mp", 2)
    wu_first = swap(after(wu_halves[0], x_one), "mp", 2)
    held = step_in(1, x_one, held)
    held = step_in(2, x_two, held)
    x_three, pack_two, wu_first, *held = lax.optimization_barrier((x_three, pack_two, wu_first, *held))

    pack_one = swap(jnp.concatenate([tail, pack_two[:last]], 0), "mp", 1)
    wu_second = swap(after(wu_halves[1], x_three), "mp", 2)
    held = step_in(3, x_three, held)
    merged, normed, z_qkv = held
    other, stat_other = attend(index ^ 2, merged, seg, slopes, 2)
    other, pack_one, pack_two, wu_first, wu_second, merged = lax.optimization_barrier(
        (other, pack_one, pack_two, wu_first, wu_second, merged)
    )

    m_two = swap(other, "mp", 2)
    bu_far, an_far = pack_two[last:last + rank], pack_two[last + rank:]
    packs = (pack_one[:last], pack_two, pack_one[last:])
    slices = jnp.concatenate([wu_first, wu_second, *(p[:size] for p in packs)], 0)
    shared = lax.all_gather(slices, "dp", axis=0).reshape(copies, 7, size, width)
    ad = jnp.concatenate([ad] + [p[size:last].reshape(rank, local_width) for p in packs], 1)
    mine, stat_mine = attend(index, merged, seg, slopes, 2)
    m_two, mine = lax.optimization_barrier((m_two, mine))

    m_one = swap(mine, "mp", 1)
    m_three = swap(m_two, "mp", 1)
    wn_halves = jnp.split(after(slice_of(w_down), m_two), 2, axis=0)
    wn_first = swap(wn_halves[0], "mp", 2)
    m_one, m_three, wn_first = lax.optimization_barrier((m_one, m_three, wn_first))

    m_parts = [mine, m_one, m_two, m_three]
    cot_far = swap(after(cotangent, m_one), "mp", 1)
    wn_second = swap(after(wn_halves[1], m_one), "mp", 2)

    middle, second, z_dense, z_up = dense(
        layer_in, x_one, m_parts, ad, bd, second_gain, second_bias, au, w_dense, shared
    )
    wn_second, second, cot_far = lax.optimization_barrier((wn_second, second, cot_far))
    wn_far = lax.all_gather(jnp.concatenate([wn_first, wn_second], 0), "dp", axis=0, tiled=True)

    cots = (cotangent, cot_far)
    dz_down = jnp.concatenate([dot_nt(c, bn).astype(BF16) for c in cots], 0)
    act, dh, dzu, so_far = feed(
        0, 2 * own_rows, second, cots, w_up.reshape(copies, 4, size, width), w_down, z_up, dz_down, bu, an, au, None, F32
    )
    gn_own, gu_own, zn, out_so_far = emit(0, act, dh, w_down, an, bn, z_up, dz_down, None, F32)
    out_so_far, so_far = lax.optimization_barrier((out_so_far, so_far))
    far_args = (shared, wn_far, z_up, dz_down, bu_far, an_far, au, so_far)
    act_a, dh_a, dzu_a, d_send = feed(1, own_rows, second, (cot_far,), *far_args, BF16)
    second, d_send = lax.optimization_barrier((second, d_send))

    d_near = swap(d_send, "mp", 1)
    act_b, dh_b, dzu_b, d_own = feed(0, own_rows, second, (cotangent,), *far_args, BF16)
    act_a, d_own = lax.optimization_barrier((act_a, d_own))
    gn_a, gu_a, zn_a, out_send = emit(1, act_a, dh_a, wn_far, an_far, bn, z_up, dz_down, out_so_far, BF16)
    d_near, d_own, out_send = lax.optimization_barrier((d_near, d_own, out_send))

    d_low, dz_dense, *d_mixed = dense_back(
        d_own, d_near, middle, cotangent, second_gain, bd, ad, w_dense, shared
    )
    d_low, dz_dense, act_b, *d_mixed = lax.optimization_barrier((d_low, dz_dense, act_b, *d_mixed))
    g_blocks = [d_mixed[0]] + [swap(d_mixed[r], "mp", r) for r in (1, 2, 3)]
    gn_b, gu_b, zn_b, out_own = emit(0, act_b, dh_b, wn_far, an_far, bn, z_up, dz_down, out_so_far, F32)

    def join(value, own, far):
        return (value.astype(F32) + jnp.concatenate([own, far], 0).astype(F32)).astype(BF16)

    ga_up = dot_tn(join(dzu, dzu_b, dzu_a), second)
    zn = join(zn, zn_b, zn_a)
    gb_down = dot_tn(zn[:own_rows], cotangent) + dot_tn(zn[own_rows:], cot_far)
    gb_dense = dot_tn(z_dense[:own_rows], d_low)
    gd = [dot_tn(dz_dense, m[(r % 2) * own_rows:(r % 2 + 1) * own_rows]) for r, m in enumerate(m_parts)]
    gu_far, gn_far = ((a.astype(F32) + b.astype(F32)).astype(BF16) for a, b in ((gu_a, gu_b), (gn_a, gn_b)))
    sums = jnp.concatenate([ga_up, gb_down, gb_dense], 1)
    near = swap(jnp.concatenate([sums, gd[1], gd[3]], 1).astype(BF16), "mp", 1)
    *g_blocks, near = lax.optimization_barrier((*g_blocks, near))

    near = near.astype(F32)
    sums = sums + near[:, :3 * width]
    gd_own = gd[0] + near[:, 3 * width:3 * width + local_width]
    gd_far = gd[2] + near[:, 3 * width + local_width:]
    mate = swap(jnp.concatenate([sums.astype(BF16), gu_far, gn_far, gd_far.astype(BF16)], 1), "mp", 2)
    out_near = swap(after(out_send, near), "mp", 1)
    d_merged = attend_back(index, merged, (mine, other), g_blocks, (stat_mine, stat_other), seg, slopes)
    (send,) = project_back(index, d_merged, wq, aq, bq, (3,))
    send, d_merged, mate, out_near = lax.optimization_barrier((send, d_merged, mate, out_near))

    relay = swap(send, "mp", 1)
    first_pack = jnp.concatenate([sums, gu_own, gn_own, gd_own], 1) + mate.astype(F32)
    first_pack = jnp.concatenate([first_pack.astype(BF16), jnp.full((rank, 128), which, BF16)], 1)
    first_pack = lax.all_gather(first_pack, "dp", axis=0)
    ga_qkv, gb_qkv = inner_grads(d_merged, z_qkv, normed, bq)
    ga_low, d_merged = lax.optimization_barrier((ga_qkv.astype(BF16), d_merged))
    ga_others = [swap(ga_low, "mp", r) for r in (1, 2, 3)]
    send_two, send_one = project_back(index, d_merged, wq, aq, bq, (2, 1))
    relay, send_one, send_two, *ga_others = lax.optimization_barrier((relay, send_one, send_two, *ga_others))

    d_two = swap((send_two.astype(F32) + relay.astype(F32)).astype(BF16), "mp", 2)
    d_one = swap(send_one, "mp", 1)
    layer_out = (middle[:own_rows].astype(F32) + out_own + out_near.astype(F32)).astype(BF16)
    ga_qkv = ga_qkv + sum(g.astype(F32) for g in ga_others)
    second_pack = jnp.concatenate([ga_qkv, gb_qkv], 1).astype(BF16)
    second_pack = lax.all_gather(second_pack, "dp", axis=0)
    ids = first_pack[:, 0, -1].astype(jnp.int32)
    (kept,) = project_back(after(index, ids), d_merged, wq, aq, bq, (0,))
    ga_up, gb_down, gb_dense, gb_up, ga_down, ga_dense, ga_qkv, gb_qkv = spread(
        ids, first_pack, second_pack, kinds, width, local_width, local_ff
    )
    d_one, d_two = lax.optimization_barrier((d_one, d_two, gb_qkv))[:2]
    input_grad = last_norm(kept, d_one, d_two, layer_in, d_low, first_gain)
    return (
        layer_out,
        input_grad,
        ga_qkv.transpose(2, 0, 1),
        gb_qkv.transpose(0, 2, 1, 3),
        ga_dense.transpose(2, 0, 1),
        gb_dense,
        ga_up.transpose(2, 0, 1),
        gb_up,
        ga_down.transpose(2, 0, 1),
        gb_down,
    )


def solution(mesh):
    return jax.shard_map(
        local,
        mesh=mesh,
        in_specs=(
            P(("dp", "mp"), None), P(), P(), P(None, None, "mp"), P(), P(None, None, None, "mp"), P("mp", None),
            P("mp", None, None), P(), P(), P(), P(None, "mp"), P(), P(None, None, "mp"), P("mp", None),
            P("mp", None, None), P(), P("dp", None), P("dp"), P(("dp", "mp"), None),
        ),
        out_specs=(
            P(("dp", "mp"), None), P(("dp", "mp"), None), P(), P(None, None, None, "mp"), P("mp", None, None), P(),
            P(), P(None, None, "mp"), P("mp", None, None), P(),
        ),
        check_vma=False,
    )
```

```python
import functools

import jax
import jax.numpy as jnp
from jax import lax
from jax.experimental import pallas as pl
from jax.experimental.pallas import tpu as pltpu
from jax.sharding import PartitionSpec as P

HEADS = 32
HD = 64
LONGEST = 512
EPSILON = 1e-05
F32 = jnp.float32
BF16 = jnp.bfloat16
MASKED = -1e30
WHOLE = pl.BlockSpec(memory_space=pltpu.VMEM)
REMOTE = pl.BlockSpec(memory_space=pl.ANY)


def shape(dims, kind=BF16):
    return jax.ShapeDtypeStruct(dims, kind)


def statistics(values):
    center = jnp.mean(values, -1, keepdims=True)
    centred = values - center
    variance = jnp.mean(centred * centred, -1, keepdims=True)
    scaler = lax.rsqrt(variance + EPSILON)
    return centred * scaler, scaler


def layer_norm(values, gain, bias):
    return statistics(values)[0] * gain.astype(F32) + bias.astype(F32)


def norm_back(grad, values, gain):
    normal, scaler = statistics(values)
    scaled = grad * gain.astype(F32)
    first_mean = jnp.mean(scaled, -1, keepdims=True)
    second_mean = jnp.mean(scaled * normal, -1, keepdims=True)
    return (scaled - first_mean - normal * second_mean) * scaler


def by_rows(count, body, chunk=32):
    for i in range(count // chunk):
        body(slice(i * chunk, (i + 1) * chunk))


def dot_nn(left, right):
    return jnp.dot(left, right, preferred_element_type=F32)


def dot_nt(left, right):
    return lax.dot_general(left, right, (((1,), (1,)), ((), ())), preferred_element_type=F32)


def dot_tn(left, right):
    return lax.dot_general(left, right, (((0,), (0,)), ((), ())), preferred_element_type=F32)


def swap(value, axis, bit):
    pairs = [(i, i ^ bit) for i in range(lax.axis_size(axis))]
    return lax.ppermute(value, axis, pairs)


def after(value, *others):
    return lax.optimization_barrier((value, *others))[0]


def gelu_pair(values):
    below = 0.5 * (1.0 + lax.erf(values * 0.5 ** 0.5))
    density = jnp.exp(values * values * -0.5) * 0.3989422804014327
    return values * below, below + values * density


def project_kernel(kept, at_ref, x_ref, gain_ref, bias_ref, aq_ref, bq_ref, wq_ref, *refs):
    merged_ref, normed_ref, z_ref, w_ref, out_ref, low_ref, thin_ref, sems, loads = refs[kept:]
    count = x_ref.shape[0]
    rows = pl.ds(pl.multiple_of(at_ref[0] * count, count), count)
    parts = wq_ref.shape[0]

    def load(i):
        return pltpu.make_async_copy(wq_ref.at[i], w_ref.at[i], loads.at[i])

    def save(i):
        return pltpu.make_async_copy(out_ref.at[i], merged_ref.at[i, rows, :], sems.at[2 + i])

    for i in range(parts):
        load(i).start()

    chunk = min(64, count)

    def norm(i, carry):
        part = pl.ds(pl.multiple_of(i * chunk, chunk), chunk)
        low_ref[part, :] = layer_norm(x_ref[part, :].astype(F32), gain_ref[...], bias_ref[...]).astype(BF16)
        return carry

    lax.fori_loop(0, count // chunk, norm, 0)
    copies = [pltpu.make_async_copy(low_ref, normed_ref.at[rows, :], sems.at[0])]
    copies[0].start()
    thin_ref[...] = dot_nt(low_ref[...], aq_ref[...]).astype(BF16)
    copies.append(pltpu.make_async_copy(thin_ref, z_ref.at[rows, :], sems.at[1]))
    copies[1].start()

    width = out_ref.shape[2]
    tile = min(256, width)
    tiles = width // tile

    def one(step, carry):
        i, t = step // tiles, step % tiles
        cols = pl.ds(pl.multiple_of(t * tile, tile), tile)

        @pl.when(t == 0)
        def _():
            load(i).wait()

        value = dot_nn(low_ref[...], w_ref[i, :, cols]) + dot_nn(thin_ref[...], bq_ref[i, :, cols])
        out_ref[i, :, cols] = value.astype(BF16)

        @pl.when(t == tiles - 1)
        def _():
            save(i).start()

        return carry

    lax.fori_loop(0, parts * tiles, one, 0)
    for copy in copies + [save(i) for i in range(parts)]:
        copy.wait()


def project(at, rows, gain, bias, aq, bq, wq, total, earlier):
    count, width = rows.shape
    parts, _, local_width = wq.shape
    rank = aq.shape[0]
    kept = len(earlier)
    return pl.pallas_call(
        functools.partial(project_kernel, kept),
        out_shape=(shape((parts, total, local_width)), shape((total, width)), shape((total, rank))),
        grid_spec=pltpu.PrefetchScalarGridSpec(
            num_scalar_prefetch=1,
            grid=(),
            in_specs=[WHOLE] * 5 + [REMOTE] * (1 + kept),
            out_specs=(REMOTE,) * 3,
            scratch_shapes=[
                pltpu.VMEM(wq.shape, BF16),
                pltpu.VMEM((parts, count, local_width), BF16),
                pltpu.VMEM((count, width), BF16),
                pltpu.VMEM((count, rank), BF16),
                pltpu.SemaphoreType.DMA((2 + parts,)),
                pltpu.SemaphoreType.DMA((parts,)),
            ],
        ),
        input_output_aliases={7 + i: i for i in range(kept)},
        name="project",
    )(at.reshape(1), rows, gain, bias, aq, bq, wq, *earlier)


def lane_mask(half):
    return (lax.broadcasted_iota(jnp.int32, (1, 2 * HD), 1) // HD) == half


def allowed_pairs(seg_col, seg_row, causal):
    dims = (seg_col.shape[0], seg_row.shape[1])
    allowed = seg_col == seg_row
    if causal:
        allowed = allowed & (lax.broadcasted_iota(jnp.int32, dims, 0) <= lax.broadcasted_iota(jnp.int32, dims, 1))
    return allowed


def reach_of(block):
    return -(-LONGEST // block)


def attend_kernel(block, count, first_ref, seg_ref, slope_ref, col_ref, row_ref, q_ref, k_ref, v_ref,
                  o_ref, stat_ref, turned_ref, top_ref, total_ref, sum_ref):
    pair = pl.program_id(0)
    turned_ref[...] = v_ref[0].T

    for own in range(count):
        i = first_ref[0] ^ own
        start = pl.multiple_of(i * block, block)
        here = pl.ds(own * block, block)
        query = q_ref[0, pl.ds(start, block), :] * HD ** -0.5
        scaled = [jnp.where(lane_mask(half), query, 0).astype(BF16) for half in range(2)]

        def one(back):
            at = pl.multiple_of(start - back * block, block)
            keys = pl.ds(at, block)
            allowed = allowed_pairs(col_ref[keys, :1], row_ref[:, pl.ds(start, block)], back == 0)
            place = lax.broadcasted_iota(jnp.int32, (block, block), 0).astype(F32)
            for half in range(2):
                slope = slope_ref[2 * pair + half]
                shift = slope * at.astype(F32)
                scores = jnp.where(allowed, dot_nt(k_ref[0, keys, :], scaled[half]) + slope * place, MASKED)
                best = jnp.max(scores, 0, keepdims=True) + shift
                if back:
                    before = top_ref[half]
                    best = jnp.maximum(best, before)
                weights = jnp.exp(scores - (best - shift))
                total = jnp.sum(weights, 0, keepdims=True)
                result = dot_nn(turned_ref[half * HD:(half + 1) * HD, keys], weights.astype(BF16))
                if back:
                    fade = jnp.exp(before - best)
                    total = total + fade * total_ref[half]
                    result = result + fade * sum_ref[half]
                top_ref[half] = best
                total_ref[half] = total
                sum_ref[half] = result

        one(0)
        for back in range(1, reach_of(block) + 1):
            last = jnp.maximum(start - (back - 1) * block - 1, 0)

            @pl.when((i >= back) & (seg_ref[last] == seg_ref[start]))
            def _(back=back):
                one(back)

        for half in range(2):
            stat_ref[half, :, here] = top_ref[half] + jnp.log(total_ref[half])
        done = jnp.concatenate([sum_ref[half] / total_ref[half] for half in range(2)], 0)
        o_ref[here, :] = done.T.astype(BF16)


def attend(first, merged, seg, col, slopes, count):
    _, rows, width = merged.shape
    block = min(256, rows)
    heads = width // HD

    def part(i):
        return pl.BlockSpec((1, rows, 2 * HD), lambda h, *_: (i, 0, h))

    return pl.pallas_call(
        functools.partial(attend_kernel, block, count),
        out_shape=(shape((count * block, width)), shape((heads, 1, count * block), F32)),
        grid_spec=pltpu.PrefetchScalarGridSpec(
            num_scalar_prefetch=3,
            grid=(heads // 2,),
            in_specs=[
                pl.BlockSpec((rows, 128), lambda h, *_: (0, 0)),
                pl.BlockSpec((1, rows), lambda h, *_: (0, 0)),
                part(0), part(1), part(2),
            ],
            out_specs=(
                pl.BlockSpec((count * block, 2 * HD), lambda h, *_: (0, h)),
                pl.BlockSpec((2, 1, count * block), lambda h, *_: (h, 0, 0)),
            ),
            scratch_shapes=[
                pltpu.VMEM((2 * HD, rows), BF16),
                pltpu.VMEM((2, 1, block), F32),
                pltpu.VMEM((2, 1, block), F32),
                pltpu.VMEM((2, HD, block), F32),
            ],
        ),
        name="attend",
    )(first.reshape(1), seg, slopes, col, seg[None, :], merged, merged, merged)


def attend_back_kernel(block, at_ref, seg_ref, slope_ref, col_ref, row_ref, *refs):
    stats, mixed, grads_in = refs[:2], refs[2:4], refs[4:8]
    q_ref, k_ref, v_ref, d_ref, stat_ref, m_ref, g_ref, turned_ref, center_ref, qsum_ref, ksum_ref, vsum_ref = refs[8:]
    pair = pl.program_id(0)
    count = g_ref.shape[0] // block
    size = grads_in[0].shape[0]
    for r, ref in enumerate(grads_in):
        rows = pl.ds(pl.multiple_of((at_ref[0] ^ r) * size, size), size)
        part = slice((r % 2) * size, (r % 2 + 1) * size)
        g_ref[rows, :] = ref[...]
        m_ref[rows, :] = mixed[r // 2][part, :]
        stat_ref[:, :, rows] = stats[r // 2][:, :, part]
    turned_ref[...] = k_ref[0].T
    product = (g_ref[...].astype(F32) * m_ref[...].astype(F32)).T
    for half in range(2):
        center_ref[half:half + 1] = jnp.sum(product[half * HD:(half + 1) * HD], 0, keepdims=True)
    qsum_ref[...] = jnp.zeros_like(qsum_ref)
    ksum_ref[...] = jnp.zeros_like(ksum_ref)
    vsum_ref[...] = jnp.zeros_like(vsum_ref)

    for i in range(count):
        queries = pl.ds(i * block, block)
        query = q_ref[0, queries, :] * HD ** -0.5
        scaled = [jnp.where(lane_mask(half), query, 0).astype(BF16) for half in range(2)]
        grads = [jnp.where(lane_mask(half), g_ref[queries, :], 0).astype(BF16) for half in range(2)]

        def one(j):
            keys = pl.ds(j * block, block)
            allowed = allowed_pairs(col_ref[keys, :1], row_ref[:, queries], i == j)
            place = lax.broadcasted_iota(jnp.int32, (block, block), 0).astype(F32)
            val_part, key_part = 0.0, 0.0
            for half in range(2):
                slope = slope_ref[2 * pair + half]
                shift = slope * float(j * block)
                scores = jnp.where(allowed, dot_nt(k_ref[0, keys, :], scaled[half]) + slope * place, MASKED)
                probs = jnp.exp(scores - (stat_ref[half, :, queries] - shift))
                d_probs = dot_nt(v_ref[0, keys, :], grads[half])
                d_scores = (probs * (d_probs - center_ref[half:half + 1, queries])).astype(BF16)
                val_part = val_part + dot_nn(probs.astype(BF16), grads[half])
                key_part = key_part + dot_nn(d_scores, scaled[half])
                rows = slice(half * HD, (half + 1) * HD)
                qsum_ref[rows, queries] += dot_nn(turned_ref[rows, keys], d_scores)
            vsum_ref[keys, :] += val_part
            ksum_ref[keys, :] += key_part

        one(i)
        for back in range(1, min(i, reach_of(block)) + 1):
            j = i - back

            @pl.when(seg_ref[j * block + block - 1] == seg_ref[i * block])
            def _(j=j):
                one(j)

    d_ref[0] = (qsum_ref[...] * HD ** -0.5).T.astype(BF16)
    d_ref[1] = ksum_ref[...].astype(BF16)
    d_ref[2] = vsum_ref[...].astype(BF16)


def attend_back(at, merged, mixed, grads, stats, seg, col, slopes):
    parts, rows, width = merged.shape
    block = min(256, rows)
    half = rows // 2

    def wide(count):
        return pl.BlockSpec((count, 2 * HD), lambda h, *_: (0, h))

    def part(i):
        return pl.BlockSpec((1, rows, 2 * HD), lambda h, *_: (i, 0, h))

    return pl.pallas_call(
        functools.partial(attend_back_kernel, block),
        out_shape=shape(merged.shape),
        grid_spec=pltpu.PrefetchScalarGridSpec(
            num_scalar_prefetch=3,
            grid=(width // (2 * HD),),
            in_specs=[
                pl.BlockSpec((rows, 128), lambda h, *_: (0, 0)),
                pl.BlockSpec((1, rows), lambda h, *_: (0, 0)),
            ] + [pl.BlockSpec((2, 1, half), lambda h, *_: (h, 0, 0))] * 2 + [wide(half)] * 2 + [wide(rows // 4)] * 4 + [
                part(0), part(1), part(2),
            ],
            out_specs=pl.BlockSpec((parts, rows, 2 * HD), lambda h, *_: (0, 0, h)),
            scratch_shapes=[
                pltpu.VMEM((2, 1, rows), F32),
                pltpu.VMEM((rows, 2 * HD), BF16),
                pltpu.VMEM((rows, 2 * HD), BF16),
                pltpu.VMEM((2 * HD, rows), BF16),
                pltpu.VMEM((2, rows), F32),
                pltpu.VMEM((2 * HD, rows), F32),
                pltpu.VMEM((rows, 2 * HD), F32),
                pltpu.VMEM((rows, 2 * HD), F32),
            ],
        ),
        name="attend_back",
    )(at.reshape(1), seg, slopes, col, seg[None, :], *stats, *mixed, *grads, merged, merged, merged)


def dense_kernel(x0_ref, x1_ref, m0_ref, m1_ref, m2_ref, m3_ref, a_ref, bd_ref, gain_ref, bias_ref, au_ref,
                 own_ref, far_ref, middle_ref, second_ref, zd_ref, zu_ref, w_ref, m_ref, sum_ref, loads):
    size = m0_ref.shape[1]
    count = x0_ref.shape[0]
    tiles, pieces, _, thick, tile = w_ref.shape

    def columns(t):
        return pl.ds(pl.multiple_of(t * tile, tile), tile)

    def load(t):
        cols = columns(t)
        own = own_ref.reshape(pieces, thick, own_ref.shape[1]).at[:, :, cols]
        far = far_ref.at[:, pl.ds(4, 3), :, cols]
        return (
            pltpu.make_async_copy(own, w_ref.at[t, :, 0], loads.at[0, t]),
            pltpu.make_async_copy(far, w_ref.at[t, :, pl.ds(1, 3)], loads.at[1, t]),
        )

    def start(t, carry):
        for copy in load(t):
            copy.start()
        return carry

    lax.fori_loop(0, tiles, start, 0)
    for r, m in enumerate((m0_ref, m1_ref, m2_ref, m3_ref)):
        cols = slice(r * size, (r + 1) * size)
        m_ref[:count, cols] = m[(r % 2) * count:(r % 2 + 1) * count, :]
        m_ref[count:, cols] = m[(1 - r % 2) * count:(2 - r % 2) * count, :]
    zd_ref[...] = dot_nt(m_ref[...], a_ref[...]).astype(BF16)

    def one(t, carry):
        cols = columns(t)
        for copy in load(t):
            copy.wait()
        total = dot_nn(zd_ref[...], bd_ref[:, cols])
        for r in range(4):
            weights = w_ref[t, :, r].reshape(pieces * thick, tile)
            total = total + dot_nn(m_ref[:, r * size:(r + 1) * size], weights)
        sum_ref[:count, cols] = total[:count] + x0_ref[:, cols].astype(F32)
        sum_ref[count:, cols] = total[count:] + x1_ref[:, cols].astype(F32)
        return carry

    lax.fori_loop(0, tiles, one, 0)
    chunk = min(64, count)

    def norm(i, carry):
        part = pl.ds(pl.multiple_of(i * chunk, chunk), chunk)
        values = sum_ref[part, :]
        middle_ref[part, :] = values.astype(BF16)
        second_ref[part, :] = layer_norm(values, gain_ref[...], bias_ref[...]).astype(BF16)
        return carry

    lax.fori_loop(0, 2 * count // chunk, norm, 0)
    zu_ref[...] = dot_nt(second_ref[...], au_ref[...]).astype(BF16)


def dense(x_own, x_far, m_parts, ad, bd, gain, bias, au, w_own, w_far):
    count, width = x_own.shape
    rank = ad.shape[0]
    tile = min(256, width)
    pieces, _, thick, _ = w_far.shape
    return pl.pallas_call(
        dense_kernel,
        out_shape=(
            shape((2 * count, width)), shape((2 * count, width)), shape((2 * count, rank)),
            shape((2 * count, rank)),
        ),
        in_specs=[WHOLE] * 11 + [REMOTE] * 2,
        out_specs=(WHOLE,) * 4,
        scratch_shapes=[
            pltpu.VMEM((width // tile, pieces, 4, thick, tile), BF16), pltpu.VMEM((2 * count, width), BF16),
            pltpu.VMEM((2 * count, width), F32), pltpu.SemaphoreType.DMA((2, width // tile)),
        ],
        name="dense",
    )(x_own, x_far, *m_parts, ad, bd, gain, bias, au, w_own, w_far)


def feed_kernel(grads, earlier, at_ref, x_ref, up_ref, down_ref, zu_ref, bu_ref, an_ref, au_ref, *refs):
    step = pl.program_id(0)
    g_refs, other_ref, refs = refs[:grads], refs[grads], refs[grads + 1:]
    if earlier:
        before_ref, active_ref, hidden_ref, dz_out_ref, out_ref, g_ref, total_ref, inner_ref, held_ref, sem = refs
        dz_ref = other_ref
        count = held_ref.shape[0]
        copy = pltpu.make_async_copy(before_ref.at[pl.ds(at_ref[0] * count, count), :], held_ref, sem)
    else:
        active_ref, hidden_ref, dz_out_ref, out_ref, dz_ref, g_ref, total_ref, inner_ref = refs

    @pl.when(step == 0)
    def _():
        if earlier:
            copy.start()
        start = 0
        for ref in g_refs:
            g_ref[start:start + ref.shape[0], :] = ref[...]
            start += ref.shape[0]
        total_ref[...] = jnp.zeros_like(total_ref)
        inner_ref[...] = jnp.zeros_like(inner_ref)
        if not earlier:
            dz_ref[...] = dot_nt(g_ref[...], other_ref[...]).astype(BF16)

    up = up_ref[...].reshape(x_ref.shape[1], hidden_ref.shape[1])
    hidden = dot_nn(x_ref[...], up) + dot_nn(zu_ref[...], bu_ref[...])
    d_active = dot_nt(g_ref[...], down_ref[...]) + dot_nn(dz_ref[...], an_ref[...])
    active, slope = gelu_pair(hidden)
    active_ref[...] = active.astype(BF16)
    d_hidden = (d_active * slope).astype(BF16)
    hidden_ref[...] = d_hidden
    total_ref[...] += dot_nt(d_hidden, up)
    inner_ref[...] += dot_nt(d_hidden, bu_ref[...])

    @pl.when(step == pl.num_programs(0) - 1)
    def _():
        inner = inner_ref[...].astype(BF16)
        dz_out_ref[...] = inner
        total = total_ref[...] + dot_nn(inner, au_ref[...])
        if earlier:
            copy.wait()
            total = total + held_ref[...]
        out_ref[...] = total.astype(out_ref.dtype)


def feed(at, count, x, g, up, down, zu, other, bu, an, au, before, kind):
    width = x.shape[1]
    ff = up.shape[3]
    tile = min(512, ff)
    rank = bu.shape[0]
    earlier = before is not None
    once = pl.Buffered(1)
    rows = pl.BlockSpec((count, width), lambda t, at: (at[0], 0), pipeline_mode=once)
    thin = pl.BlockSpec((count, rank), lambda t, at: (at[0], 0))
    cols = pl.BlockSpec((count, tile), lambda t, at: (0, t))
    row = pl.BlockSpec((rank, tile), lambda t, at: (0, t))
    flat = pl.BlockSpec((rank, width), lambda t, at: (0, 0))
    out_shape = [shape((count, ff)), shape((count, ff)), shape((count, rank)), shape((count, width), kind)]
    out_specs = [
        cols, cols, pl.BlockSpec((count, rank), lambda t, at: (0, 0)),
        pl.BlockSpec((count, width), lambda t, at: (0, 0), pipeline_mode=once),
    ]
    scratch = [pltpu.VMEM((count, width), BF16), pltpu.VMEM((count, width), F32), pltpu.VMEM((count, rank), F32)]
    if earlier:
        extra = [thin, REMOTE]
        scratch += [pltpu.VMEM((count, width), F32), pltpu.SemaphoreType.DMA(())]
    else:
        extra = [flat]
        out_shape.append(shape((count, rank)))
        out_specs.append(pl.BlockSpec((count, rank), lambda t, at: (0, 0)))
    return pl.pallas_call(
        functools.partial(feed_kernel, len(g), earlier),
        out_shape=tuple(out_shape),
        grid_spec=pltpu.PrefetchScalarGridSpec(
            num_scalar_prefetch=1,
            grid=(ff // tile,),
            in_specs=[
                rows, pl.BlockSpec((up.shape[0], 4, up.shape[2], tile), lambda t, at: (0, 0, 0, t)),
                pl.BlockSpec((tile, width), lambda t, at: (t, 0)), thin, row, row, flat,
            ] + [pl.BlockSpec(b.shape, lambda t, at: (0, 0), pipeline_mode=once) for b in g] + extra,
            out_specs=tuple(out_specs),
            scratch_shapes=scratch,
        ),
        name="feed",
    )(jnp.full((1,), at, jnp.int32), x, up, down, zu, bu, an, au, *g, other, *((before,) if earlier else ()))


def emit_kernel(earlier, at_ref, active_ref, hidden_ref, down_ref, an_ref, bn_ref, z_in_ref, d_in_ref, *refs):
    if earlier:
        before_ref, gn_ref, gu_ref, z_ref, out_ref = refs
    else:
        gn_ref, gu_ref, z_ref, out_ref = refs

    @pl.when(pl.program_id(0) == 0)
    def _():
        z_ref[...] = dot_nt(active_ref[...], an_ref[...]).astype(BF16)
        gn_ref[...] = dot_tn(d_in_ref[...], active_ref[...]).astype(BF16)
        gu_ref[...] = dot_tn(z_in_ref[...], hidden_ref[...]).astype(BF16)

    total = dot_nn(active_ref[...], down_ref[...]) + dot_nn(z_ref[...], bn_ref[...])
    if earlier:
        total = total + before_ref[...]
    out_ref[...] = total.astype(out_ref.dtype)


def emit(at, active, hidden, down, an, bn, zu, dz, before, kind):
    count, ff = active.shape
    width = down.shape[1]
    tile = min(512, width)
    rank = an.shape[0]
    earlier = before is not None
    once = pl.Buffered(1)
    whole = pl.BlockSpec((count, ff), lambda t, at: (0, 0), pipeline_mode=once)
    flat = pl.BlockSpec((rank, ff), lambda t, at: (0, 0))
    thin = pl.BlockSpec((count, rank), lambda t, at: (at[0], 0))
    return pl.pallas_call(
        functools.partial(emit_kernel, earlier),
        out_shape=(shape((rank, ff)), shape((rank, ff)), shape((count, rank)), shape((count, width), kind)),
        grid_spec=pltpu.PrefetchScalarGridSpec(
            num_scalar_prefetch=1,
            grid=(width // tile,),
            in_specs=[
                whole, whole, pl.BlockSpec((ff, tile), lambda t, at: (0, t)), flat,
                pl.BlockSpec((rank, tile), lambda t, at: (0, t)), thin, thin,
            ] + [pl.BlockSpec((count, tile), lambda t, at: (at[0], t))] * earlier,
            out_specs=(
                flat, flat, pl.BlockSpec((count, rank), lambda t, at: (0, 0)),
                pl.BlockSpec((count, tile), lambda t, at: (0, t)),
            ),
        ),
        name="emit",
    )(jnp.full((1,), at, jnp.int32), active, hidden, down, an, bn, zu, dz, *((before,) if earlier else ()))


def dense_back_kernel(own_ref, far_ref, cot_ref, gain_ref, bd_ref, ad_ref, middle_ref, w0_ref, w1_ref,
                      low_out_ref, dz_ref, *refs):
    outs = refs[:4]
    mid_ref, w_ref, loads = refs[4:]
    count, width = own_ref.shape
    size = outs[0].shape[1]
    pieces, _, thick, _ = w1_ref.shape
    first = pltpu.make_async_copy(middle_ref.at[pl.ds(0, count), :], mid_ref, loads.at[4])
    first.start()
    pltpu.make_async_copy(w0_ref.reshape(pieces, thick, width), w_ref.at[0], loads.at[0]).start()

    def start(r, carry):
        pltpu.make_async_copy(w1_ref.at[:, r + 3], w_ref.at[r], loads.at[r]).start()
        return carry

    lax.fori_loop(1, 4, start, 0)
    first.wait()
    chunk = min(64, count)

    def norm(i, carry):
        part = pl.ds(pl.multiple_of(i * chunk, chunk), chunk)
        grad = own_ref[part, :].astype(F32) + far_ref[part, :].astype(F32)
        change = norm_back(grad, mid_ref[part, :].astype(F32), gain_ref[...])
        low_out_ref[part, :] = (cot_ref[part, :].astype(F32) + change).astype(BF16)
        return carry

    lax.fori_loop(0, count // chunk, norm, 0)
    dz_ref[...] = dot_nt(low_out_ref[...], bd_ref[...]).astype(BF16)

    def one(r, carry):
        pltpu.make_async_copy(w1_ref.at[:, 0], w_ref.at[r], loads.at[r]).wait()
        weights = w_ref[r].reshape(size, width)
        cols = pl.ds(pl.multiple_of(r * size, size), size)
        value = (dot_nt(low_out_ref[...], weights) + dot_nn(dz_ref[...], ad_ref[:, cols])).astype(BF16)
        for n, out in enumerate(outs):

            @pl.when(r == n)
            def _(out=out):
                out[...] = value

        return carry

    lax.fori_loop(0, 4, one, 0)


def dense_back(own, far, middle, cot, gain, bd, ad, w_own, w_far):
    count, width = own.shape
    rank = bd.shape[0]
    return pl.pallas_call(
        dense_back_kernel,
        out_shape=(shape((count, width)), shape((count, rank))) + (shape((count, width // 4)),) * 4,
        in_specs=[WHOLE] * 6 + [REMOTE] * 3,
        out_specs=(WHOLE,) * 6,
        scratch_shapes=[
            pltpu.VMEM((count, width), BF16), pltpu.VMEM((4, w_far.shape[0]) + w_far.shape[2:], BF16),
            pltpu.SemaphoreType.DMA((5,)),
        ],
        name="dense_back",
    )(own, far, cot, gain, bd, ad, middle, w_own, w_far)


def project_back_kernel(order, at_ref, aq_ref, bq_ref, d_ref, wq_ref, *refs):
    outs = refs[:len(order)]
    part_ref, w_ref, inner_ref, sems, loads = refs[len(order):]
    count = outs[0].shape[0]
    tiles, _, tile, _ = w_ref.shape

    def columns(t):
        return pl.ds(pl.multiple_of(t * tile, tile), tile)

    def fetch(place):
        rows = pl.ds(pl.multiple_of((at_ref[0] ^ order[place]) * count, count), count)
        here = pl.ds(place * count, count)
        return pltpu.make_async_copy(d_ref.at[:, rows, :], part_ref.at[:, here, :], sems.at[place])

    def load(t):
        return pltpu.make_async_copy(wq_ref.at[:, columns(t), :], w_ref.at[t], loads.at[t])

    def start(t, carry):
        load(t).start()
        return carry

    blocks = [fetch(place) for place in range(len(order))]
    for copy in blocks:
        copy.start()
    lax.fori_loop(0, tiles, start, 0)
    for copy in blocks:
        copy.wait()
    inner_ref[...] = sum(dot_nt(part_ref[i], bq_ref[i]) for i in range(3)).astype(BF16)

    def one(t, carry):
        load(t).wait()
        cols = columns(t)
        total = dot_nn(inner_ref[...], aq_ref[:, cols])
        for i in range(3):
            total = total + dot_nt(part_ref[i], w_ref[t, i])
        for place, out in enumerate(outs):
            out[:, cols] = total[place * count:(place + 1) * count].astype(BF16)
        return carry

    lax.fori_loop(0, tiles, one, 0)


def project_back(at, d_merged, wq, aq, bq, order):
    parts, total, local_width = d_merged.shape
    width = wq.shape[1]
    count = total // 4
    tile = min(512, width)
    rows = len(order) * count
    return pl.pallas_call(
        functools.partial(project_back_kernel, order),
        out_shape=(shape((count, width)),) * len(order),
        in_specs=[pl.BlockSpec(memory_space=pltpu.SMEM)] + [WHOLE] * 2 + [REMOTE] * 2,
        out_specs=(WHOLE,) * len(order),
        scratch_shapes=[
            pltpu.VMEM((parts, rows, local_width), BF16), pltpu.VMEM((width // tile, parts, tile, local_width), BF16),
            pltpu.VMEM((rows, aq.shape[0]), BF16),
            pltpu.SemaphoreType.DMA((len(order),)), pltpu.SemaphoreType.DMA((width // tile,)),
        ],
        name="project_back",
    )(at.reshape(1), aq, bq, d_merged, wq)


def inner_kernel(d_ref, z_ref, n_ref, bq_ref, ga_ref, gb_ref):
    step = pl.program_id(0)

    @pl.when(step == 0)
    def _():
        ga_ref[...] = jnp.zeros_like(ga_ref)
        gb_ref[...] = jnp.zeros_like(gb_ref)

    inner = sum(dot_nt(d_ref[i], bq_ref[i]) for i in range(3)).astype(BF16)
    ga_ref[...] += dot_tn(inner, n_ref[...])
    width = d_ref.shape[2]
    for i in range(3):
        gb_ref[:, i * width:(i + 1) * width] += dot_tn(z_ref[...], d_ref[i])


def inner_grads(d_merged, z_qkv, normed, bq):
    parts, total, local_width = d_merged.shape
    width = normed.shape[1]
    rank = z_qkv.shape[1]
    count = total // 2
    return pl.pallas_call(
        inner_kernel,
        out_shape=(shape((rank, width), F32), shape((rank, parts * local_width), F32)),
        grid=(2,),
        in_specs=[
            pl.BlockSpec((parts, count, local_width), lambda i: (0, i, 0)),
            pl.BlockSpec((count, rank), lambda i: (i, 0)),
            pl.BlockSpec((count, width), lambda i: (i, 0)),
            pl.BlockSpec(bq.shape, lambda i: (0, 0, 0)),
        ],
        out_specs=(
            pl.BlockSpec((rank, width), lambda i: (0, 0)),
            pl.BlockSpec((rank, parts * local_width), lambda i: (0, 0)),
        ),
        name="inner_grads",
    )(d_merged, z_qkv, normed, bq)


def spread_kernel(ids_ref, first_ref, second_ref, *outs):
    step = pl.program_id(0)

    @pl.when(step == 0)
    def _():
        for out in outs:
            out[...] = jnp.zeros_like(out)

    which = ids_ref[step]
    ga_up, gb_down, gb_dense, gb_up, ga_down, ga_dense, ga_qkv, gb_qkv = outs
    at = 0
    for out in (ga_up, gb_down, gb_dense, gb_up, ga_down, ga_dense):
        size = out.shape[2]
        out[which] += first_ref[0, :, at:at + size].astype(F32)
        at += size
    size = ga_qkv.shape[2]
    ga_qkv[which] += second_ref[0, :, :size].astype(F32)
    local_width = gb_qkv.shape[3]
    for i in range(3):
        gb_qkv[which, i] += second_ref[0, :, size + i * local_width:size + (i + 1) * local_width].astype(F32)


def spread(ids, first, second, kinds, width, local_width, local_ff):
    copies, rank, _ = first.shape
    dims = [(kinds, rank, n) for n in (width, width, width, local_ff, local_ff, local_width, width)]
    dims.append((kinds, 3, rank, local_width))
    return pl.pallas_call(
        spread_kernel,
        out_shape=tuple(shape(d, F32) for d in dims),
        grid_spec=pltpu.PrefetchScalarGridSpec(
            num_scalar_prefetch=1,
            grid=(copies,),
            in_specs=[
                pl.BlockSpec((1,) + first.shape[1:], lambda s, _: (s, 0, 0)),
                pl.BlockSpec((1,) + second.shape[1:], lambda s, _: (s, 0, 0)),
            ],
            out_specs=tuple(
                pl.BlockSpec(d, lambda s, _, n=len(d): (0,) * n, pipeline_mode=pl.Buffered(1)) for d in dims
            ),
        ),
        name="spread",
    )(ids, first, second)


def last_kernel(kept_ref, one_ref, two_ref, x_ref, d_ref, gain_ref, out_ref):
    grad = kept_ref[...].astype(F32) + one_ref[...].astype(F32) + two_ref[...].astype(F32)
    change = norm_back(grad, x_ref[...].astype(F32), gain_ref[...])
    out_ref[...] = (d_ref[...].astype(F32) + change).astype(BF16)


def last_norm(kept, one, two, x, d, gain):
    count, width = x.shape
    chunk = min(64, count)
    rows = pl.BlockSpec((chunk, width), lambda i: (i, 0))
    return pl.pallas_call(
        last_kernel,
        out_shape=shape((count, width)),
        grid=(count // chunk,),
        in_specs=[rows] * 5 + [pl.BlockSpec((1, width), lambda i: (0, 0))],
        out_specs=rows,
        name="last_norm",
    )(kept, one, two, x, d, gain)


def turned(factor, which):
    return lax.dynamic_index_in_dim(factor.transpose(1, 2, 0), which, 0, False)


def local(
    layer_in, first_gain, first_bias, w_qkv, a_qkv, b_qkv, w_dense, a_dense, b_dense, second_gain, second_bias,
    w_up, a_up, b_up, w_down, a_down, b_down, segment_ids, adapter_ids, cotangent,
):
    own_rows, width = layer_in.shape
    kinds = a_qkv.shape[1]
    rank = a_qkv.shape[2]
    local_width = w_dense.shape[0]
    local_ff = w_up.shape[1]
    local_heads = local_width // HD
    index = lax.axis_index("mp")
    spot = lax.axis_index("dp")
    copies = lax.axis_size("dp")
    total_rows = 4 * own_rows
    low, high = index & 1, index >> 1
    which = adapter_ids[0]
    seg = segment_ids[0]
    head_ids = (index * local_heads + lax.iota(jnp.int32, local_heads)).astype(F32)
    slopes = jnp.exp2(-8.0 * (head_ids + 1.0) / HEADS)
    first_gain, first_bias, second_gain, second_bias = (
        v[None, :] for v in (first_gain, first_bias, second_gain, second_bias)
    )

    aq, ad, au, an = (turned(a, which) for a in (a_qkv, a_dense, a_up, a_down))
    bq = lax.dynamic_index_in_dim(b_qkv.transpose(0, 2, 1, 3), which, 0, False)
    bd, bu, bn = (lax.dynamic_index_in_dim(b, which, 0, False) for b in (b_dense, b_up, b_down))
    wq = w_qkv.transpose(1, 0, 2)

    def slice_of(weight):
        size = weight.shape[0] // copies
        return lax.dynamic_slice_in_dim(weight, spot * size, size, 0)

    x_one = swap(layer_in, "mp", 1)
    x_two = swap(layer_in, "mp", 2)
    wd_slice = slice_of(w_dense)
    size = wd_slice.shape[0]
    ad_flat = ad.reshape(-1, width)
    last = size + ad_flat.shape[0]
    tail = jnp.concatenate([wd_slice, ad_flat], 0)

    def step_in(r, block, held):
        return project(index ^ r, block, first_gain, first_bias, aq, bq, wq, total_rows, held)

    held = step_in(0, layer_in, ())
    wu_halves = jnp.split(slice_of(w_up), 2, axis=0)
    wn_halves = jnp.split(slice_of(w_down), 2, axis=0)
    cot_halves = jnp.split(cotangent, 2, axis=0)
    pack = jnp.concatenate([tail, bu, an], 0)
    col = jnp.broadcast_to(seg[:, None], (total_rows, 128))
    early = (au, bd, bn, bu, an, first_bias, second_gain, second_bias, tail, pack, col)
    x_one, x_two, held, early, wu_halves, wn_halves, cot_halves = lax.optimization_barrier(
        (x_one, x_two, held, early, wu_halves, wn_halves, cot_halves)
    )
    au, bd, bn, bu, an, first_bias, second_gain, second_bias, tail, pack, col = early

    x_three = swap(x_two, "mp", 1)
    pack_two = swap(pack, "mp", 2)
    wu_first = swap(wu_halves[0], "mp", 2)
    held = step_in(1, x_one, held)
    held = step_in(2, x_two, held)
    x_three, pack_two, wu_first, *held = lax.optimization_barrier((x_three, pack_two, wu_first, *held))

    pack_one = swap(jnp.concatenate([tail, pack_two[:last]], 0), "mp", 1)
    wu_second = swap(after(wu_halves[1], x_three), "mp", 2)
    held = step_in(3, x_three, held)
    merged, normed, z_qkv = held
    other, stat_other = attend(index ^ 2, merged, seg, col, slopes, 2)
    other, pack_one, pack_two, wu_first, wu_second, merged = lax.optimization_barrier(
        (other, pack_one, pack_two, wu_first, wu_second, merged)
    )

    m_two = swap(other, "mp", 2)
    cot_first = swap(after(cot_halves[0], other), "mp", 1)
    bu_far, an_far = pack_two[last:last + rank], pack_two[last + rank:]
    packs = (pack_one[:last], pack_two, pack_one[last:])
    slices = jnp.concatenate([wu_first, wu_second, *(p[:size] for p in packs)], 0)
    shared = lax.all_gather(slices, "dp", axis=0).reshape(copies, 7, size, width)
    ad = jnp.concatenate([ad] + [p[size:last].reshape(rank, local_width) for p in packs], 1)
    mine, stat_mine = attend(index, merged, seg, col, slopes, 2)
    m_two, mine, cot_first = lax.optimization_barrier((m_two, mine, cot_first))

    m_one = swap(mine, "mp", 1)
    m_three = swap(m_two, "mp", 1)
    wn_first = swap(after(wn_halves[0], m_two), "mp", 2)
    m_one, m_three, wn_first = lax.optimization_barrier((m_one, m_three, wn_first))

    m_parts = [mine, m_one, m_two, m_three]
    cot_second = swap(after(cot_halves[1], m_one), "mp", 1)
    wn_second = swap(after(wn_halves[1], m_one), "mp", 2)
    wn_second, cot_second, shared = lax.optimization_barrier((wn_second, cot_second, shared))
    wn_far = lax.all_gather(jnp.concatenate([wn_first, wn_second], 0), "dp", axis=0, tiled=True)

    middle, second, z_dense, z_up = dense(
        layer_in, x_one, m_parts, ad, bd, second_gain, second_bias, au, w_dense, shared
    )

    cot_parts = (cot_first, cot_second)
    act, dh, dzu, so_far, dz_down = feed(
        0, 2 * own_rows, second, (cotangent, *cot_parts), w_up.reshape(copies, 4, size, width), w_down, z_up, bn, bu, an,
        au, None, F32
    )
    gn_own, gu_own, zn, out_so_far = emit(0, act, dh, w_down, an, bn, z_up, dz_down, None, F32)
    out_so_far, so_far = lax.optimization_barrier((out_so_far, so_far))
    far_args = (shared, wn_far, z_up, dz_down, bu_far, an_far, au, so_far)
    act_a, dh_a, dzu_a, d_send = feed(1, own_rows, second, cot_parts, *far_args, BF16)
    second, d_send = lax.optimization_barrier((second, d_send))

    d_near = swap(d_send, "mp", 1)
    act_b, dh_b, dzu_b, d_own = feed(0, own_rows, second, (cotangent,), *far_args, BF16)
    act_a, d_own = lax.optimization_barrier((act_a, d_own))
    gn_a, gu_a, zn_a, out_send = emit(1, act_a, dh_a, wn_far, an_far, bn, z_up, dz_down, out_so_far, BF16)
    d_near, d_own, out_send = lax.optimization_barrier((d_near, d_own, out_send))

    d_low, dz_dense, *d_mixed = dense_back(
        d_own, d_near, middle, cotangent, second_gain, bd, ad, w_dense, shared
    )
    d_low, dz_dense, act_b, *d_mixed = lax.optimization_barrier((d_low, dz_dense, act_b, *d_mixed))
    g_blocks = [d_mixed[0]] + [swap(d_mixed[r], "mp", r) for r in (1, 2, 3)]
    gn_b, gu_b, zn_b, out_own = emit(0, act_b, dh_b, wn_far, an_far, bn, z_up, dz_down, out_so_far, F32)

    def join(value, own, far):
        return (value.astype(F32) + jnp.concatenate([own, far], 0).astype(F32)).astype(BF16)

    ga_up = dot_tn(join(dzu, dzu_b, dzu_a), second)
    zn = join(zn, zn_b, zn_a)
    gb_down = dot_tn(zn[:own_rows], cotangent) + dot_tn(zn[own_rows:], jnp.concatenate(cot_parts, 0))
    gb_dense = dot_tn(z_dense[:own_rows], d_low)
    gd = [dot_tn(dz_dense, m[(r % 2) * own_rows:(r % 2 + 1) * own_rows]) for r, m in enumerate(m_parts)]
    gu_far, gn_far = ((a.astype(F32) + b.astype(F32)).astype(BF16) for a, b in ((gu_a, gu_b), (gn_a, gn_b)))
    sums = jnp.concatenate([ga_up, gb_down, gb_dense], 1)
    near = swap(jnp.concatenate([sums, gd[1], gd[3]], 1).astype(BF16), "mp", 1)
    *g_blocks, near = lax.optimization_barrier((*g_blocks, near))

    near = near.astype(F32)
    sums = sums + near[:, :3 * width]
    gd_own = gd[0] + near[:, 3 * width:3 * width + local_width]
    gd_far = gd[2] + near[:, 3 * width + local_width:]
    mate = swap(jnp.concatenate([sums.astype(BF16), gu_far, gn_far, gd_far.astype(BF16)], 1), "mp", 2)
    out_near = swap(after(out_send, near), "mp", 1)
    d_merged = attend_back(index, merged, (mine, other), g_blocks, (stat_mine, stat_other), seg, col, slopes)
    (send,) = project_back(index, d_merged, wq, aq, bq, (3,))
    send, d_merged, mate, out_near = lax.optimization_barrier((send, d_merged, mate, out_near))

    relay = swap(send, "mp", 1)
    first_pack = jnp.concatenate([sums, gu_own, gn_own, gd_own], 1) + mate.astype(F32)
    first_pack = jnp.concatenate([first_pack.astype(BF16), jnp.full((rank, 128), which, BF16)], 1)
    first_pack = lax.all_gather(first_pack, "dp", axis=0)
    ga_qkv, gb_qkv = inner_grads(d_merged, z_qkv, normed, bq)
    ga_low, d_merged = lax.optimization_barrier((ga_qkv.astype(BF16), d_merged))
    ga_others = [swap(ga_low, "mp", r) for r in (1, 2, 3)]
    send_two, send_one = project_back(index, d_merged, wq, aq, bq, (2, 1))
    relay, send_one, send_two, *ga_others = lax.optimization_barrier((relay, send_one, send_two, *ga_others))

    d_two = swap((send_two.astype(F32) + relay.astype(F32)).astype(BF16), "mp", 2)
    d_one = swap(send_one, "mp", 1)
    layer_out = (middle[:own_rows].astype(F32) + out_own + out_near.astype(F32)).astype(BF16)
    ga_qkv = ga_qkv + sum(g.astype(F32) for g in ga_others)
    second_pack = jnp.concatenate([ga_qkv, gb_qkv], 1).astype(BF16)
    second_pack = lax.all_gather(second_pack, "dp", axis=0)
    ids = first_pack[:, 0, -1].astype(jnp.int32)
    (kept,) = project_back(after(index, ids), d_merged, wq, aq, bq, (0,))
    ga_up, gb_down, gb_dense, gb_up, ga_down, ga_dense, ga_qkv, gb_qkv = spread(
        ids, first_pack, second_pack, kinds, width, local_width, local_ff
    )
    d_one, d_two = lax.optimization_barrier((d_one, d_two, gb_qkv))[:2]
    input_grad = last_norm(kept, d_one, d_two, layer_in, d_low, first_gain)
    return (
        layer_out,
        input_grad,
        ga_qkv.transpose(2, 0, 1),
        gb_qkv.transpose(0, 2, 1, 3),
        ga_dense.transpose(2, 0, 1),
        gb_dense,
        ga_up.transpose(2, 0, 1),
        gb_up,
        ga_down.transpose(2, 0, 1),
        gb_down,
    )


def solution(mesh):
    return jax.shard_map(
        local,
        mesh=mesh,
        in_specs=(
            P(("dp", "mp"), None), P(), P(), P(None, None, "mp"), P(), P(None, None, None, "mp"), P("mp", None),
            P("mp", None, None), P(), P(), P(), P(None, "mp"), P(), P(None, None, "mp"), P("mp", None),
            P("mp", None, None), P(), P("dp", None), P("dp"), P(("dp", "mp"), None),
        ),
        out_specs=(
            P(("dp", "mp"), None), P(("dp", "mp"), None), P(), P(None, None, None, "mp"), P("mp", None, None), P(),
            P(), P(None, None, "mp"), P("mp", None, None), P(),
        ),
        check_vma=False,
    )
```

```python
import functools

import jax
import jax.numpy as jnp
from jax import lax
from jax.experimental import pallas as pl
from jax.experimental.pallas import tpu as pltpu
from jax.sharding import PartitionSpec as P

HEADS = 32
HD = 64
LONGEST = 512
EPSILON = 1e-05
F32 = jnp.float32
BF16 = jnp.bfloat16
MASKED = -1e30
WHOLE = pl.BlockSpec(memory_space=pltpu.VMEM)
REMOTE = pl.BlockSpec(memory_space=pl.ANY)


def shape(dims, kind=BF16):
    return jax.ShapeDtypeStruct(dims, kind)


def statistics(values):
    center = jnp.mean(values, -1, keepdims=True)
    centred = values - center
    variance = jnp.mean(centred * centred, -1, keepdims=True)
    scaler = lax.rsqrt(variance + EPSILON)
    return centred * scaler, scaler


def layer_norm(values, gain, bias):
    return statistics(values)[0] * gain.astype(F32) + bias.astype(F32)


def norm_back(grad, values, gain):
    normal, scaler = statistics(values)
    scaled = grad * gain.astype(F32)
    first_mean = jnp.mean(scaled, -1, keepdims=True)
    second_mean = jnp.mean(scaled * normal, -1, keepdims=True)
    return (scaled - first_mean - normal * second_mean) * scaler


def by_rows(count, body, chunk=32):
    for i in range(count // chunk):
        body(slice(i * chunk, (i + 1) * chunk))


def dot_nn(left, right):
    return jnp.dot(left, right, preferred_element_type=F32)


def dot_nt(left, right):
    return lax.dot_general(left, right, (((1,), (1,)), ((), ())), preferred_element_type=F32)


def dot_tn(left, right):
    return lax.dot_general(left, right, (((0,), (0,)), ((), ())), preferred_element_type=F32)


def swap(value, axis, bit):
    pairs = [(i, i ^ bit) for i in range(lax.axis_size(axis))]
    return lax.ppermute(value, axis, pairs)


def after(value, *others):
    return lax.optimization_barrier((value, *others))[0]


def gelu_pair(values):
    below = 0.5 * (1.0 + lax.erf(values * 0.5 ** 0.5))
    density = jnp.exp(values * values * -0.5) * 0.3989422804014327
    return values * below, below + values * density


def project_kernel(kept, at_ref, x_ref, gain_ref, bias_ref, aq_ref, bq_ref, wq_ref, *refs):
    merged_ref, normed_ref, z_ref, w_ref, out_ref, low_ref, thin_ref, sems, loads = refs[kept:]
    count = x_ref.shape[0]
    rows = pl.ds(pl.multiple_of(at_ref[0] * count, count), count)
    parts = wq_ref.shape[0]

    def load(i):
        return pltpu.make_async_copy(wq_ref.at[i], w_ref.at[i], loads.at[i])

    def save(i):
        return pltpu.make_async_copy(out_ref.at[i], merged_ref.at[i, rows, :], sems.at[2 + i])

    for i in range(parts):
        load(i).start()

    chunk = min(64, count)

    def norm(i, carry):
        part = pl.ds(pl.multiple_of(i * chunk, chunk), chunk)
        low_ref[part, :] = layer_norm(x_ref[part, :].astype(F32), gain_ref[...], bias_ref[...]).astype(BF16)
        return carry

    lax.fori_loop(0, count // chunk, norm, 0, unroll=2)
    copies = [pltpu.make_async_copy(low_ref, normed_ref.at[rows, :], sems.at[0])]
    copies[0].start()
    thin_ref[...] = dot_nt(low_ref[...], aq_ref[...]).astype(BF16)
    copies.append(pltpu.make_async_copy(thin_ref, z_ref.at[rows, :], sems.at[1]))
    copies[1].start()

    width = out_ref.shape[2]
    tile = min(256, width)
    tiles = width // tile

    def one(step, carry):
        i, t = step // tiles, step % tiles
        cols = pl.ds(pl.multiple_of(t * tile, tile), tile)

        @pl.when(t == 0)
        def _():
            load(i).wait()

        value = dot_nn(low_ref[...], w_ref[i, :, cols]) + dot_nn(thin_ref[...], bq_ref[i, :, cols])
        out_ref[i, :, cols] = value.astype(BF16)

        @pl.when(t == tiles - 1)
        def _():
            save(i).start()

        return carry

    lax.fori_loop(0, parts * tiles, one, 0)
    for copy in copies + [save(i) for i in range(parts)]:
        copy.wait()


def project(at, rows, gain, bias, aq, bq, wq, total, earlier):
    count, width = rows.shape
    parts, _, local_width = wq.shape
    rank = aq.shape[0]
    kept = len(earlier)
    return pl.pallas_call(
        functools.partial(project_kernel, kept),
        out_shape=(shape((parts, total, local_width)), shape((total, width)), shape((total, rank))),
        grid_spec=pltpu.PrefetchScalarGridSpec(
            num_scalar_prefetch=1,
            grid=(),
            in_specs=[WHOLE] * 5 + [REMOTE] * (1 + kept),
            out_specs=(REMOTE,) * 3,
            scratch_shapes=[
                pltpu.VMEM(wq.shape, BF16),
                pltpu.VMEM((parts, count, local_width), BF16),
                pltpu.VMEM((count, width), BF16),
                pltpu.VMEM((count, rank), BF16),
                pltpu.SemaphoreType.DMA((2 + parts,)),
                pltpu.SemaphoreType.DMA((parts,)),
            ],
        ),
        input_output_aliases={7 + i: i for i in range(kept)},
        name="project",
    )(at.reshape(1), rows, gain, bias, aq, bq, wq, *earlier)


def lane_mask(half):
    return (lax.broadcasted_iota(jnp.int32, (1, 2 * HD), 1) // HD) == half


def allowed_pairs(seg_col, seg_row, causal):
    dims = (seg_col.shape[0], seg_row.shape[1])
    allowed = seg_col == seg_row
    if causal:
        allowed = allowed & (lax.broadcasted_iota(jnp.int32, dims, 0) <= lax.broadcasted_iota(jnp.int32, dims, 1))
    return allowed


def reach_of(block):
    return -(-LONGEST // block)


def attend_kernel(block, count, first_ref, seg_ref, slope_ref, col_ref, row_ref, q_ref, k_ref, v_ref,
                  o_ref, stat_ref, turned_ref, top_ref, total_ref, sum_ref):
    pair = pl.program_id(0)
    turned_ref[...] = v_ref[0].T

    for own in range(count):
        i = first_ref[0] ^ own
        start = pl.multiple_of(i * block, block)
        here = pl.ds(own * block, block)
        query = q_ref[0, pl.ds(start, block), :] * HD ** -0.5
        scaled = [jnp.where(lane_mask(half), query, 0).astype(BF16) for half in range(2)]

        def one(back):
            at = pl.multiple_of(start - back * block, block)
            keys = pl.ds(at, block)
            allowed = allowed_pairs(col_ref[keys, :1], row_ref[:, pl.ds(start, block)], back == 0)
            place = lax.broadcasted_iota(jnp.int32, (block, block), 0).astype(F32)
            for half in range(2):
                slope = slope_ref[2 * pair + half]
                shift = slope * at.astype(F32)
                scores = jnp.where(allowed, dot_nt(k_ref[0, keys, :], scaled[half]) + slope * place, MASKED)
                best = jnp.max(scores, 0, keepdims=True) + shift
                if back:
                    before = top_ref[half]
                    best = jnp.maximum(best, before)
                weights = jnp.exp(scores - (best - shift))
                total = jnp.sum(weights, 0, keepdims=True)
                result = dot_nn(turned_ref[half * HD:(half + 1) * HD, keys], weights.astype(BF16))
                if back:
                    fade = jnp.exp(before - best)
                    total = total + fade * total_ref[half]
                    result = result + fade * sum_ref[half]
                top_ref[half] = best
                total_ref[half] = total
                sum_ref[half] = result

        one(0)
        for back in range(1, reach_of(block) + 1):
            last = jnp.maximum(start - (back - 1) * block - 1, 0)

            @pl.when((i >= back) & (seg_ref[last] == seg_ref[start]))
            def _(back=back):
                one(back)

        for half in range(2):
            stat_ref[half, :, here] = top_ref[half] + jnp.log(total_ref[half])
        done = jnp.concatenate([sum_ref[half] / total_ref[half] for half in range(2)], 0)
        o_ref[here, :] = done.T.astype(BF16)


def attend(first, merged, seg, col, slopes, count):
    _, rows, width = merged.shape
    block = min(256, rows)
    heads = width // HD

    def part(i):
        return pl.BlockSpec((1, rows, 2 * HD), lambda h, *_: (i, 0, h))

    return pl.pallas_call(
        functools.partial(attend_kernel, block, count),
        out_shape=(shape((count * block, width)), shape((heads, 1, count * block), F32)),
        grid_spec=pltpu.PrefetchScalarGridSpec(
            num_scalar_prefetch=3,
            grid=(heads // 2,),
            in_specs=[
                pl.BlockSpec((rows, 128), lambda h, *_: (0, 0)),
                pl.BlockSpec((1, rows), lambda h, *_: (0, 0)),
                part(0), part(1), part(2),
            ],
            out_specs=(
                pl.BlockSpec((count * block, 2 * HD), lambda h, *_: (0, h)),
                pl.BlockSpec((2, 1, count * block), lambda h, *_: (h, 0, 0)),
            ),
            scratch_shapes=[
                pltpu.VMEM((2 * HD, rows), BF16),
                pltpu.VMEM((2, 1, block), F32),
                pltpu.VMEM((2, 1, block), F32),
                pltpu.VMEM((2, HD, block), F32),
            ],
        ),
        name="attend",
    )(first.reshape(1), seg, slopes, col, seg[None, :], merged, merged, merged)


def attend_back_kernel(block, at_ref, seg_ref, slope_ref, col_ref, row_ref, *refs):
    stats, mixed, grads_in = refs[:2], refs[2:4], refs[4:8]
    q_ref, k_ref, v_ref, aq_ref, bq_ref, wq_ref, d_ref, send_ref = refs[8:16]
    stat_ref, m_ref, g_ref, turned_ref, center_ref, qsum_ref, ksum_ref, vsum_ref, w_ref, held_ref, loads = refs[16:]
    pair = pl.program_id(0)

    def load(i):
        return pltpu.make_async_copy(wq_ref.at[i], w_ref.at[i], loads.at[i])

    @pl.when(pair == 0)
    def _():
        for i in range(3):
            load(i).start()

    count = g_ref.shape[0] // block
    size = grads_in[0].shape[0]
    for r, ref in enumerate(grads_in):
        rows = pl.ds(pl.multiple_of((at_ref[0] ^ r) * size, size), size)
        part = slice((r % 2) * size, (r % 2 + 1) * size)
        g_ref[rows, :] = ref[...]
        m_ref[rows, :] = mixed[r // 2][part, :]
        stat_ref[:, :, rows] = stats[r // 2][:, :, part]
    turned_ref[...] = k_ref[0].T
    product = (g_ref[...].astype(F32) * m_ref[...].astype(F32)).T
    for half in range(2):
        center_ref[half:half + 1] = jnp.sum(product[half * HD:(half + 1) * HD], 0, keepdims=True)
    qsum_ref[...] = jnp.zeros_like(qsum_ref)
    ksum_ref[...] = jnp.zeros_like(ksum_ref)
    vsum_ref[...] = jnp.zeros_like(vsum_ref)

    for i in range(count):
        queries = pl.ds(i * block, block)
        query = q_ref[0, queries, :] * HD ** -0.5
        scaled = [jnp.where(lane_mask(half), query, 0).astype(BF16) for half in range(2)]
        grads = [jnp.where(lane_mask(half), g_ref[queries, :], 0).astype(BF16) for half in range(2)]

        def one(j):
            keys = pl.ds(j * block, block)
            allowed = allowed_pairs(col_ref[keys, :1], row_ref[:, queries], i == j)
            place = lax.broadcasted_iota(jnp.int32, (block, block), 0).astype(F32)
            val_part, key_part = 0.0, 0.0
            for half in range(2):
                slope = slope_ref[2 * pair + half]
                shift = slope * float(j * block)
                scores = jnp.where(allowed, dot_nt(k_ref[0, keys, :], scaled[half]) + slope * place, MASKED)
                probs = jnp.exp(scores - (stat_ref[half, :, queries] - shift))
                d_probs = dot_nt(v_ref[0, keys, :], grads[half])
                d_scores = (probs * (d_probs - center_ref[half:half + 1, queries])).astype(BF16)
                val_part = val_part + dot_nn(probs.astype(BF16), grads[half])
                key_part = key_part + dot_nn(d_scores, scaled[half])
                rows = slice(half * HD, (half + 1) * HD)
                qsum_ref[rows, queries] += dot_nn(turned_ref[rows, keys], d_scores)
            vsum_ref[keys, :] += val_part
            ksum_ref[keys, :] += key_part

        one(i)
        for back in range(1, min(i, reach_of(block)) + 1):
            j = i - back

            @pl.when(seg_ref[j * block + block - 1] == seg_ref[i * block])
            def _(j=j):
                one(j)

    d_ref[0] = (qsum_ref[...] * HD ** -0.5).T.astype(BF16)
    d_ref[1] = ksum_ref[...].astype(BF16)
    d_ref[2] = vsum_ref[...].astype(BF16)
    sent = pl.ds(pl.multiple_of((at_ref[0] ^ 3) * size, size), size)
    cols = pl.ds(pl.multiple_of(pair * 2 * HD, 2 * HD), 2 * HD)
    for i in range(3):
        held_ref[i, :, cols] = d_ref[i, sent, :]

    @pl.when(pair == pl.num_programs(0) - 1)
    def _():
        for i in range(3):
            load(i).wait()
        inner = sum(dot_nt(held_ref[i], bq_ref[i]) for i in range(3)).astype(BF16)
        tile = 512

        def one(t, carry):
            here = pl.ds(pl.multiple_of(t * tile, tile), tile)
            total = dot_nn(inner, aq_ref[:, here])
            for i in range(3):
                total = total + dot_nt(held_ref[i], w_ref[i, here, :])
            send_ref[:, here] = total.astype(BF16)
            return carry

        lax.fori_loop(0, send_ref.shape[1] // tile, one, 0)


def attend_back(at, merged, mixed, grads, stats, seg, col, slopes, aq, bq, wq):
    parts, rows, width = merged.shape
    block = min(256, rows)
    half = rows // 2

    def wide(count):
        return pl.BlockSpec((count, 2 * HD), lambda h, *_: (0, h))

    def part(i):
        return pl.BlockSpec((1, rows, 2 * HD), lambda h, *_: (i, 0, h))

    return pl.pallas_call(
        functools.partial(attend_back_kernel, block),
        out_shape=(shape(merged.shape), shape((rows // 4, aq.shape[1]))),
        grid_spec=pltpu.PrefetchScalarGridSpec(
            num_scalar_prefetch=3,
            grid=(width // (2 * HD),),
            in_specs=[
                pl.BlockSpec((rows, 128), lambda h, *_: (0, 0)),
                pl.BlockSpec((1, rows), lambda h, *_: (0, 0)),
            ] + [pl.BlockSpec((2, 1, half), lambda h, *_: (h, 0, 0))] * 2 + [wide(half)] * 2 + [wide(rows // 4)] * 4 + [
                part(0), part(1), part(2),
                pl.BlockSpec(aq.shape, lambda h, *_: (0, 0)), pl.BlockSpec(bq.shape, lambda h, *_: (0, 0, 0)), REMOTE,
            ],
            out_specs=(
                pl.BlockSpec((parts, rows, 2 * HD), lambda h, *_: (0, 0, h)),
                pl.BlockSpec((rows // 4, aq.shape[1]), lambda h, *_: (0, 0)),
            ),
            scratch_shapes=[
                pltpu.VMEM((2, 1, rows), F32),
                pltpu.VMEM((rows, 2 * HD), BF16),
                pltpu.VMEM((rows, 2 * HD), BF16),
                pltpu.VMEM((2 * HD, rows), BF16),
                pltpu.VMEM((2, rows), F32),
                pltpu.VMEM((2 * HD, rows), F32),
                pltpu.VMEM((rows, 2 * HD), F32),
                pltpu.VMEM((rows, 2 * HD), F32),
                pltpu.VMEM(wq.shape, BF16),
                pltpu.VMEM((parts, rows // 4, width), BF16),
                pltpu.SemaphoreType.DMA((parts,)),
            ],
        ),
        name="attend_back",
    )(at.reshape(1), seg, slopes, col, seg[None, :], *stats, *mixed, *grads, merged, merged, merged, aq, bq, wq)


def dense_kernel(x0_ref, x1_ref, m0_ref, m1_ref, m2_ref, m3_ref, a_ref, bd_ref, gain_ref, bias_ref, au_ref,
                 own_ref, far_ref, middle_ref, second_ref, zd_ref, zu_ref, w_ref, m_ref, sum_ref, loads):
    size = m0_ref.shape[1]
    count = x0_ref.shape[0]
    tiles, pieces, _, thick, tile = w_ref.shape

    def columns(t):
        return pl.ds(pl.multiple_of(t * tile, tile), tile)

    def load(t):
        cols = columns(t)
        own = own_ref.reshape(pieces, thick, own_ref.shape[1]).at[:, :, cols]
        far = far_ref.at[:, pl.ds(4, 3), :, cols]
        return (
            pltpu.make_async_copy(own, w_ref.at[t, :, 0], loads.at[0, t]),
            pltpu.make_async_copy(far, w_ref.at[t, :, pl.ds(1, 3)], loads.at[1, t]),
        )

    def start(t, carry):
        for copy in load(t):
            copy.start()
        return carry

    lax.fori_loop(0, tiles, start, 0)
    for r, m in enumerate((m0_ref, m1_ref, m2_ref, m3_ref)):
        cols = slice(r * size, (r + 1) * size)
        m_ref[:count, cols] = m[(r % 2) * count:(r % 2 + 1) * count, :]
        m_ref[count:, cols] = m[(1 - r % 2) * count:(2 - r % 2) * count, :]
    zd_ref[...] = dot_nt(m_ref[...], a_ref[...]).astype(BF16)

    def one(t, carry):
        cols = columns(t)
        for copy in load(t):
            copy.wait()
        total = dot_nn(zd_ref[...], bd_ref[:, cols])
        for r in range(4):
            weights = w_ref[t, :, r].reshape(pieces * thick, tile)
            total = total + dot_nn(m_ref[:, r * size:(r + 1) * size], weights)
        sum_ref[:count, cols] = total[:count] + x0_ref[:, cols].astype(F32)
        sum_ref[count:, cols] = total[count:] + x1_ref[:, cols].astype(F32)
        return carry

    lax.fori_loop(0, tiles, one, 0)
    chunk = min(64, count)

    def norm(i, carry):
        part = pl.ds(pl.multiple_of(i * chunk, chunk), chunk)
        values = sum_ref[part, :]
        middle_ref[part, :] = values.astype(BF16)
        second_ref[part, :] = layer_norm(values, gain_ref[...], bias_ref[...]).astype(BF16)
        return carry

    lax.fori_loop(0, 2 * count // chunk, norm, 0, unroll=2)
    zu_ref[...] = dot_nt(second_ref[...], au_ref[...]).astype(BF16)


def dense(x_own, x_far, m_parts, ad, bd, gain, bias, au, w_own, w_far):
    count, width = x_own.shape
    rank = ad.shape[0]
    tile = min(256, width)
    pieces, _, thick, _ = w_far.shape
    return pl.pallas_call(
        dense_kernel,
        out_shape=(
            shape((2 * count, width)), shape((2 * count, width)), shape((2 * count, rank)),
            shape((2 * count, rank)),
        ),
        in_specs=[WHOLE] * 11 + [REMOTE] * 2,
        out_specs=(WHOLE,) * 4,
        scratch_shapes=[
            pltpu.VMEM((width // tile, pieces, 4, thick, tile), BF16), pltpu.VMEM((2 * count, width), BF16),
            pltpu.VMEM((2 * count, width), F32), pltpu.SemaphoreType.DMA((2, width // tile)),
        ],
        name="dense",
    )(x_own, x_far, *m_parts, ad, bd, gain, bias, au, w_own, w_far)


def feed_kernel(grads, earlier, at_ref, x_ref, up_ref, down_ref, zu_ref, bu_ref, an_ref, au_ref, *refs):
    step = pl.program_id(0)
    g_refs, other_ref, refs = refs[:grads], refs[grads], refs[grads + 1:]
    if earlier:
        before_ref, active_ref, hidden_ref, dz_out_ref, out_ref, g_ref, total_ref, inner_ref, held_ref, sem = refs
        dz_ref = other_ref
        count = held_ref.shape[0]
        copy = pltpu.make_async_copy(before_ref.at[pl.ds(at_ref[0] * count, count), :], held_ref, sem)
    else:
        active_ref, hidden_ref, dz_out_ref, out_ref, dz_ref, g_ref, total_ref, inner_ref = refs

    @pl.when(step == 0)
    def _():
        if earlier:
            copy.start()
        start = 0
        for ref in g_refs:
            g_ref[start:start + ref.shape[0], :] = ref[...]
            start += ref.shape[0]
        total_ref[...] = jnp.zeros_like(total_ref)
        inner_ref[...] = jnp.zeros_like(inner_ref)
        if not earlier:
            dz_ref[...] = dot_nt(g_ref[...], other_ref[...]).astype(BF16)

    up = up_ref[...].reshape(x_ref.shape[1], hidden_ref.shape[1])
    hidden = dot_nn(x_ref[...], up) + dot_nn(zu_ref[...], bu_ref[...])
    d_active = dot_nt(g_ref[...], down_ref[...]) + dot_nn(dz_ref[...], an_ref[...])
    active, slope = gelu_pair(hidden)
    active_ref[...] = active.astype(BF16)
    d_hidden = (d_active * slope).astype(BF16)
    hidden_ref[...] = d_hidden
    total_ref[...] += dot_nt(d_hidden, up)
    inner_ref[...] += dot_nt(d_hidden, bu_ref[...])

    @pl.when(step == pl.num_programs(0) - 1)
    def _():
        inner = inner_ref[...].astype(BF16)
        dz_out_ref[...] = inner
        total = total_ref[...] + dot_nn(inner, au_ref[...])
        if earlier:
            copy.wait()
            total = total + held_ref[...]
        out_ref[...] = total.astype(out_ref.dtype)


def feed(at, count, x, g, up, down, zu, other, bu, an, au, before, kind):
    width = x.shape[1]
    ff = up.shape[3]
    tile = min(512, ff)
    rank = bu.shape[0]
    earlier = before is not None
    once = pl.Buffered(1)
    rows = pl.BlockSpec((count, width), lambda t, at: (at[0], 0), pipeline_mode=once)
    thin = pl.BlockSpec((count, rank), lambda t, at: (at[0], 0))
    cols = pl.BlockSpec((count, tile), lambda t, at: (0, t))
    row = pl.BlockSpec((rank, tile), lambda t, at: (0, t))
    flat = pl.BlockSpec((rank, width), lambda t, at: (0, 0))
    out_shape = [shape((count, ff)), shape((count, ff)), shape((count, rank)), shape((count, width), kind)]
    out_specs = [
        cols, cols, pl.BlockSpec((count, rank), lambda t, at: (0, 0)),
        pl.BlockSpec((count, width), lambda t, at: (0, 0), pipeline_mode=once),
    ]
    scratch = [pltpu.VMEM((count, width), BF16), pltpu.VMEM((count, width), F32), pltpu.VMEM((count, rank), F32)]
    if earlier:
        extra = [thin, REMOTE]
        scratch += [pltpu.VMEM((count, width), F32), pltpu.SemaphoreType.DMA(())]
    else:
        extra = [flat]
        out_shape.append(shape((count, rank)))
        out_specs.append(pl.BlockSpec((count, rank), lambda t, at: (0, 0)))
    return pl.pallas_call(
        functools.partial(feed_kernel, len(g), earlier),
        out_shape=tuple(out_shape),
        grid_spec=pltpu.PrefetchScalarGridSpec(
            num_scalar_prefetch=1,
            grid=(ff // tile,),
            in_specs=[
                rows, pl.BlockSpec((up.shape[0], 4, up.shape[2], tile), lambda t, at: (0, 0, 0, t)),
                pl.BlockSpec((tile, width), lambda t, at: (t, 0)), thin, row, row, flat,
            ] + [pl.BlockSpec(b.shape, lambda t, at: (0, 0), pipeline_mode=once) for b in g] + extra,
            out_specs=tuple(out_specs),
            scratch_shapes=scratch,
        ),
        name="feed",
    )(jnp.full((1,), at, jnp.int32), x, up, down, zu, bu, an, au, *g, other, *((before,) if earlier else ()))


def emit_kernel(earlier, at_ref, active_ref, hidden_ref, down_ref, an_ref, bn_ref, z_in_ref, d_in_ref, *refs):
    if earlier:
        before_ref, gn_ref, gu_ref, z_ref, out_ref = refs
    else:
        gn_ref, gu_ref, z_ref, out_ref = refs

    @pl.when(pl.program_id(0) == 0)
    def _():
        z_ref[...] = dot_nt(active_ref[...], an_ref[...]).astype(BF16)
        gn_ref[...] = dot_tn(d_in_ref[...], active_ref[...]).astype(BF16)
        gu_ref[...] = dot_tn(z_in_ref[...], hidden_ref[...]).astype(BF16)

    total = dot_nn(active_ref[...], down_ref[...]) + dot_nn(z_ref[...], bn_ref[...])
    if earlier:
        total = total + before_ref[...]
    out_ref[...] = total.astype(out_ref.dtype)


def emit(at, active, hidden, down, an, bn, zu, dz, before, kind):
    count, ff = active.shape
    width = down.shape[1]
    tile = min(512, width)
    rank = an.shape[0]
    earlier = before is not None
    once = pl.Buffered(1)
    whole = pl.BlockSpec((count, ff), lambda t, at: (0, 0), pipeline_mode=once)
    flat = pl.BlockSpec((rank, ff), lambda t, at: (0, 0))
    thin = pl.BlockSpec((count, rank), lambda t, at: (at[0], 0))
    return pl.pallas_call(
        functools.partial(emit_kernel, earlier),
        out_shape=(shape((rank, ff)), shape((rank, ff)), shape((count, rank)), shape((count, width), kind)),
        grid_spec=pltpu.PrefetchScalarGridSpec(
            num_scalar_prefetch=1,
            grid=(width // tile,),
            in_specs=[
                whole, whole, pl.BlockSpec((ff, tile), lambda t, at: (0, t)), flat,
                pl.BlockSpec((rank, tile), lambda t, at: (0, t)), thin, thin,
            ] + [pl.BlockSpec((count, tile), lambda t, at: (at[0], t))] * earlier,
            out_specs=(
                flat, flat, pl.BlockSpec((count, rank), lambda t, at: (0, 0)),
                pl.BlockSpec((count, tile), lambda t, at: (0, t)),
            ),
        ),
        name="emit",
    )(jnp.full((1,), at, jnp.int32), active, hidden, down, an, bn, zu, dz, *((before,) if earlier else ()))


def dense_back_kernel(own_ref, far_ref, cot_ref, gain_ref, bd_ref, ad_ref, middle_ref, w0_ref, w1_ref,
                      low_out_ref, dz_ref, *refs):
    outs = refs[:4]
    mid_ref, w_ref, loads = refs[4:]
    count, width = own_ref.shape
    size = outs[0].shape[1]
    pieces, _, thick, _ = w1_ref.shape
    first = pltpu.make_async_copy(middle_ref.at[pl.ds(0, count), :], mid_ref, loads.at[4])
    first.start()
    pltpu.make_async_copy(w0_ref.reshape(pieces, thick, width), w_ref.at[0], loads.at[0]).start()

    def start(r, carry):
        pltpu.make_async_copy(w1_ref.at[:, r + 3], w_ref.at[r], loads.at[r]).start()
        return carry

    lax.fori_loop(1, 4, start, 0)
    first.wait()
    chunk = min(64, count)

    def norm(i, carry):
        part = pl.ds(pl.multiple_of(i * chunk, chunk), chunk)
        grad = own_ref[part, :].astype(F32) + far_ref[part, :].astype(F32)
        change = norm_back(grad, mid_ref[part, :].astype(F32), gain_ref[...])
        low_out_ref[part, :] = (cot_ref[part, :].astype(F32) + change).astype(BF16)
        return carry

    lax.fori_loop(0, count // chunk, norm, 0, unroll=2)
    dz_ref[...] = dot_nt(low_out_ref[...], bd_ref[...]).astype(BF16)

    def one(r, carry):
        pltpu.make_async_copy(w1_ref.at[:, 0], w_ref.at[r], loads.at[r]).wait()
        weights = w_ref[r].reshape(size, width)
        cols = pl.ds(pl.multiple_of(r * size, size), size)
        value = (dot_nt(low_out_ref[...], weights) + dot_nn(dz_ref[...], ad_ref[:, cols])).astype(BF16)
        for n, out in enumerate(outs):

            @pl.when(r == n)
            def _(out=out):
                out[...] = value

        return carry

    lax.fori_loop(0, 4, one, 0)


def dense_back(own, far, middle, cot, gain, bd, ad, w_own, w_far):
    count, width = own.shape
    rank = bd.shape[0]
    return pl.pallas_call(
        dense_back_kernel,
        out_shape=(shape((count, width)), shape((count, rank))) + (shape((count, width // 4)),) * 4,
        in_specs=[WHOLE] * 6 + [REMOTE] * 3,
        out_specs=(WHOLE,) * 6,
        scratch_shapes=[
            pltpu.VMEM((count, width), BF16), pltpu.VMEM((4, w_far.shape[0]) + w_far.shape[2:], BF16),
            pltpu.SemaphoreType.DMA((5,)),
        ],
        name="dense_back",
    )(own, far, cot, gain, bd, ad, middle, w_own, w_far)


def project_back_kernel(order, at_ref, aq_ref, bq_ref, d_ref, wq_ref, *refs):
    outs = refs[:len(order)]
    part_ref, w_ref, inner_ref, sems, loads = refs[len(order):]
    count = outs[0].shape[0]
    tiles, _, tile, _ = w_ref.shape

    def columns(t):
        return pl.ds(pl.multiple_of(t * tile, tile), tile)

    def fetch(place):
        rows = pl.ds(pl.multiple_of((at_ref[0] ^ order[place]) * count, count), count)
        here = pl.ds(place * count, count)
        return pltpu.make_async_copy(d_ref.at[:, rows, :], part_ref.at[:, here, :], sems.at[place])

    def load(t):
        return pltpu.make_async_copy(wq_ref.at[:, columns(t), :], w_ref.at[t], loads.at[t])

    def start(t, carry):
        load(t).start()
        return carry

    blocks = [fetch(place) for place in range(len(order))]
    for copy in blocks:
        copy.start()
    lax.fori_loop(0, tiles, start, 0)
    for copy in blocks:
        copy.wait()
    inner_ref[...] = sum(dot_nt(part_ref[i], bq_ref[i]) for i in range(3)).astype(BF16)

    def one(t, carry):
        load(t).wait()
        cols = columns(t)
        total = dot_nn(inner_ref[...], aq_ref[:, cols])
        for i in range(3):
            total = total + dot_nt(part_ref[i], w_ref[t, i])
        for place, out in enumerate(outs):
            out[:, cols] = total[place * count:(place + 1) * count].astype(BF16)
        return carry

    lax.fori_loop(0, tiles, one, 0)


def project_back(at, d_merged, wq, aq, bq, order):
    parts, total, local_width = d_merged.shape
    width = wq.shape[1]
    count = total // 4
    tile = min(512, width)
    rows = len(order) * count
    return pl.pallas_call(
        functools.partial(project_back_kernel, order),
        out_shape=(shape((count, width)),) * len(order),
        in_specs=[pl.BlockSpec(memory_space=pltpu.SMEM)] + [WHOLE] * 2 + [REMOTE] * 2,
        out_specs=(WHOLE,) * len(order),
        scratch_shapes=[
            pltpu.VMEM((parts, rows, local_width), BF16), pltpu.VMEM((width // tile, parts, tile, local_width), BF16),
            pltpu.VMEM((rows, aq.shape[0]), BF16),
            pltpu.SemaphoreType.DMA((len(order),)), pltpu.SemaphoreType.DMA((width // tile,)),
        ],
        name="project_back",
    )(at.reshape(1), aq, bq, d_merged, wq)


def inner_kernel(d_ref, z_ref, n_ref, bq_ref, ga_ref, gb_ref):
    step = pl.program_id(0)

    @pl.when(step == 0)
    def _():
        ga_ref[...] = jnp.zeros_like(ga_ref)
        gb_ref[...] = jnp.zeros_like(gb_ref)

    inner = sum(dot_nt(d_ref[i], bq_ref[i]) for i in range(3)).astype(BF16)
    ga_ref[...] += dot_tn(inner, n_ref[...])
    width = d_ref.shape[2]
    for i in range(3):
        gb_ref[:, i * width:(i + 1) * width] += dot_tn(z_ref[...], d_ref[i])


def inner_grads(d_merged, z_qkv, normed, bq):
    parts, total, local_width = d_merged.shape
    width = normed.shape[1]
    rank = z_qkv.shape[1]
    count = total // 2
    return pl.pallas_call(
        inner_kernel,
        out_shape=(shape((rank, width), F32), shape((rank, parts * local_width), F32)),
        grid=(2,),
        in_specs=[
            pl.BlockSpec((parts, count, local_width), lambda i: (0, i, 0)),
            pl.BlockSpec((count, rank), lambda i: (i, 0)),
            pl.BlockSpec((count, width), lambda i: (i, 0)),
            pl.BlockSpec(bq.shape, lambda i: (0, 0, 0)),
        ],
        out_specs=(
            pl.BlockSpec((rank, width), lambda i: (0, 0)),
            pl.BlockSpec((rank, parts * local_width), lambda i: (0, 0)),
        ),
        name="inner_grads",
    )(d_merged, z_qkv, normed, bq)


def spread_kernel(ids_ref, first_ref, second_ref, *outs):
    step = pl.program_id(0)

    @pl.when(step == 0)
    def _():
        for out in outs:
            out[...] = jnp.zeros_like(out)

    which = ids_ref[step]
    ga_up, gb_down, gb_dense, gb_up, ga_down, ga_dense, ga_qkv, gb_qkv = outs
    at = 0
    for out in (ga_up, gb_down, gb_dense, gb_up, ga_down, ga_dense):
        size = out.shape[2]
        out[which] += first_ref[0, :, at:at + size].astype(F32)
        at += size
    size = ga_qkv.shape[2]
    ga_qkv[which] += second_ref[0, :, :size].astype(F32)
    local_width = gb_qkv.shape[3]
    for i in range(3):
        gb_qkv[which, i] += second_ref[0, :, size + i * local_width:size + (i + 1) * local_width].astype(F32)


def spread(ids, first, second, kinds, width, local_width, local_ff):
    copies, rank, _ = first.shape
    dims = [(kinds, rank, n) for n in (width, width, width, local_ff, local_ff, local_width, width)]
    dims.append((kinds, 3, rank, local_width))
    return pl.pallas_call(
        spread_kernel,
        out_shape=tuple(shape(d, F32) for d in dims),
        grid_spec=pltpu.PrefetchScalarGridSpec(
            num_scalar_prefetch=1,
            grid=(copies,),
            in_specs=[
                pl.BlockSpec((1,) + first.shape[1:], lambda s, _: (s, 0, 0)),
                pl.BlockSpec((1,) + second.shape[1:], lambda s, _: (s, 0, 0)),
            ],
            out_specs=tuple(
                pl.BlockSpec(d, lambda s, _, n=len(d): (0,) * n, pipeline_mode=pl.Buffered(1)) for d in dims
            ),
        ),
        name="spread",
    )(ids, first, second)


def last_kernel(kept_ref, one_ref, two_ref, x_ref, d_ref, gain_ref, out_ref):
    grad = kept_ref[...].astype(F32) + one_ref[...].astype(F32) + two_ref[...].astype(F32)
    change = norm_back(grad, x_ref[...].astype(F32), gain_ref[...])
    out_ref[...] = (d_ref[...].astype(F32) + change).astype(BF16)


def last_norm(kept, one, two, x, d, gain):
    count, width = x.shape
    chunk = min(128, count)
    rows = pl.BlockSpec((chunk, width), lambda i: (i, 0))
    return pl.pallas_call(
        last_kernel,
        out_shape=shape((count, width)),
        grid=(count // chunk,),
        in_specs=[rows] * 5 + [pl.BlockSpec((1, width), lambda i: (0, 0))],
        out_specs=rows,
        name="last_norm",
    )(kept, one, two, x, d, gain)


def turned(factor, which):
    return lax.dynamic_index_in_dim(factor.transpose(1, 2, 0), which, 0, False)


def local(
    layer_in, first_gain, first_bias, w_qkv, a_qkv, b_qkv, w_dense, a_dense, b_dense, second_gain, second_bias,
    w_up, a_up, b_up, w_down, a_down, b_down, segment_ids, adapter_ids, cotangent,
):
    own_rows, width = layer_in.shape
    kinds = a_qkv.shape[1]
    rank = a_qkv.shape[2]
    local_width = w_dense.shape[0]
    local_ff = w_up.shape[1]
    local_heads = local_width // HD
    index = lax.axis_index("mp")
    spot = lax.axis_index("dp")
    copies = lax.axis_size("dp")
    total_rows = 4 * own_rows
    low, high = index & 1, index >> 1
    which = adapter_ids[0]
    seg = segment_ids[0]
    head_ids = (index * local_heads + lax.iota(jnp.int32, local_heads)).astype(F32)
    slopes = jnp.exp2(-8.0 * (head_ids + 1.0) / HEADS)
    first_gain, first_bias, second_gain, second_bias = (
        v[None, :] for v in (first_gain, first_bias, second_gain, second_bias)
    )

    aq, ad, au, an = (turned(a, which) for a in (a_qkv, a_dense, a_up, a_down))
    bq = lax.dynamic_index_in_dim(b_qkv.transpose(0, 2, 1, 3), which, 0, False)
    bd, bu, bn = (lax.dynamic_index_in_dim(b, which, 0, False) for b in (b_dense, b_up, b_down))
    wq = w_qkv.transpose(1, 0, 2)

    def slice_of(weight):
        size = weight.shape[0] // copies
        return lax.dynamic_slice_in_dim(weight, spot * size, size, 0)

    x_one = swap(layer_in, "mp", 1)
    x_two = swap(layer_in, "mp", 2)
    wd_slice = slice_of(w_dense)
    size = wd_slice.shape[0]
    ad_flat = ad.reshape(-1, width)
    last = size + ad_flat.shape[0]
    tail = jnp.concatenate([wd_slice, ad_flat], 0)

    def step_in(r, block, held):
        return project(index ^ r, block, first_gain, first_bias, aq, bq, wq, total_rows, held)

    held = step_in(0, layer_in, ())
    wu_halves = jnp.split(slice_of(w_up), 2, axis=0)
    wn_halves = slice_of(w_down)
    wn_halves = jnp.split(wn_halves, [3 * wn_halves.shape[0] // 4], axis=0)
    cot_halves = jnp.split(cotangent, 2, axis=0)
    pack = jnp.concatenate([tail, bu, an], 0)
    col = jnp.broadcast_to(seg[:, None], (total_rows, 128))
    early = (au, bd, bn, bu, an, first_bias, second_gain, second_bias, tail, pack, col)
    x_one, x_two, held, early, wu_halves, wn_halves, cot_halves = lax.optimization_barrier(
        (x_one, x_two, held, early, wu_halves, wn_halves, cot_halves)
    )
    au, bd, bn, bu, an, first_bias, second_gain, second_bias, tail, pack, col = early

    x_three = swap(x_two, "mp", 1)
    pack_two = swap(pack, "mp", 2)
    wu_first = swap(wu_halves[0], "mp", 2)
    held = step_in(1, x_one, held)
    held = step_in(2, x_two, held)
    x_three, pack_two, wu_first, *held = lax.optimization_barrier((x_three, pack_two, wu_first, *held))

    pack_one = swap(jnp.concatenate([tail, pack_two[:last]], 0), "mp", 1)
    wu_second = swap(after(wu_halves[1], x_three), "mp", 2)
    held = step_in(3, x_three, held)
    merged, normed, z_qkv = held
    other, stat_other = attend(index ^ 2, merged, seg, col, slopes, 2)
    other, pack_one, pack_two, wu_first, wu_second, merged = lax.optimization_barrier(
        (other, pack_one, pack_two, wu_first, wu_second, merged)
    )

    m_two = swap(other, "mp", 2)
    cot_first = swap(after(cot_halves[0], other), "mp", 1)
    bu_far, an_far = pack_two[last:last + rank], pack_two[last + rank:]
    packs = (pack_one[:last], pack_two, pack_one[last:])
    slices = jnp.concatenate([wu_first, wu_second, *(p[:size] for p in packs)], 0)
    shared = lax.all_gather(slices, "dp", axis=0).reshape(copies, 7, size, width)
    ad = jnp.concatenate([ad] + [p[size:last].reshape(rank, local_width) for p in packs], 1)
    mine, stat_mine = attend(index, merged, seg, col, slopes, 2)
    m_two, mine, cot_first = lax.optimization_barrier((m_two, mine, cot_first))

    m_one = swap(mine, "mp", 1)
    m_three = swap(m_two, "mp", 1)
    wn_first = swap(after(wn_halves[0], m_two), "mp", 2)
    m_one, m_three, wn_first = lax.optimization_barrier((m_one, m_three, wn_first))

    m_parts = [mine, m_one, m_two, m_three]
    wn_second = swap(after(wn_halves[1], m_one), "mp", 2)
    wn_second, shared = lax.optimization_barrier((wn_second, shared))
    cot_second = swap(after(cot_halves[1], wn_second), "mp", 1)
    wn_far = lax.all_gather(jnp.concatenate([wn_first, wn_second], 0), "dp", axis=0, tiled=True)

    middle, second, z_dense, z_up = dense(
        layer_in, x_one, m_parts, ad, bd, second_gain, second_bias, au, w_dense, shared
    )
    second, cot_second = lax.optimization_barrier((second, cot_second))

    cot_parts = (cot_first, cot_second)
    act, dh, dzu, so_far, dz_down = feed(
        0, 2 * own_rows, second, (cotangent, *cot_parts), w_up.reshape(copies, 4, size, width), w_down, z_up, bn, bu, an,
        au, None, F32
    )
    gn_own, gu_own, zn, out_so_far = emit(0, act, dh, w_down, an, bn, z_up, dz_down, None, F32)
    out_so_far, so_far = lax.optimization_barrier((out_so_far, so_far))
    far_args = (shared, wn_far, z_up, dz_down, bu_far, an_far, au, so_far)
    act_a, dh_a, dzu_a, d_send = feed(1, own_rows, second, cot_parts, *far_args, BF16)
    second, d_send = lax.optimization_barrier((second, d_send))

    d_near = swap(d_send, "mp", 1)
    act_b, dh_b, dzu_b, d_own = feed(0, own_rows, second, (cotangent,), *far_args, BF16)
    act_a, d_own = lax.optimization_barrier((act_a, d_own))
    gn_a, gu_a, zn_a, out_send = emit(1, act_a, dh_a, wn_far, an_far, bn, z_up, dz_down, out_so_far, BF16)
    d_near, d_own, out_send = lax.optimization_barrier((d_near, d_own, out_send))

    d_low, dz_dense, *d_mixed = dense_back(
        d_own, d_near, middle, cotangent, second_gain, bd, ad, w_dense, shared
    )
    d_low, dz_dense, act_b, *d_mixed = lax.optimization_barrier((d_low, dz_dense, act_b, *d_mixed))
    g_blocks = [d_mixed[0]] + [swap(d_mixed[r], "mp", r) for r in (1, 2, 3)]
    gn_b, gu_b, zn_b, out_own = emit(0, act_b, dh_b, wn_far, an_far, bn, z_up, dz_down, out_so_far, F32)

    def join(value, own, far):
        return (value.astype(F32) + jnp.concatenate([own, far], 0).astype(F32)).astype(BF16)

    dzu, zn_a = lax.optimization_barrier((dzu, zn_a, d_low))[:2]
    ga_up = dot_tn(join(dzu, dzu_b, dzu_a), second)
    zn = join(zn, zn_b, zn_a)
    gb_down = dot_tn(zn[:own_rows], cotangent) + dot_tn(zn[own_rows:], jnp.concatenate(cot_parts, 0))
    gb_dense = dot_tn(z_dense[:own_rows], d_low)
    gd = [dot_tn(dz_dense, m[(r % 2) * own_rows:(r % 2 + 1) * own_rows]) for r, m in enumerate(m_parts)]
    gu_far, gn_far = ((a.astype(F32) + b.astype(F32)).astype(BF16) for a, b in ((gu_a, gu_b), (gn_a, gn_b)))
    sums = jnp.concatenate([ga_up, gb_down, gb_dense], 1)
    near = swap(jnp.concatenate([sums, gd[1], gd[3]], 1).astype(BF16), "mp", 1)
    *g_blocks, near = lax.optimization_barrier((*g_blocks, near))

    near = near.astype(F32)
    sums = sums + near[:, :3 * width]
    gd_own = gd[0] + near[:, 3 * width:3 * width + local_width]
    gd_far = gd[2] + near[:, 3 * width + local_width:]
    mate = swap(jnp.concatenate([sums.astype(BF16), gu_far, gn_far, gd_far.astype(BF16)], 1), "mp", 2)
    out_near = swap(after(out_send, near), "mp", 1)
    d_merged, send = attend_back(
        index, merged, (mine, other), g_blocks, (stat_mine, stat_other), seg, col, slopes, aq, bq, wq
    )
    send, d_merged, mate, out_near = lax.optimization_barrier((send, d_merged, mate, out_near))

    relay = swap(send, "mp", 1)
    first_pack = jnp.concatenate([sums, gu_own, gn_own, gd_own], 1) + mate.astype(F32)
    first_pack = jnp.concatenate([first_pack.astype(BF16), jnp.full((rank, 128), which, BF16)], 1)
    first_pack = lax.all_gather(first_pack, "dp", axis=0)
    ga_qkv, gb_qkv = inner_grads(d_merged, z_qkv, normed, bq)
    ga_low, d_merged = lax.optimization_barrier((ga_qkv.astype(BF16), d_merged))
    ga_others = [swap(ga_low, "mp", r) for r in (1, 2, 3)]
    send_two, send_one = project_back(index, d_merged, wq, aq, bq, (2, 1))
    relay, send_one, send_two, *ga_others = lax.optimization_barrier((relay, send_one, send_two, *ga_others))

    d_two = swap((send_two.astype(F32) + relay.astype(F32)).astype(BF16), "mp", 2)
    d_one = swap(send_one, "mp", 1)
    layer_out = (middle[:own_rows].astype(F32) + out_own + out_near.astype(F32)).astype(BF16)
    ga_qkv = ga_qkv + sum(g.astype(F32) for g in ga_others)
    second_pack = jnp.concatenate([ga_qkv, gb_qkv], 1).astype(BF16)
    second_pack = lax.all_gather(second_pack, "dp", axis=0)
    ids = first_pack[:, 0, -1].astype(jnp.int32)
    (kept,) = project_back(after(index, ids), d_merged, wq, aq, bq, (0,))
    ga_up, gb_down, gb_dense, gb_up, ga_down, ga_dense, ga_qkv, gb_qkv = spread(
        ids, first_pack, second_pack, kinds, width, local_width, local_ff
    )
    d_one, d_two = lax.optimization_barrier((d_one, d_two, gb_qkv))[:2]
    input_grad = last_norm(kept, d_one, d_two, layer_in, d_low, first_gain)
    return (
        layer_out,
        input_grad,
        ga_qkv.transpose(2, 0, 1),
        gb_qkv.transpose(0, 2, 1, 3),
        ga_dense.transpose(2, 0, 1),
        gb_dense,
        ga_up.transpose(2, 0, 1),
        gb_up,
        ga_down.transpose(2, 0, 1),
        gb_down,
    )


def solution(mesh):
    return jax.shard_map(
        local,
        mesh=mesh,
        in_specs=(
            P(("dp", "mp"), None), P(), P(), P(None, None, "mp"), P(), P(None, None, None, "mp"), P("mp", None),
            P("mp", None, None), P(), P(), P(), P(None, "mp"), P(), P(None, None, "mp"), P("mp", None),
            P("mp", None, None), P(), P("dp", None), P("dp"), P(("dp", "mp"), None),
        ),
        out_specs=(
            P(("dp", "mp"), None), P(("dp", "mp"), None), P(), P(None, None, None, "mp"), P("mp", None, None), P(),
            P(), P(None, None, "mp"), P("mp", None, None), P(),
        ),
        check_vma=False,
    )
```

```python
import functools

import jax
import jax.numpy as jnp
from jax import lax
from jax.experimental import pallas as pl
from jax.experimental.pallas import tpu as pltpu
from jax.sharding import PartitionSpec as P

HEADS = 32
HD = 64
LONGEST = 512
EPSILON = 1e-05
F32 = jnp.float32
BF16 = jnp.bfloat16
MASKED = -1e30
WHOLE = pl.BlockSpec(memory_space=pltpu.VMEM)
REMOTE = pl.BlockSpec(memory_space=pl.ANY)


def shape(dims, kind=BF16):
    return jax.ShapeDtypeStruct(dims, kind)


def statistics(values):
    center = jnp.mean(values, -1, keepdims=True)
    centred = values - center
    variance = jnp.mean(centred * centred, -1, keepdims=True)
    scaler = lax.rsqrt(variance + EPSILON)
    return centred * scaler, scaler


def layer_norm(values, gain, bias):
    return statistics(values)[0] * gain.astype(F32) + bias.astype(F32)


def norm_back(grad, values, gain):
    normal, scaler = statistics(values)
    scaled = grad * gain.astype(F32)
    first_mean = jnp.mean(scaled, -1, keepdims=True)
    second_mean = jnp.mean(scaled * normal, -1, keepdims=True)
    return (scaled - first_mean - normal * second_mean) * scaler


def by_rows(count, body, chunk=32):
    for i in range(count // chunk):
        body(slice(i * chunk, (i + 1) * chunk))


def dot_nn(left, right):
    return jnp.dot(left, right, preferred_element_type=F32)


def dot_nt(left, right):
    return lax.dot_general(left, right, (((1,), (1,)), ((), ())), preferred_element_type=F32)


def dot_tn(left, right):
    return lax.dot_general(left, right, (((0,), (0,)), ((), ())), preferred_element_type=F32)


def swap(value, axis, bit):
    pairs = [(i, i ^ bit) for i in range(lax.axis_size(axis))]
    return lax.ppermute(value, axis, pairs)


def after(value, *others):
    return lax.optimization_barrier((value, *others))[0]


def gelu_pair(values):
    below = 0.5 * (1.0 + lax.erf(values * 0.5 ** 0.5))
    density = jnp.exp(values * values * -0.5) * 0.3989422804014327
    return values * below, below + values * density


def project_kernel(kept, at_ref, x_ref, gain_ref, bias_ref, aq_ref, bq_ref, wq_ref, *refs):
    merged_ref, normed_ref, z_ref, w_ref, out_ref, low_ref, thin_ref, sems, loads = refs[kept:]
    count = x_ref.shape[0]
    rows = pl.ds(pl.multiple_of(at_ref[0] * count, count), count)
    parts = wq_ref.shape[0]

    def load(i):
        return pltpu.make_async_copy(wq_ref.at[i], w_ref.at[i], loads.at[i])

    def save(i):
        return pltpu.make_async_copy(out_ref.at[i], merged_ref.at[i, rows, :], sems.at[2 + i])

    for i in range(parts):
        load(i).start()

    chunk = min(64, count)

    def norm(i, carry):
        part = pl.ds(pl.multiple_of(i * chunk, chunk), chunk)
        low_ref[part, :] = layer_norm(x_ref[part, :].astype(F32), gain_ref[...], bias_ref[...]).astype(BF16)
        return carry

    lax.fori_loop(0, count // chunk, norm, 0, unroll=2)
    copies = [pltpu.make_async_copy(low_ref, normed_ref.at[rows, :], sems.at[0])]
    copies[0].start()
    thin_ref[...] = dot_nt(low_ref[...], aq_ref[...]).astype(BF16)
    copies.append(pltpu.make_async_copy(thin_ref, z_ref.at[rows, :], sems.at[1]))
    copies[1].start()

    width = out_ref.shape[2]
    tile = min(256, width)
    tiles = width // tile

    def one(step, carry):
        i, t = step // tiles, step % tiles
        cols = pl.ds(pl.multiple_of(t * tile, tile), tile)

        @pl.when(t == 0)
        def _():
            load(i).wait()

        value = dot_nn(low_ref[...], w_ref[i, :, cols]) + dot_nn(thin_ref[...], bq_ref[i, :, cols])
        out_ref[i, :, cols] = value.astype(BF16)

        @pl.when(t == tiles - 1)
        def _():
            save(i).start()

        return carry

    lax.fori_loop(0, parts * tiles, one, 0)
    for copy in copies + [save(i) for i in range(parts)]:
        copy.wait()


def project(at, rows, gain, bias, aq, bq, wq, total, earlier):
    count, width = rows.shape
    parts, _, local_width = wq.shape
    rank = aq.shape[0]
    kept = len(earlier)
    return pl.pallas_call(
        functools.partial(project_kernel, kept),
        out_shape=(shape((parts, total, local_width)), shape((total, width)), shape((total, rank))),
        grid_spec=pltpu.PrefetchScalarGridSpec(
            num_scalar_prefetch=1,
            grid=(),
            in_specs=[WHOLE] * 5 + [REMOTE] * (1 + kept),
            out_specs=(REMOTE,) * 3,
            scratch_shapes=[
                pltpu.VMEM(wq.shape, BF16),
                pltpu.VMEM((parts, count, local_width), BF16),
                pltpu.VMEM((count, width), BF16),
                pltpu.VMEM((count, rank), BF16),
                pltpu.SemaphoreType.DMA((2 + parts,)),
                pltpu.SemaphoreType.DMA((parts,)),
            ],
        ),
        input_output_aliases={7 + i: i for i in range(kept)},
        name="project",
    )(at.reshape(1), rows, gain, bias, aq, bq, wq, *earlier)


def lane_mask(half):
    return (lax.broadcasted_iota(jnp.int32, (1, 2 * HD), 1) // HD) == half


def allowed_pairs(seg_col, seg_row, causal):
    dims = (seg_col.shape[0], seg_row.shape[1])
    allowed = seg_col == seg_row
    if causal:
        allowed = allowed & (lax.broadcasted_iota(jnp.int32, dims, 0) <= lax.broadcasted_iota(jnp.int32, dims, 1))
    return allowed


def reach_of(block):
    return -(-LONGEST // block)


def attend_kernel(block, count, first_ref, seg_ref, slope_ref, col_ref, row_ref, q_ref, k_ref, v_ref,
                  o_ref, stat_ref, turned_ref, top_ref, total_ref, sum_ref):
    pair = pl.program_id(0)
    turned_ref[...] = v_ref[0].T

    for own in range(count):
        i = first_ref[0] ^ own
        start = pl.multiple_of(i * block, block)
        here = pl.ds(own * block, block)
        query = q_ref[0, pl.ds(start, block), :] * HD ** -0.5
        scaled = [jnp.where(lane_mask(half), query, 0).astype(BF16) for half in range(2)]

        def one(back):
            at = pl.multiple_of(start - back * block, block)
            keys = pl.ds(at, block)
            allowed = allowed_pairs(col_ref[keys, :1], row_ref[:, pl.ds(start, block)], back == 0)
            place = lax.broadcasted_iota(jnp.int32, (block, block), 0).astype(F32)
            for half in range(2):
                slope = slope_ref[2 * pair + half]
                shift = slope * at.astype(F32)
                scores = jnp.where(allowed, dot_nt(k_ref[0, keys, :], scaled[half]) + slope * place, MASKED)
                best = jnp.max(scores, 0, keepdims=True) + shift
                if back:
                    before = top_ref[half]
                    best = jnp.maximum(best, before)
                weights = jnp.exp(scores - (best - shift))
                total = jnp.sum(weights, 0, keepdims=True)
                result = dot_nn(turned_ref[half * HD:(half + 1) * HD, keys], weights.astype(BF16))
                if back:
                    fade = jnp.exp(before - best)
                    total = total + fade * total_ref[half]
                    result = result + fade * sum_ref[half]
                top_ref[half] = best
                total_ref[half] = total
                sum_ref[half] = result

        one(0)
        for back in range(1, reach_of(block) + 1):
            last = jnp.maximum(start - (back - 1) * block - 1, 0)

            @pl.when((i >= back) & (seg_ref[last] == seg_ref[start]))
            def _(back=back):
                one(back)

        for half in range(2):
            stat_ref[half, :, here] = top_ref[half] + jnp.log(total_ref[half])
        done = jnp.concatenate([sum_ref[half] / total_ref[half] for half in range(2)], 0)
        o_ref[here, :] = done.T.astype(BF16)


def attend(first, merged, seg, col, slopes, count):
    _, rows, width = merged.shape
    block = min(256, rows)
    heads = width // HD

    def part(i):
        return pl.BlockSpec((1, rows, 2 * HD), lambda h, *_: (i, 0, h))

    return pl.pallas_call(
        functools.partial(attend_kernel, block, count),
        out_shape=(shape((count * block, width)), shape((heads, 1, count * block), F32)),
        grid_spec=pltpu.PrefetchScalarGridSpec(
            num_scalar_prefetch=3,
            grid=(heads // 2,),
            in_specs=[
                pl.BlockSpec((rows, 128), lambda h, *_: (0, 0)),
                pl.BlockSpec((1, rows), lambda h, *_: (0, 0)),
                part(0), part(1), part(2),
            ],
            out_specs=(
                pl.BlockSpec((count * block, 2 * HD), lambda h, *_: (0, h)),
                pl.BlockSpec((2, 1, count * block), lambda h, *_: (h, 0, 0)),
            ),
            scratch_shapes=[
                pltpu.VMEM((2 * HD, rows), BF16),
                pltpu.VMEM((2, 1, block), F32),
                pltpu.VMEM((2, 1, block), F32),
                pltpu.VMEM((2, HD, block), F32),
            ],
        ),
        name="attend",
    )(first.reshape(1), seg, slopes, col, seg[None, :], merged, merged, merged)


def attend_back_kernel(block, at_ref, seg_ref, slope_ref, col_ref, row_ref, *refs):
    stats, mixed, grads_in = refs[:2], refs[2:4], refs[4:8]
    q_ref, k_ref, v_ref, aq_ref, bq_ref, wq_ref, d_ref, send_ref = refs[8:16]
    stat_ref, m_ref, g_ref, turned_ref, center_ref, qsum_ref, ksum_ref, vsum_ref, w_ref, held_ref, loads = refs[16:]
    pair = pl.program_id(0)

    def load(i):
        return pltpu.make_async_copy(wq_ref.at[i], w_ref.at[i], loads.at[i])

    @pl.when(pair == 0)
    def _():
        for i in range(3):
            load(i).start()

    count = g_ref.shape[0] // block
    size = grads_in[0].shape[0]
    for r, ref in enumerate(grads_in):
        rows = pl.ds(pl.multiple_of((at_ref[0] ^ r) * size, size), size)
        part = slice((r % 2) * size, (r % 2 + 1) * size)
        g_ref[rows, :] = ref[...]
        m_ref[rows, :] = mixed[r // 2][part, :]
        stat_ref[:, :, rows] = stats[r // 2][:, :, part]
    turned_ref[...] = k_ref[0].T
    product = (g_ref[...].astype(F32) * m_ref[...].astype(F32)).T
    for half in range(2):
        center_ref[half:half + 1] = jnp.sum(product[half * HD:(half + 1) * HD], 0, keepdims=True)
    qsum_ref[...] = jnp.zeros_like(qsum_ref)
    ksum_ref[...] = jnp.zeros_like(ksum_ref)
    vsum_ref[...] = jnp.zeros_like(vsum_ref)

    for i in range(count):
        queries = pl.ds(i * block, block)
        query = q_ref[0, queries, :] * HD ** -0.5
        scaled = [jnp.where(lane_mask(half), query, 0).astype(BF16) for half in range(2)]
        grads = [jnp.where(lane_mask(half), g_ref[queries, :], 0).astype(BF16) for half in range(2)]

        def one(j):
            keys = pl.ds(j * block, block)
            allowed = allowed_pairs(col_ref[keys, :1], row_ref[:, queries], i == j)
            place = lax.broadcasted_iota(jnp.int32, (block, block), 0).astype(F32)
            val_part, key_part = 0.0, 0.0
            for half in range(2):
                slope = slope_ref[2 * pair + half]
                shift = slope * float(j * block)
                scores = jnp.where(allowed, dot_nt(k_ref[0, keys, :], scaled[half]) + slope * place, MASKED)
                probs = jnp.exp(scores - (stat_ref[half, :, queries] - shift))
                d_probs = dot_nt(v_ref[0, keys, :], grads[half])
                d_scores = (probs * (d_probs - center_ref[half:half + 1, queries])).astype(BF16)
                val_part = val_part + dot_nn(probs.astype(BF16), grads[half])
                key_part = key_part + dot_nn(d_scores, scaled[half])
                rows = slice(half * HD, (half + 1) * HD)
                qsum_ref[rows, queries] += dot_nn(turned_ref[rows, keys], d_scores)
            vsum_ref[keys, :] += val_part
            ksum_ref[keys, :] += key_part

        one(i)
        for back in range(1, min(i, reach_of(block)) + 1):
            j = i - back

            @pl.when(seg_ref[j * block + block - 1] == seg_ref[i * block])
            def _(j=j):
                one(j)

    d_ref[0] = (qsum_ref[...] * HD ** -0.5).T.astype(BF16)
    d_ref[1] = ksum_ref[...].astype(BF16)
    d_ref[2] = vsum_ref[...].astype(BF16)
    sent = pl.ds(pl.multiple_of((at_ref[0] ^ 3) * size, size), size)
    cols = pl.ds(pl.multiple_of(pair * 2 * HD, 2 * HD), 2 * HD)
    for i in range(3):
        held_ref[i, :, cols] = d_ref[i, sent, :]

    @pl.when(pair == pl.num_programs(0) - 1)
    def _():
        for i in range(3):
            load(i).wait()
        inner = sum(dot_nt(held_ref[i], bq_ref[i]) for i in range(3)).astype(BF16)
        tile = 512

        def one(t, carry):
            here = pl.ds(pl.multiple_of(t * tile, tile), tile)
            total = dot_nn(inner, aq_ref[:, here])
            for i in range(3):
                total = total + dot_nt(held_ref[i], w_ref[i, here, :])
            send_ref[:, here] = total.astype(BF16)
            return carry

        lax.fori_loop(0, send_ref.shape[1] // tile, one, 0)


def attend_back(at, merged, mixed, grads, stats, seg, col, slopes, aq, bq, wq):
    parts, rows, width = merged.shape
    block = min(256, rows)
    half = rows // 2

    def wide(count):
        return pl.BlockSpec((count, 2 * HD), lambda h, *_: (0, h))

    def part(i):
        return pl.BlockSpec((1, rows, 2 * HD), lambda h, *_: (i, 0, h))

    return pl.pallas_call(
        functools.partial(attend_back_kernel, block),
        out_shape=(shape(merged.shape), shape((rows // 4, aq.shape[1]))),
        grid_spec=pltpu.PrefetchScalarGridSpec(
            num_scalar_prefetch=3,
            grid=(width // (2 * HD),),
            in_specs=[
                pl.BlockSpec((rows, 128), lambda h, *_: (0, 0)),
                pl.BlockSpec((1, rows), lambda h, *_: (0, 0)),
            ] + [pl.BlockSpec((2, 1, half), lambda h, *_: (h, 0, 0))] * 2 + [wide(half)] * 2 + [wide(rows // 4)] * 4 + [
                part(0), part(1), part(2),
                pl.BlockSpec(aq.shape, lambda h, *_: (0, 0)), pl.BlockSpec(bq.shape, lambda h, *_: (0, 0, 0)), REMOTE,
            ],
            out_specs=(
                pl.BlockSpec((parts, rows, 2 * HD), lambda h, *_: (0, 0, h)),
                pl.BlockSpec((rows // 4, aq.shape[1]), lambda h, *_: (0, 0)),
            ),
            scratch_shapes=[
                pltpu.VMEM((2, 1, rows), F32),
                pltpu.VMEM((rows, 2 * HD), BF16),
                pltpu.VMEM((rows, 2 * HD), BF16),
                pltpu.VMEM((2 * HD, rows), BF16),
                pltpu.VMEM((2, rows), F32),
                pltpu.VMEM((2 * HD, rows), F32),
                pltpu.VMEM((rows, 2 * HD), F32),
                pltpu.VMEM((rows, 2 * HD), F32),
                pltpu.VMEM(wq.shape, BF16),
                pltpu.VMEM((parts, rows // 4, width), BF16),
                pltpu.SemaphoreType.DMA((parts,)),
            ],
        ),
        name="attend_back",
    )(at.reshape(1), seg, slopes, col, seg[None, :], *stats, *mixed, *grads, merged, merged, merged, aq, bq, wq)


def dense_kernel(x0_ref, x1_ref, m0_ref, m1_ref, m2_ref, m3_ref, a_ref, bd_ref, gain_ref, bias_ref, au_ref,
                 own_ref, far_ref, middle_ref, second_ref, zd_ref, zu_ref, w_ref, m_ref, sum_ref, loads):
    size = m0_ref.shape[1]
    count = x0_ref.shape[0]
    tiles, pieces, _, thick, tile = w_ref.shape

    def columns(t):
        return pl.ds(pl.multiple_of(t * tile, tile), tile)

    def load(t):
        cols = columns(t)
        own = own_ref.reshape(pieces, thick, own_ref.shape[1]).at[:, :, cols]
        far = far_ref.at[:, pl.ds(4, 3), :, cols]
        return (
            pltpu.make_async_copy(own, w_ref.at[t, :, 0], loads.at[0, t]),
            pltpu.make_async_copy(far, w_ref.at[t, :, pl.ds(1, 3)], loads.at[1, t]),
        )

    def start(t, carry):
        for copy in load(t):
            copy.start()
        return carry

    lax.fori_loop(0, tiles, start, 0)
    for r, m in enumerate((m0_ref, m1_ref, m2_ref, m3_ref)):
        cols = slice(r * size, (r + 1) * size)
        m_ref[:count, cols] = m[(r % 2) * count:(r % 2 + 1) * count, :]
        m_ref[count:, cols] = m[(1 - r % 2) * count:(2 - r % 2) * count, :]
    zd_ref[...] = dot_nt(m_ref[...], a_ref[...]).astype(BF16)

    def one(t, carry):
        cols = columns(t)
        for copy in load(t):
            copy.wait()
        total = dot_nn(zd_ref[...], bd_ref[:, cols])
        for r in range(4):
            weights = w_ref[t, :, r].reshape(pieces * thick, tile)
            total = total + dot_nn(m_ref[:, r * size:(r + 1) * size], weights)
        sum_ref[:count, cols] = total[:count] + x0_ref[:, cols].astype(F32)
        sum_ref[count:, cols] = total[count:] + x1_ref[:, cols].astype(F32)
        return carry

    lax.fori_loop(0, tiles, one, 0)
    chunk = min(64, count)

    def norm(i, carry):
        part = pl.ds(pl.multiple_of(i * chunk, chunk), chunk)
        values = sum_ref[part, :]
        middle_ref[part, :] = values.astype(BF16)
        second_ref[part, :] = layer_norm(values, gain_ref[...], bias_ref[...]).astype(BF16)
        return carry

    lax.fori_loop(0, 2 * count // chunk, norm, 0, unroll=2)
    zu_ref[...] = dot_nt(second_ref[...], au_ref[...]).astype(BF16)


def dense(x_own, x_far, m_parts, ad, bd, gain, bias, au, w_own, w_far):
    count, width = x_own.shape
    rank = ad.shape[0]
    tile = min(256, width)
    pieces, _, thick, _ = w_far.shape
    return pl.pallas_call(
        dense_kernel,
        out_shape=(
            shape((2 * count, width)), shape((2 * count, width)), shape((2 * count, rank)),
            shape((2 * count, rank)),
        ),
        in_specs=[WHOLE] * 11 + [REMOTE] * 2,
        out_specs=(WHOLE,) * 4,
        scratch_shapes=[
            pltpu.VMEM((width // tile, pieces, 4, thick, tile), BF16), pltpu.VMEM((2 * count, width), BF16),
            pltpu.VMEM((2 * count, width), F32), pltpu.SemaphoreType.DMA((2, width // tile)),
        ],
        name="dense",
    )(x_own, x_far, *m_parts, ad, bd, gain, bias, au, w_own, w_far)


def feed_kernel(grads, earlier, known, at_ref, x_ref, up_ref, down_ref, zu_ref, bu_ref, an_ref, au_ref, *refs):
    step = pl.program_id(0)
    g_refs, other_ref, refs = refs[:grads], refs[grads], refs[grads + 1:]
    if known:
        slope_ref, refs = refs[0], refs[1:]
    if earlier:
        active_ref, refs = (None, refs) if known else (refs[1], refs[:1] + refs[2:])
        before_ref, hidden_ref, dz_out_ref, out_ref, g_ref, total_ref, inner_ref, held_ref, sem = refs
        dz_ref = other_ref
        count = held_ref.shape[0]
        copy = pltpu.make_async_copy(before_ref.at[pl.ds(at_ref[0] * count, count), :], held_ref, sem)
    else:
        active_ref, hidden_ref, dz_out_ref, out_ref, dz_ref, g_ref, total_ref, inner_ref = refs

    @pl.when(step == 0)
    def _():
        if earlier:
            copy.start()
        start = 0
        for ref in g_refs:
            g_ref[start:start + ref.shape[0], :] = ref[...]
            start += ref.shape[0]
        total_ref[...] = jnp.zeros_like(total_ref)
        inner_ref[...] = jnp.zeros_like(inner_ref)
        if not earlier:
            dz_ref[...] = dot_nt(g_ref[...], other_ref[...]).astype(BF16)

    up = up_ref[...].reshape(x_ref.shape[1], hidden_ref.shape[1])
    d_active = dot_nt(g_ref[...], down_ref[...]) + dot_nn(dz_ref[...], an_ref[...])
    if known:
        slope = slope_ref[...].astype(F32)
    else:
        hidden = dot_nn(x_ref[...], up) + dot_nn(zu_ref[...], bu_ref[...])
        active, slope = gelu_pair(hidden)
        active_ref[...] = active.astype(BF16)
    d_hidden = (d_active * slope).astype(BF16)
    hidden_ref[...] = d_hidden
    total_ref[...] += dot_nt(d_hidden, up)
    inner_ref[...] += dot_nt(d_hidden, bu_ref[...])

    @pl.when(step == pl.num_programs(0) - 1)
    def _():
        inner = inner_ref[...].astype(BF16)
        dz_out_ref[...] = inner
        total = total_ref[...] + dot_nn(inner, au_ref[...])
        if earlier:
            copy.wait()
            total = total + held_ref[...]
        out_ref[...] = total.astype(out_ref.dtype)


def hidden_kernel(at_ref, x_ref, up_ref, zu_ref, bu_ref, active_ref, slope_ref):
    up = up_ref[...].reshape(x_ref.shape[1], active_ref.shape[1])
    active, slope = gelu_pair(dot_nn(x_ref[...], up) + dot_nn(zu_ref[...], bu_ref[...]))
    active_ref[...] = active.astype(BF16)
    slope_ref[...] = slope.astype(BF16)


def hidden_units(at, count, x, up, zu, bu):
    width = x.shape[1]
    ff = up.shape[3]
    tile = min(512, ff)
    rank = bu.shape[0]
    cols = pl.BlockSpec((count, tile), lambda t, at: (0, t))
    return pl.pallas_call(
        hidden_kernel,
        out_shape=(shape((count, ff)),) * 2,
        grid_spec=pltpu.PrefetchScalarGridSpec(
            num_scalar_prefetch=1,
            grid=(ff // tile,),
            in_specs=[
                pl.BlockSpec((count, width), lambda t, at: (at[0], 0), pipeline_mode=pl.Buffered(1)),
                pl.BlockSpec((up.shape[0], 4, up.shape[2], tile), lambda t, at: (0, 0, 0, t)),
                pl.BlockSpec((count, rank), lambda t, at: (at[0], 0)), pl.BlockSpec((rank, tile), lambda t, at: (0, t)),
            ],
            out_specs=(cols, cols),
        ),
        name="hidden_units",
    )(jnp.full((1,), at, jnp.int32), x, up, zu, bu)


def feed(at, count, x, g, up, down, zu, other, bu, an, au, before, kind, slope=None):
    width = x.shape[1]
    ff = up.shape[3]
    tile = min(512, ff)
    rank = bu.shape[0]
    earlier = before is not None
    once = pl.Buffered(1)
    rows = pl.BlockSpec((count, width), lambda t, at: (at[0], 0), pipeline_mode=once)
    thin = pl.BlockSpec((count, rank), lambda t, at: (at[0], 0))
    cols = pl.BlockSpec((count, tile), lambda t, at: (0, t))
    row = pl.BlockSpec((rank, tile), lambda t, at: (0, t))
    flat = pl.BlockSpec((rank, width), lambda t, at: (0, 0))
    out_shape = [shape((count, ff)), shape((count, ff)), shape((count, rank)), shape((count, width), kind)]
    out_specs = [
        cols, cols, pl.BlockSpec((count, rank), lambda t, at: (0, 0)),
        pl.BlockSpec((count, width), lambda t, at: (0, 0), pipeline_mode=once),
    ]
    scratch = [pltpu.VMEM((count, width), BF16), pltpu.VMEM((count, width), F32), pltpu.VMEM((count, rank), F32)]
    known = slope is not None
    if known:
        out_shape, out_specs = out_shape[1:], out_specs[1:]
    if earlier:
        extra = [thin] + [cols] * known + [REMOTE]
        scratch += [pltpu.VMEM((count, width), F32), pltpu.SemaphoreType.DMA(())]
    else:
        extra = [flat]
        out_shape.append(shape((count, rank)))
        out_specs.append(pl.BlockSpec((count, rank), lambda t, at: (0, 0)))
    return pl.pallas_call(
        functools.partial(feed_kernel, len(g), earlier, known),
        out_shape=tuple(out_shape),
        grid_spec=pltpu.PrefetchScalarGridSpec(
            num_scalar_prefetch=1,
            grid=(ff // tile,),
            in_specs=[
                rows, pl.BlockSpec((up.shape[0], 4, up.shape[2], tile), lambda t, at: (0, 0, 0, t)),
                pl.BlockSpec((tile, width), lambda t, at: (t, 0)), thin, row, row, flat,
            ] + [pl.BlockSpec(b.shape, lambda t, at: (0, 0), pipeline_mode=once) for b in g] + extra,
            out_specs=tuple(out_specs),
            scratch_shapes=scratch,
        ),
        name="feed",
    )(
        jnp.full((1,), at, jnp.int32), x, up, down, zu, bu, an, au, *g, other, *((slope,) if known else ()),
        *((before,) if earlier else ()),
    )


def emit_kernel(earlier, at_ref, active_ref, hidden_ref, down_ref, an_ref, bn_ref, z_in_ref, d_in_ref, *refs):
    if earlier:
        before_ref, gn_ref, gu_ref, z_ref, out_ref = refs
    else:
        gn_ref, gu_ref, z_ref, out_ref = refs

    @pl.when(pl.program_id(0) == 0)
    def _():
        z_ref[...] = dot_nt(active_ref[...], an_ref[...]).astype(BF16)
        gn_ref[...] = dot_tn(d_in_ref[...], active_ref[...]).astype(BF16)
        gu_ref[...] = dot_tn(z_in_ref[...], hidden_ref[...]).astype(BF16)

    total = dot_nn(active_ref[...], down_ref[...]) + dot_nn(z_ref[...], bn_ref[...])
    if earlier:
        total = total + before_ref[...]
    out_ref[...] = total.astype(out_ref.dtype)


def emit(at, active, hidden, down, an, bn, zu, dz, before, kind):
    count, ff = active.shape
    width = down.shape[1]
    tile = min(512, width)
    rank = an.shape[0]
    earlier = before is not None
    once = pl.Buffered(1)
    whole = pl.BlockSpec((count, ff), lambda t, at: (0, 0), pipeline_mode=once)
    flat = pl.BlockSpec((rank, ff), lambda t, at: (0, 0))
    thin = pl.BlockSpec((count, rank), lambda t, at: (at[0], 0))
    return pl.pallas_call(
        functools.partial(emit_kernel, earlier),
        out_shape=(shape((rank, ff)), shape((rank, ff)), shape((count, rank)), shape((count, width), kind)),
        grid_spec=pltpu.PrefetchScalarGridSpec(
            num_scalar_prefetch=1,
            grid=(width // tile,),
            in_specs=[
                whole, whole, pl.BlockSpec((ff, tile), lambda t, at: (0, t)), flat,
                pl.BlockSpec((rank, tile), lambda t, at: (0, t)), thin, thin,
            ] + [pl.BlockSpec((count, tile), lambda t, at: (at[0], t))] * earlier,
            out_specs=(
                flat, flat, pl.BlockSpec((count, rank), lambda t, at: (0, 0)),
                pl.BlockSpec((count, tile), lambda t, at: (0, t)),
            ),
        ),
        name="emit",
    )(jnp.full((1,), at, jnp.int32), active, hidden, down, an, bn, zu, dz, *((before,) if earlier else ()))


def dense_back_kernel(own_ref, far_ref, cot_ref, gain_ref, bd_ref, ad_ref, middle_ref, w0_ref, w1_ref,
                      low_out_ref, dz_ref, *refs):
    outs = refs[:4]
    mid_ref, w_ref, loads = refs[4:]
    count, width = own_ref.shape
    size = outs[0].shape[1]
    pieces, _, thick, _ = w1_ref.shape
    first = pltpu.make_async_copy(middle_ref.at[pl.ds(0, count), :], mid_ref, loads.at[4])
    first.start()
    pltpu.make_async_copy(w0_ref.reshape(pieces, thick, width), w_ref.at[0], loads.at[0]).start()

    def start(r, carry):
        pltpu.make_async_copy(w1_ref.at[:, r + 3], w_ref.at[r], loads.at[r]).start()
        return carry

    lax.fori_loop(1, 4, start, 0)
    first.wait()
    chunk = min(64, count)

    def norm(i, carry):
        part = pl.ds(pl.multiple_of(i * chunk, chunk), chunk)
        grad = own_ref[part, :].astype(F32) + far_ref[part, :].astype(F32)
        change = norm_back(grad, mid_ref[part, :].astype(F32), gain_ref[...])
        low_out_ref[part, :] = (cot_ref[part, :].astype(F32) + change).astype(BF16)
        return carry

    lax.fori_loop(0, count // chunk, norm, 0, unroll=2)
    dz_ref[...] = dot_nt(low_out_ref[...], bd_ref[...]).astype(BF16)

    def one(r, carry):
        pltpu.make_async_copy(w1_ref.at[:, 0], w_ref.at[r], loads.at[r]).wait()
        weights = w_ref[r].reshape(size, width)
        cols = pl.ds(pl.multiple_of(r * size, size), size)
        value = (dot_nt(low_out_ref[...], weights) + dot_nn(dz_ref[...], ad_ref[:, cols])).astype(BF16)
        for n, out in enumerate(outs):

            @pl.when(r == n)
            def _(out=out):
                out[...] = value

        return carry

    lax.fori_loop(0, 4, one, 0)


def dense_back(own, far, middle, cot, gain, bd, ad, w_own, w_far):
    count, width = own.shape
    rank = bd.shape[0]
    return pl.pallas_call(
        dense_back_kernel,
        out_shape=(shape((count, width)), shape((count, rank))) + (shape((count, width // 4)),) * 4,
        in_specs=[WHOLE] * 6 + [REMOTE] * 3,
        out_specs=(WHOLE,) * 6,
        scratch_shapes=[
            pltpu.VMEM((count, width), BF16), pltpu.VMEM((4, w_far.shape[0]) + w_far.shape[2:], BF16),
            pltpu.SemaphoreType.DMA((5,)),
        ],
        name="dense_back",
    )(own, far, cot, gain, bd, ad, middle, w_own, w_far)


def project_back_kernel(order, at_ref, aq_ref, bq_ref, d_ref, wq_ref, *refs):
    outs = refs[:len(order)]
    part_ref, w_ref, inner_ref, sems, loads = refs[len(order):]
    count = outs[0].shape[0]
    tiles, _, tile, _ = w_ref.shape

    def columns(t):
        return pl.ds(pl.multiple_of(t * tile, tile), tile)

    def fetch(place):
        rows = pl.ds(pl.multiple_of((at_ref[0] ^ order[place]) * count, count), count)
        here = pl.ds(place * count, count)
        return pltpu.make_async_copy(d_ref.at[:, rows, :], part_ref.at[:, here, :], sems.at[place])

    def load(t):
        return pltpu.make_async_copy(wq_ref.at[:, columns(t), :], w_ref.at[t], loads.at[t])

    def start(t, carry):
        load(t).start()
        return carry

    blocks = [fetch(place) for place in range(len(order))]
    for copy in blocks:
        copy.start()
    lax.fori_loop(0, tiles, start, 0)
    for copy in blocks:
        copy.wait()
    inner_ref[...] = sum(dot_nt(part_ref[i], bq_ref[i]) for i in range(3)).astype(BF16)

    def one(t, carry):
        load(t).wait()
        cols = columns(t)
        total = dot_nn(inner_ref[...], aq_ref[:, cols])
        for i in range(3):
            total = total + dot_nt(part_ref[i], w_ref[t, i])
        for place, out in enumerate(outs):
            out[:, cols] = total[place * count:(place + 1) * count].astype(BF16)
        return carry

    lax.fori_loop(0, tiles, one, 0)


def project_back(at, d_merged, wq, aq, bq, order):
    parts, total, local_width = d_merged.shape
    width = wq.shape[1]
    count = total // 4
    tile = min(512, width)
    rows = len(order) * count
    return pl.pallas_call(
        functools.partial(project_back_kernel, order),
        out_shape=(shape((count, width)),) * len(order),
        in_specs=[pl.BlockSpec(memory_space=pltpu.SMEM)] + [WHOLE] * 2 + [REMOTE] * 2,
        out_specs=(WHOLE,) * len(order),
        scratch_shapes=[
            pltpu.VMEM((parts, rows, local_width), BF16), pltpu.VMEM((width // tile, parts, tile, local_width), BF16),
            pltpu.VMEM((rows, aq.shape[0]), BF16),
            pltpu.SemaphoreType.DMA((len(order),)), pltpu.SemaphoreType.DMA((width // tile,)),
        ],
        name="project_back",
    )(at.reshape(1), aq, bq, d_merged, wq)


def inner_kernel(d_ref, z_ref, n_ref, bq_ref, ga_ref, gb_ref):
    step = pl.program_id(0)

    @pl.when(step == 0)
    def _():
        ga_ref[...] = jnp.zeros_like(ga_ref)
        gb_ref[...] = jnp.zeros_like(gb_ref)

    inner = sum(dot_nt(d_ref[i], bq_ref[i]) for i in range(3)).astype(BF16)
    ga_ref[...] += dot_tn(inner, n_ref[...])
    width = d_ref.shape[2]
    for i in range(3):
        gb_ref[:, i * width:(i + 1) * width] += dot_tn(z_ref[...], d_ref[i])


def inner_grads(d_merged, z_qkv, normed, bq):
    parts, total, local_width = d_merged.shape
    width = normed.shape[1]
    rank = z_qkv.shape[1]
    count = total // 2
    return pl.pallas_call(
        inner_kernel,
        out_shape=(shape((rank, width), F32), shape((rank, parts * local_width), F32)),
        grid=(2,),
        in_specs=[
            pl.BlockSpec((parts, count, local_width), lambda i: (0, i, 0)),
            pl.BlockSpec((count, rank), lambda i: (i, 0)),
            pl.BlockSpec((count, width), lambda i: (i, 0)),
            pl.BlockSpec(bq.shape, lambda i: (0, 0, 0)),
        ],
        out_specs=(
            pl.BlockSpec((rank, width), lambda i: (0, 0)),
            pl.BlockSpec((rank, parts * local_width), lambda i: (0, 0)),
        ),
        name="inner_grads",
    )(d_merged, z_qkv, normed, bq)


def spread_kernel(ids_ref, first_ref, second_ref, *outs):
    step = pl.program_id(0)

    @pl.when(step == 0)
    def _():
        for out in outs:
            out[...] = jnp.zeros_like(out)

    which = ids_ref[step]
    ga_up, gb_down, gb_dense, gb_up, ga_down, ga_dense, ga_qkv, gb_qkv = outs
    at = 0
    for out in (ga_up, gb_down, gb_dense, gb_up, ga_down, ga_dense):
        size = out.shape[2]
        out[which] += first_ref[0, :, at:at + size].astype(F32)
        at += size
    size = ga_qkv.shape[2]
    ga_qkv[which] += second_ref[0, :, :size].astype(F32)
    local_width = gb_qkv.shape[3]
    for i in range(3):
        gb_qkv[which, i] += second_ref[0, :, size + i * local_width:size + (i + 1) * local_width].astype(F32)


def spread(ids, first, second, kinds, width, local_width, local_ff):
    copies, rank, _ = first.shape
    dims = [(kinds, rank, n) for n in (width, width, width, local_ff, local_ff, local_width, width)]
    dims.append((kinds, 3, rank, local_width))
    return pl.pallas_call(
        spread_kernel,
        out_shape=tuple(shape(d, F32) for d in dims),
        grid_spec=pltpu.PrefetchScalarGridSpec(
            num_scalar_prefetch=1,
            grid=(copies,),
            in_specs=[
                pl.BlockSpec((1,) + first.shape[1:], lambda s, _: (s, 0, 0)),
                pl.BlockSpec((1,) + second.shape[1:], lambda s, _: (s, 0, 0)),
            ],
            out_specs=tuple(
                pl.BlockSpec(d, lambda s, _, n=len(d): (0,) * n, pipeline_mode=pl.Buffered(1)) for d in dims
            ),
        ),
        name="spread",
    )(ids, first, second)


def last_kernel(kept_ref, one_ref, two_ref, x_ref, d_ref, gain_ref, out_ref):
    grad = kept_ref[...].astype(F32) + one_ref[...].astype(F32) + two_ref[...].astype(F32)
    change = norm_back(grad, x_ref[...].astype(F32), gain_ref[...])
    out_ref[...] = (d_ref[...].astype(F32) + change).astype(BF16)


def last_norm(kept, one, two, x, d, gain):
    count, width = x.shape
    chunk = min(128, count)
    rows = pl.BlockSpec((chunk, width), lambda i: (i, 0))
    return pl.pallas_call(
        last_kernel,
        out_shape=shape((count, width)),
        grid=(count // chunk,),
        in_specs=[rows] * 5 + [pl.BlockSpec((1, width), lambda i: (0, 0))],
        out_specs=rows,
        name="last_norm",
    )(kept, one, two, x, d, gain)


def turned(factor, which):
    return lax.dynamic_index_in_dim(factor.transpose(1, 2, 0), which, 0, False)


def local(
    layer_in, first_gain, first_bias, w_qkv, a_qkv, b_qkv, w_dense, a_dense, b_dense, second_gain, second_bias,
    w_up, a_up, b_up, w_down, a_down, b_down, segment_ids, adapter_ids, cotangent,
):
    own_rows, width = layer_in.shape
    kinds = a_qkv.shape[1]
    rank = a_qkv.shape[2]
    local_width = w_dense.shape[0]
    local_ff = w_up.shape[1]
    local_heads = local_width // HD
    index = lax.axis_index("mp")
    spot = lax.axis_index("dp")
    copies = lax.axis_size("dp")
    total_rows = 4 * own_rows
    low, high = index & 1, index >> 1
    which = adapter_ids[0]
    seg = segment_ids[0]
    head_ids = (index * local_heads + lax.iota(jnp.int32, local_heads)).astype(F32)
    slopes = jnp.exp2(-8.0 * (head_ids + 1.0) / HEADS)
    first_gain, first_bias, second_gain, second_bias = (
        v[None, :] for v in (first_gain, first_bias, second_gain, second_bias)
    )

    aq, ad, au, an = (turned(a, which) for a in (a_qkv, a_dense, a_up, a_down))
    bq = lax.dynamic_index_in_dim(b_qkv.transpose(0, 2, 1, 3), which, 0, False)
    bd, bu, bn = (lax.dynamic_index_in_dim(b, which, 0, False) for b in (b_dense, b_up, b_down))
    wq = w_qkv.transpose(1, 0, 2)

    def slice_of(weight):
        size = weight.shape[0] // copies
        return lax.dynamic_slice_in_dim(weight, spot * size, size, 0)

    x_one = swap(layer_in, "mp", 1)
    x_two = swap(layer_in, "mp", 2)
    wd_slice = slice_of(w_dense)
    size = wd_slice.shape[0]
    ad_flat = ad.reshape(-1, width)
    last = size + ad_flat.shape[0]
    tail = jnp.concatenate([wd_slice, ad_flat], 0)

    def step_in(r, block, held):
        return project(index ^ r, block, first_gain, first_bias, aq, bq, wq, total_rows, held)

    held = step_in(0, layer_in, ())
    wu_halves = jnp.split(slice_of(w_up), 2, axis=0)
    wn_halves = slice_of(w_down)
    wn_halves = jnp.split(wn_halves, [3 * wn_halves.shape[0] // 4], axis=0)
    cot_halves = jnp.split(cotangent, 2, axis=0)
    pack = jnp.concatenate([tail, bu, an], 0)
    col = jnp.broadcast_to(seg[:, None], (total_rows, 128))
    early = (au, bd, bn, bu, an, first_bias, second_gain, second_bias, tail, pack, col)
    x_one, x_two, held, early, wu_halves, wn_halves, cot_halves = lax.optimization_barrier(
        (x_one, x_two, held, early, wu_halves, wn_halves, cot_halves)
    )
    au, bd, bn, bu, an, first_bias, second_gain, second_bias, tail, pack, col = early

    x_three = swap(x_two, "mp", 1)
    pack_two = swap(pack, "mp", 2)
    wu_first = swap(wu_halves[0], "mp", 2)
    held = step_in(1, x_one, held)
    held = step_in(2, x_two, held)
    x_three, pack_two, wu_first, *held = lax.optimization_barrier((x_three, pack_two, wu_first, *held))

    pack_one = swap(jnp.concatenate([tail, pack_two[:last]], 0), "mp", 1)
    wu_second = swap(after(wu_halves[1], x_three), "mp", 2)
    held = step_in(3, x_three, held)
    merged, normed, z_qkv = held
    other, stat_other = attend(index ^ 2, merged, seg, col, slopes, 2)
    other, pack_one, pack_two, wu_first, wu_second, merged = lax.optimization_barrier(
        (other, pack_one, pack_two, wu_first, wu_second, merged)
    )

    m_two = swap(other, "mp", 2)
    cot_first = swap(after(cot_halves[0], other), "mp", 1)
    bu_far, an_far = pack_two[last:last + rank], pack_two[last + rank:]
    packs = (pack_one[:last], pack_two, pack_one[last:])
    slices = jnp.concatenate([wu_first, wu_second, *(p[:size] for p in packs)], 0)
    shared = lax.all_gather(slices, "dp", axis=0).reshape(copies, 7, size, width)
    ad = jnp.concatenate([ad] + [p[size:last].reshape(rank, local_width) for p in packs], 1)
    mine, stat_mine = attend(index, merged, seg, col, slopes, 2)
    m_two, mine, cot_first = lax.optimization_barrier((m_two, mine, cot_first))

    m_one = swap(mine, "mp", 1)
    m_three = swap(m_two, "mp", 1)
    wn_first = swap(after(wn_halves[0], m_two), "mp", 2)
    m_one, m_three, wn_first = lax.optimization_barrier((m_one, m_three, wn_first))

    m_parts = [mine, m_one, m_two, m_three]
    wn_second = swap(after(wn_halves[1], m_one), "mp", 2)
    cot_second = swap(after(cot_halves[1], wn_second), "mp", 1)
    wn_far = lax.all_gather(jnp.concatenate([wn_first, wn_second], 0), "dp", axis=0, tiled=True)

    middle, second, z_dense, z_up = dense(
        layer_in, x_one, m_parts, ad, bd, second_gain, second_bias, au, w_dense, shared
    )
    second, cot_second = lax.optimization_barrier((second, cot_second))

    cot_parts = (cot_first, cot_second)
    act, dh, dzu, so_far, dz_down = feed(
        0, 2 * own_rows, second, (cotangent, *cot_parts), w_up.reshape(copies, 4, size, width), w_down, z_up, bn, bu, an,
        au, None, F32
    )
    gn_own, gu_own, zn, out_so_far = emit(0, act, dh, w_down, an, bn, z_up, dz_down, None, F32)
    act_a, slope_a = hidden_units(1, own_rows, second, shared, z_up, bu_far)
    out_so_far, so_far, act_a, slope_a = lax.optimization_barrier((out_so_far, so_far, act_a, slope_a))
    far_args = (shared, wn_far, z_up, dz_down, bu_far, an_far, au, so_far)
    dh_a, dzu_a, d_send = feed(1, own_rows, second, cot_parts, *far_args, BF16, slope_a)
    second, d_send = lax.optimization_barrier((second, d_send))

    d_near = swap(d_send, "mp", 1)
    act_b, dh_b, dzu_b, d_own = feed(0, own_rows, second, (cotangent,), *far_args, BF16)
    act_a, d_own = lax.optimization_barrier((act_a, d_own))
    gn_a, gu_a, zn_a, out_send = emit(1, act_a, dh_a, wn_far, an_far, bn, z_up, dz_down, out_so_far, BF16)
    d_near, d_own, out_send = lax.optimization_barrier((d_near, d_own, out_send))

    d_low, dz_dense, *d_mixed = dense_back(
        d_own, d_near, middle, cotangent, second_gain, bd, ad, w_dense, shared
    )
    d_low, dz_dense, act_b, *d_mixed = lax.optimization_barrier((d_low, dz_dense, act_b, *d_mixed))
    g_blocks = [d_mixed[0]] + [swap(d_mixed[r], "mp", r) for r in (1, 2, 3)]
    gn_b, gu_b, zn_b, out_own = emit(0, act_b, dh_b, wn_far, an_far, bn, z_up, dz_down, out_so_far, F32)

    def join(value, own, far):
        return (value.astype(F32) + jnp.concatenate([own, far], 0).astype(F32)).astype(BF16)

    dzu, zn_a = lax.optimization_barrier((dzu, zn_a, d_low))[:2]
    ga_up = dot_tn(join(dzu, dzu_b, dzu_a), second)
    zn = join(zn, zn_b, zn_a)
    gb_down = dot_tn(zn[:own_rows], cotangent) + dot_tn(zn[own_rows:], jnp.concatenate(cot_parts, 0))
    gb_dense = dot_tn(z_dense[:own_rows], d_low)
    gd = [dot_tn(dz_dense, m[(r % 2) * own_rows:(r % 2 + 1) * own_rows]) for r, m in enumerate(m_parts)]
    gu_far, gn_far = ((a.astype(F32) + b.astype(F32)).astype(BF16) for a, b in ((gu_a, gu_b), (gn_a, gn_b)))
    sums = jnp.concatenate([ga_up, gb_down, gb_dense], 1)
    near = swap(jnp.concatenate([sums, gd[1], gd[3]], 1).astype(BF16), "mp", 1)
    *g_blocks, near = lax.optimization_barrier((*g_blocks, near))

    near = near.astype(F32)
    sums = sums + near[:, :3 * width]
    gd_own = gd[0] + near[:, 3 * width:3 * width + local_width]
    gd_far = gd[2] + near[:, 3 * width + local_width:]
    mate = swap(jnp.concatenate([sums.astype(BF16), gu_far, gn_far, gd_far.astype(BF16)], 1), "mp", 2)
    out_near = swap(after(out_send, near), "mp", 1)
    d_merged, send = attend_back(
        index, merged, (mine, other), g_blocks, (stat_mine, stat_other), seg, col, slopes, aq, bq, wq
    )
    send, d_merged, mate, out_near = lax.optimization_barrier((send, d_merged, mate, out_near))

    relay = swap(send, "mp", 1)
    first_pack = jnp.concatenate([sums, gu_own, gn_own, gd_own], 1) + mate.astype(F32)
    first_pack = jnp.concatenate([first_pack.astype(BF16), jnp.full((rank, 128), which, BF16)], 1)
    first_pack = lax.all_gather(first_pack, "dp", axis=0)
    ga_qkv, gb_qkv = inner_grads(d_merged, z_qkv, normed, bq)
    ga_low, d_merged = lax.optimization_barrier((ga_qkv.astype(BF16), d_merged))
    ga_others = [swap(ga_low, "mp", r) for r in (1, 2, 3)]
    send_two, send_one = project_back(index, d_merged, wq, aq, bq, (2, 1))
    relay, send_one, send_two, out_near, *ga_others = lax.optimization_barrier(
        (relay, send_one, send_two, out_near, *ga_others)
    )

    d_two = swap((send_two.astype(F32) + relay.astype(F32)).astype(BF16), "mp", 2)
    d_one = swap(send_one, "mp", 1)
    layer_out = (middle[:own_rows].astype(F32) + out_own + out_near.astype(F32)).astype(BF16)
    ga_qkv = ga_qkv + sum(g.astype(F32) for g in ga_others)
    second_pack = jnp.concatenate([ga_qkv, gb_qkv], 1).astype(BF16)
    second_pack = lax.all_gather(second_pack, "dp", axis=0)
    ids = first_pack[:, 0, -1].astype(jnp.int32)
    (kept,) = project_back(after(index, ids), d_merged, wq, aq, bq, (0,))
    ga_up, gb_down, gb_dense, gb_up, ga_down, ga_dense, ga_qkv, gb_qkv = spread(
        ids, first_pack, second_pack, kinds, width, local_width, local_ff
    )
    d_one, d_two = lax.optimization_barrier((d_one, d_two, gb_qkv))[:2]
    input_grad = last_norm(kept, d_one, d_two, layer_in, d_low, first_gain)
    return (
        layer_out,
        input_grad,
        ga_qkv.transpose(2, 0, 1),
        gb_qkv.transpose(0, 2, 1, 3),
        ga_dense.transpose(2, 0, 1),
        gb_dense,
        ga_up.transpose(2, 0, 1),
        gb_up,
        ga_down.transpose(2, 0, 1),
        gb_down,
    )


def solution(mesh):
    return jax.shard_map(
        local,
        mesh=mesh,
        in_specs=(
            P(("dp", "mp"), None), P(), P(), P(None, None, "mp"), P(), P(None, None, None, "mp"), P("mp", None),
            P("mp", None, None), P(), P(), P(), P(None, "mp"), P(), P(None, None, "mp"), P("mp", None),
            P("mp", None, None), P(), P("dp", None), P("dp"), P(("dp", "mp"), None),
        ),
        out_specs=(
            P(("dp", "mp"), None), P(("dp", "mp"), None), P(), P(None, None, None, "mp"), P("mp", None, None), P(),
            P(), P(None, None, "mp"), P("mp", None, None), P(),
        ),
        check_vma=False,
    )
```

```python
import functools

import jax
import jax.numpy as jnp
from jax import lax
from jax.experimental import pallas as pl
from jax.experimental.pallas import tpu as pltpu
from jax.sharding import PartitionSpec as P

HEADS = 32
HD = 64
LONGEST = 512
EPSILON = 1e-05
F32 = jnp.float32
BF16 = jnp.bfloat16
MASKED = -1e30
WHOLE = pl.BlockSpec(memory_space=pltpu.VMEM)
REMOTE = pl.BlockSpec(memory_space=pl.ANY)


def shape(dims, kind=BF16):
    return jax.ShapeDtypeStruct(dims, kind)


def statistics(values):
    center = jnp.mean(values, -1, keepdims=True)
    centred = values - center
    variance = jnp.mean(centred * centred, -1, keepdims=True)
    scaler = lax.rsqrt(variance + EPSILON)
    return centred * scaler, scaler


def layer_norm(values, gain, bias):
    return statistics(values)[0] * gain.astype(F32) + bias.astype(F32)


def norm_back(grad, values, gain):
    normal, scaler = statistics(values)
    scaled = grad * gain.astype(F32)
    first_mean = jnp.mean(scaled, -1, keepdims=True)
    second_mean = jnp.mean(scaled * normal, -1, keepdims=True)
    return (scaled - first_mean - normal * second_mean) * scaler


def by_rows(count, body, chunk=32):
    for i in range(count // chunk):
        body(slice(i * chunk, (i + 1) * chunk))


def dot_nn(left, right):
    return jnp.dot(left, right, preferred_element_type=F32)


def dot_nt(left, right):
    return lax.dot_general(left, right, (((1,), (1,)), ((), ())), preferred_element_type=F32)


def dot_tn(left, right):
    return lax.dot_general(left, right, (((0,), (0,)), ((), ())), preferred_element_type=F32)


def swap(value, axis, bit):
    pairs = [(i, i ^ bit) for i in range(lax.axis_size(axis))]
    return lax.ppermute(value, axis, pairs)


def after(value, *others):
    return lax.optimization_barrier((value, *others))[0]


def gelu_pair(values):
    below = 0.5 * (1.0 + lax.erf(values * 0.5 ** 0.5))
    density = jnp.exp(values * values * -0.5) * 0.3989422804014327
    return values * below, below + values * density


def project_kernel(kept, at_ref, x_ref, gain_ref, bias_ref, aq_ref, bq_ref, wq_ref, *refs):
    merged_ref, normed_ref, z_ref, w_ref, out_ref, low_ref, thin_ref, sems, loads = refs[kept:]
    count = x_ref.shape[0]
    rows = pl.ds(pl.multiple_of(at_ref[0] * count, count), count)
    parts = wq_ref.shape[0]

    def load(i):
        return pltpu.make_async_copy(wq_ref.at[i], w_ref.at[i], loads.at[i])

    def save(i):
        return pltpu.make_async_copy(out_ref.at[i], merged_ref.at[i, rows, :], sems.at[2 + i])

    for i in range(parts):
        load(i).start()

    chunk = min(64, count)

    def norm(i, carry):
        part = pl.ds(pl.multiple_of(i * chunk, chunk), chunk)
        low_ref[part, :] = layer_norm(x_ref[part, :].astype(F32), gain_ref[...], bias_ref[...]).astype(BF16)
        return carry

    lax.fori_loop(0, count // chunk, norm, 0, unroll=2)
    copies = [pltpu.make_async_copy(low_ref, normed_ref.at[rows, :], sems.at[0])]
    copies[0].start()
    thin_ref[...] = dot_nt(low_ref[...], aq_ref[...]).astype(BF16)
    copies.append(pltpu.make_async_copy(thin_ref, z_ref.at[rows, :], sems.at[1]))
    copies[1].start()

    width = out_ref.shape[2]
    tile = min(256, width)
    tiles = width // tile

    def one(step, carry):
        i, t = step // tiles, step % tiles
        cols = pl.ds(pl.multiple_of(t * tile, tile), tile)

        @pl.when(t == 0)
        def _():
            load(i).wait()

        value = dot_nn(low_ref[...], w_ref[i, :, cols]) + dot_nn(thin_ref[...], bq_ref[i, :, cols])
        out_ref[i, :, cols] = value.astype(BF16)

        @pl.when(t == tiles - 1)
        def _():
            save(i).start()

        return carry

    lax.fori_loop(0, parts * tiles, one, 0)
    for copy in copies + [save(i) for i in range(parts)]:
        copy.wait()


def project(at, rows, gain, bias, aq, bq, wq, total, earlier):
    count, width = rows.shape
    parts, _, local_width = wq.shape
    rank = aq.shape[0]
    kept = len(earlier)
    return pl.pallas_call(
        functools.partial(project_kernel, kept),
        out_shape=(shape((parts, total, local_width)), shape((total, width)), shape((total, rank))),
        grid_spec=pltpu.PrefetchScalarGridSpec(
            num_scalar_prefetch=1,
            grid=(),
            in_specs=[WHOLE] * 5 + [REMOTE] * (1 + kept),
            out_specs=(REMOTE,) * 3,
            scratch_shapes=[
                pltpu.VMEM(wq.shape, BF16),
                pltpu.VMEM((parts, count, local_width), BF16),
                pltpu.VMEM((count, width), BF16),
                pltpu.VMEM((count, rank), BF16),
                pltpu.SemaphoreType.DMA((2 + parts,)),
                pltpu.SemaphoreType.DMA((parts,)),
            ],
        ),
        input_output_aliases={7 + i: i for i in range(kept)},
        name="project",
    )(at.reshape(1), rows, gain, bias, aq, bq, wq, *earlier)


def lane_mask(half):
    return (lax.broadcasted_iota(jnp.int32, (1, 2 * HD), 1) // HD) == half


def allowed_pairs(seg_col, seg_row, causal):
    dims = (seg_col.shape[0], seg_row.shape[1])
    allowed = seg_col == seg_row
    if causal:
        allowed = allowed & (lax.broadcasted_iota(jnp.int32, dims, 0) <= lax.broadcasted_iota(jnp.int32, dims, 1))
    return allowed


def reach_of(block):
    return -(-LONGEST // block)


def attend_kernel(block, count, first_ref, seg_ref, slope_ref, col_ref, row_ref, q_ref, k_ref, v_ref,
                  o_ref, stat_ref, turned_ref, top_ref, total_ref, sum_ref):
    pair = pl.program_id(0)
    turned_ref[...] = v_ref[0].T

    for own in range(count):
        i = first_ref[0] ^ own
        start = pl.multiple_of(i * block, block)
        here = pl.ds(own * block, block)
        query = q_ref[0, pl.ds(start, block), :] * HD ** -0.5
        scaled = [jnp.where(lane_mask(half), query, 0).astype(BF16) for half in range(2)]

        def one(back):
            at = pl.multiple_of(start - back * block, block)
            keys = pl.ds(at, block)
            allowed = allowed_pairs(col_ref[keys, :1], row_ref[:, pl.ds(start, block)], back == 0)
            place = lax.broadcasted_iota(jnp.int32, (block, block), 0).astype(F32)
            for half in range(2):
                slope = slope_ref[2 * pair + half]
                shift = slope * at.astype(F32)
                scores = jnp.where(allowed, dot_nt(k_ref[0, keys, :], scaled[half]) + slope * place, MASKED)
                best = jnp.max(scores, 0, keepdims=True) + shift
                if back:
                    before = top_ref[half]
                    best = jnp.maximum(best, before)
                weights = jnp.exp(scores - (best - shift))
                total = jnp.sum(weights, 0, keepdims=True)
                result = dot_nn(turned_ref[half * HD:(half + 1) * HD, keys], weights.astype(BF16))
                if back:
                    fade = jnp.exp(before - best)
                    total = total + fade * total_ref[half]
                    result = result + fade * sum_ref[half]
                top_ref[half] = best
                total_ref[half] = total
                sum_ref[half] = result

        one(0)
        for back in range(1, reach_of(block) + 1):
            last = jnp.maximum(start - (back - 1) * block - 1, 0)

            @pl.when((i >= back) & (seg_ref[last] == seg_ref[start]))
            def _(back=back):
                one(back)

        for half in range(2):
            stat_ref[half, :, here] = top_ref[half] + jnp.log(total_ref[half])
        done = jnp.concatenate([sum_ref[half] / total_ref[half] for half in range(2)], 0)
        o_ref[here, :] = done.T.astype(BF16)


def attend(first, merged, seg, col, slopes, count):
    _, rows, width = merged.shape
    block = min(256, rows)
    heads = width // HD

    def part(i):
        return pl.BlockSpec((1, rows, 2 * HD), lambda h, *_: (i, 0, h))

    return pl.pallas_call(
        functools.partial(attend_kernel, block, count),
        out_shape=(shape((count * block, width)), shape((heads, 1, count * block), F32)),
        grid_spec=pltpu.PrefetchScalarGridSpec(
            num_scalar_prefetch=3,
            grid=(heads // 2,),
            in_specs=[
                pl.BlockSpec((rows, 128), lambda h, *_: (0, 0)),
                pl.BlockSpec((1, rows), lambda h, *_: (0, 0)),
                part(0), part(1), part(2),
            ],
            out_specs=(
                pl.BlockSpec((count * block, 2 * HD), lambda h, *_: (0, h)),
                pl.BlockSpec((2, 1, count * block), lambda h, *_: (h, 0, 0)),
            ),
            scratch_shapes=[
                pltpu.VMEM((2 * HD, rows), BF16),
                pltpu.VMEM((2, 1, block), F32),
                pltpu.VMEM((2, 1, block), F32),
                pltpu.VMEM((2, HD, block), F32),
            ],
        ),
        name="attend",
    )(first.reshape(1), seg, slopes, col, seg[None, :], merged, merged, merged)


def attend_back_kernel(block, at_ref, seg_ref, slope_ref, col_ref, row_ref, *refs):
    stats, mixed, grads_in = refs[:2], refs[2:4], refs[4:8]
    q_ref, k_ref, v_ref, aq_ref, bq_ref, wq_ref, d_ref, send_ref = refs[8:16]
    stat_ref, m_ref, g_ref, turned_ref, center_ref, qsum_ref, ksum_ref, vsum_ref, w_ref, held_ref, loads = refs[16:]
    pair = pl.program_id(0)

    def load(i):
        return pltpu.make_async_copy(wq_ref.at[i], w_ref.at[i], loads.at[i])

    @pl.when(pair == 0)
    def _():
        for i in range(3):
            load(i).start()

    count = g_ref.shape[0] // block
    size = grads_in[0].shape[0]
    for r, ref in enumerate(grads_in):
        rows = pl.ds(pl.multiple_of((at_ref[0] ^ r) * size, size), size)
        part = slice((r % 2) * size, (r % 2 + 1) * size)
        g_ref[rows, :] = ref[...]
        m_ref[rows, :] = mixed[r // 2][part, :]
        stat_ref[:, :, rows] = stats[r // 2][:, :, part]
    turned_ref[...] = k_ref[0].T
    product = (g_ref[...].astype(F32) * m_ref[...].astype(F32)).T
    for half in range(2):
        center_ref[half:half + 1] = jnp.sum(product[half * HD:(half + 1) * HD], 0, keepdims=True)
    qsum_ref[...] = jnp.zeros_like(qsum_ref)
    ksum_ref[...] = jnp.zeros_like(ksum_ref)
    vsum_ref[...] = jnp.zeros_like(vsum_ref)

    for i in range(count):
        queries = pl.ds(i * block, block)
        query = q_ref[0, queries, :] * HD ** -0.5
        scaled = [jnp.where(lane_mask(half), query, 0).astype(BF16) for half in range(2)]
        grads = [jnp.where(lane_mask(half), g_ref[queries, :], 0).astype(BF16) for half in range(2)]

        def one(j):
            keys = pl.ds(j * block, block)
            allowed = allowed_pairs(col_ref[keys, :1], row_ref[:, queries], i == j)
            place = lax.broadcasted_iota(jnp.int32, (block, block), 0).astype(F32)
            val_part, key_part = 0.0, 0.0
            for half in range(2):
                slope = slope_ref[2 * pair + half]
                shift = slope * float(j * block)
                scores = jnp.where(allowed, dot_nt(k_ref[0, keys, :], scaled[half]) + slope * place, MASKED)
                probs = jnp.exp(scores - (stat_ref[half, :, queries] - shift))
                d_probs = dot_nt(v_ref[0, keys, :], grads[half])
                d_scores = (probs * (d_probs - center_ref[half:half + 1, queries])).astype(BF16)
                val_part = val_part + dot_nn(probs.astype(BF16), grads[half])
                key_part = key_part + dot_nn(d_scores, scaled[half])
                rows = slice(half * HD, (half + 1) * HD)
                qsum_ref[rows, queries] += dot_nn(turned_ref[rows, keys], d_scores)
            vsum_ref[keys, :] += val_part
            ksum_ref[keys, :] += key_part

        one(i)
        for back in range(1, min(i, reach_of(block)) + 1):
            j = i - back

            @pl.when(seg_ref[j * block + block - 1] == seg_ref[i * block])
            def _(j=j):
                one(j)

    d_ref[0] = (qsum_ref[...] * HD ** -0.5).T.astype(BF16)
    d_ref[1] = ksum_ref[...].astype(BF16)
    d_ref[2] = vsum_ref[...].astype(BF16)
    sent = pl.ds(pl.multiple_of((at_ref[0] ^ 3) * size, size), size)
    cols = pl.ds(pl.multiple_of(pair * 2 * HD, 2 * HD), 2 * HD)
    for i in range(3):
        held_ref[i, :, cols] = d_ref[i, sent, :]

    @pl.when(pair == pl.num_programs(0) - 1)
    def _():
        for i in range(3):
            load(i).wait()
        inner = sum(dot_nt(held_ref[i], bq_ref[i]) for i in range(3)).astype(BF16)
        tile = 512

        def one(t, carry):
            here = pl.ds(pl.multiple_of(t * tile, tile), tile)
            total = dot_nn(inner, aq_ref[:, here])
            for i in range(3):
                total = total + dot_nt(held_ref[i], w_ref[i, here, :])
            send_ref[:, here] = total.astype(BF16)
            return carry

        lax.fori_loop(0, send_ref.shape[1] // tile, one, 0)


def attend_back(at, merged, mixed, grads, stats, seg, col, slopes, aq, bq, wq):
    parts, rows, width = merged.shape
    block = min(256, rows)
    half = rows // 2

    def wide(count):
        return pl.BlockSpec((count, 2 * HD), lambda h, *_: (0, h))

    def part(i):
        return pl.BlockSpec((1, rows, 2 * HD), lambda h, *_: (i, 0, h))

    return pl.pallas_call(
        functools.partial(attend_back_kernel, block),
        out_shape=(shape(merged.shape), shape((rows // 4, aq.shape[1]))),
        grid_spec=pltpu.PrefetchScalarGridSpec(
            num_scalar_prefetch=3,
            grid=(width // (2 * HD),),
            in_specs=[
                pl.BlockSpec((rows, 128), lambda h, *_: (0, 0)),
                pl.BlockSpec((1, rows), lambda h, *_: (0, 0)),
            ] + [pl.BlockSpec((2, 1, half), lambda h, *_: (h, 0, 0))] * 2 + [wide(half)] * 2 + [wide(rows // 4)] * 4 + [
                part(0), part(1), part(2),
                pl.BlockSpec(aq.shape, lambda h, *_: (0, 0)), pl.BlockSpec(bq.shape, lambda h, *_: (0, 0, 0)), REMOTE,
            ],
            out_specs=(
                pl.BlockSpec((parts, rows, 2 * HD), lambda h, *_: (0, 0, h)),
                pl.BlockSpec((rows // 4, aq.shape[1]), lambda h, *_: (0, 0)),
            ),
            scratch_shapes=[
                pltpu.VMEM((2, 1, rows), F32),
                pltpu.VMEM((rows, 2 * HD), BF16),
                pltpu.VMEM((rows, 2 * HD), BF16),
                pltpu.VMEM((2 * HD, rows), BF16),
                pltpu.VMEM((2, rows), F32),
                pltpu.VMEM((2 * HD, rows), F32),
                pltpu.VMEM((rows, 2 * HD), F32),
                pltpu.VMEM((rows, 2 * HD), F32),
                pltpu.VMEM(wq.shape, BF16),
                pltpu.VMEM((parts, rows // 4, width), BF16),
                pltpu.SemaphoreType.DMA((parts,)),
            ],
        ),
        name="attend_back",
    )(at.reshape(1), seg, slopes, col, seg[None, :], *stats, *mixed, *grads, merged, merged, merged, aq, bq, wq)


def dense_kernel(x0_ref, x1_ref, m0_ref, m1_ref, m2_ref, m3_ref, a_ref, bd_ref, gain_ref, bias_ref, au_ref,
                 own_ref, far_ref, middle_ref, second_ref, zd_ref, zu_ref, w_ref, m_ref, sum_ref, loads):
    size = m0_ref.shape[1]
    count = x0_ref.shape[0]
    tiles, pieces, _, thick, tile = w_ref.shape

    def columns(t):
        return pl.ds(pl.multiple_of(t * tile, tile), tile)

    def load(t):
        cols = columns(t)
        own = own_ref.reshape(pieces, thick, own_ref.shape[1]).at[:, :, cols]
        far = far_ref.at[:, pl.ds(4, 3), :, cols]
        return (
            pltpu.make_async_copy(own, w_ref.at[t, :, 0], loads.at[0, t]),
            pltpu.make_async_copy(far, w_ref.at[t, :, pl.ds(1, 3)], loads.at[1, t]),
        )

    def start(t, carry):
        for copy in load(t):
            copy.start()
        return carry

    lax.fori_loop(0, tiles, start, 0)
    for r, m in enumerate((m0_ref, m1_ref, m2_ref, m3_ref)):
        cols = slice(r * size, (r + 1) * size)
        m_ref[:count, cols] = m[(r % 2) * count:(r % 2 + 1) * count, :]
        m_ref[count:, cols] = m[(1 - r % 2) * count:(2 - r % 2) * count, :]
    zd_ref[...] = dot_nt(m_ref[...], a_ref[...]).astype(BF16)

    def one(t, carry):
        cols = columns(t)
        for copy in load(t):
            copy.wait()
        total = dot_nn(zd_ref[...], bd_ref[:, cols])
        for r in range(4):
            weights = w_ref[t, :, r].reshape(pieces * thick, tile)
            total = total + dot_nn(m_ref[:, r * size:(r + 1) * size], weights)
        sum_ref[:count, cols] = total[:count] + x0_ref[:, cols].astype(F32)
        sum_ref[count:, cols] = total[count:] + x1_ref[:, cols].astype(F32)
        return carry

    lax.fori_loop(0, tiles, one, 0)
    chunk = min(64, count)

    def norm(i, carry):
        part = pl.ds(pl.multiple_of(i * chunk, chunk), chunk)
        values = sum_ref[part, :]
        middle_ref[part, :] = values.astype(BF16)
        second_ref[part, :] = layer_norm(values, gain_ref[...], bias_ref[...]).astype(BF16)
        return carry

    lax.fori_loop(0, 2 * count // chunk, norm, 0, unroll=2)
    zu_ref[...] = dot_nt(second_ref[...], au_ref[...]).astype(BF16)


def dense(x_own, x_far, m_parts, ad, bd, gain, bias, au, w_own, w_far):
    count, width = x_own.shape
    rank = ad.shape[0]
    tile = min(256, width)
    pieces, _, thick, _ = w_far.shape
    return pl.pallas_call(
        dense_kernel,
        out_shape=(
            shape((2 * count, width)), shape((2 * count, width)), shape((2 * count, rank)),
            shape((2 * count, rank)),
        ),
        in_specs=[WHOLE] * 11 + [REMOTE] * 2,
        out_specs=(WHOLE,) * 4,
        scratch_shapes=[
            pltpu.VMEM((width // tile, pieces, 4, thick, tile), BF16), pltpu.VMEM((2 * count, width), BF16),
            pltpu.VMEM((2 * count, width), F32), pltpu.SemaphoreType.DMA((2, width // tile)),
        ],
        name="dense",
    )(x_own, x_far, *m_parts, ad, bd, gain, bias, au, w_own, w_far)


def feed_kernel(grads, earlier, known, at_ref, x_ref, up_ref, down_ref, zu_ref, bu_ref, an_ref, au_ref, *refs):
    step = pl.program_id(0)
    g_refs, other_ref, refs = refs[:grads], refs[grads], refs[grads + 1:]
    if known:
        slope_ref, refs = refs[0], refs[1:]
    if earlier:
        active_ref, refs = (None, refs) if known else (refs[1], refs[:1] + refs[2:])
        before_ref, hidden_ref, dz_out_ref, out_ref, g_ref, total_ref, inner_ref, held_ref, sem = refs
        dz_ref = other_ref
        count = held_ref.shape[0]
        copy = pltpu.make_async_copy(before_ref.at[pl.ds(at_ref[0] * count, count), :], held_ref, sem)
    else:
        active_ref, hidden_ref, dz_out_ref, out_ref, dz_ref, g_ref, total_ref, inner_ref = refs

    @pl.when(step == 0)
    def _():
        if earlier:
            copy.start()
        start = 0
        for ref in g_refs:
            g_ref[start:start + ref.shape[0], :] = ref[...]
            start += ref.shape[0]
        total_ref[...] = jnp.zeros_like(total_ref)
        inner_ref[...] = jnp.zeros_like(inner_ref)
        if not earlier:
            dz_ref[...] = dot_nt(g_ref[...], other_ref[...]).astype(BF16)

    up = up_ref[...].reshape(x_ref.shape[1], hidden_ref.shape[1])
    d_active = dot_nt(g_ref[...], down_ref[...]) + dot_nn(dz_ref[...], an_ref[...])
    if known:
        slope = slope_ref[...].astype(F32)
    else:
        hidden = dot_nn(x_ref[...], up) + dot_nn(zu_ref[...], bu_ref[...])
        active, slope = gelu_pair(hidden)
        active_ref[...] = active.astype(BF16)
    d_hidden = (d_active * slope).astype(BF16)
    hidden_ref[...] = d_hidden
    total_ref[...] += dot_nt(d_hidden, up)
    inner_ref[...] += dot_nt(d_hidden, bu_ref[...])

    @pl.when(step == pl.num_programs(0) - 1)
    def _():
        inner = inner_ref[...].astype(BF16)
        dz_out_ref[...] = inner
        total = total_ref[...] + dot_nn(inner, au_ref[...])
        if earlier:
            copy.wait()
            total = total + held_ref[...]
        out_ref[...] = total.astype(out_ref.dtype)


def hidden_kernel(at_ref, x_ref, up_ref, zu_ref, bu_ref, active_ref, slope_ref):
    up = up_ref[...].reshape(x_ref.shape[1], active_ref.shape[1])
    active, slope = gelu_pair(dot_nn(x_ref[...], up) + dot_nn(zu_ref[...], bu_ref[...]))
    active_ref[...] = active.astype(BF16)
    slope_ref[...] = slope.astype(BF16)


def hidden_units(at, count, x, up, zu, bu):
    width = x.shape[1]
    ff = up.shape[3]
    tile = min(512, ff)
    rank = bu.shape[0]
    cols = pl.BlockSpec((count, tile), lambda t, at: (0, t))
    return pl.pallas_call(
        hidden_kernel,
        out_shape=(shape((count, ff)),) * 2,
        grid_spec=pltpu.PrefetchScalarGridSpec(
            num_scalar_prefetch=1,
            grid=(ff // tile,),
            in_specs=[
                pl.BlockSpec((count, width), lambda t, at: (at[0], 0), pipeline_mode=pl.Buffered(1)),
                pl.BlockSpec((up.shape[0], 4, up.shape[2], tile), lambda t, at: (0, 0, 0, t)),
                pl.BlockSpec((count, rank), lambda t, at: (at[0], 0)), pl.BlockSpec((rank, tile), lambda t, at: (0, t)),
            ],
            out_specs=(cols, cols),
        ),
        name="hidden_units",
    )(jnp.full((1,), at, jnp.int32), x, up, zu, bu)


def feed(at, count, x, g, up, down, zu, other, bu, an, au, before, kind, slope=None):
    width = x.shape[1]
    ff = up.shape[3]
    tile = min(512 if before is not None else 256, ff)
    rank = bu.shape[0]
    earlier = before is not None
    once = pl.Buffered(1)
    rows = pl.BlockSpec((count, width), lambda t, at: (at[0], 0), pipeline_mode=once)
    thin = pl.BlockSpec((count, rank), lambda t, at: (at[0], 0))
    cols = pl.BlockSpec((count, tile), lambda t, at: (0, t))
    row = pl.BlockSpec((rank, tile), lambda t, at: (0, t))
    flat = pl.BlockSpec((rank, width), lambda t, at: (0, 0))
    out_shape = [shape((count, ff)), shape((count, ff)), shape((count, rank)), shape((count, width), kind)]
    out_specs = [
        cols, cols, pl.BlockSpec((count, rank), lambda t, at: (0, 0)),
        pl.BlockSpec((count, width), lambda t, at: (0, 0), pipeline_mode=once),
    ]
    scratch = [pltpu.VMEM((count, width), BF16), pltpu.VMEM((count, width), F32), pltpu.VMEM((count, rank), F32)]
    known = slope is not None
    if known:
        out_shape, out_specs = out_shape[1:], out_specs[1:]
    if earlier:
        extra = [thin] + [cols] * known + [REMOTE]
        scratch += [pltpu.VMEM((count, width), F32), pltpu.SemaphoreType.DMA(())]
    else:
        extra = [flat]
        out_shape.append(shape((count, rank)))
        out_specs.append(pl.BlockSpec((count, rank), lambda t, at: (0, 0)))
    return pl.pallas_call(
        functools.partial(feed_kernel, len(g), earlier, known),
        out_shape=tuple(out_shape),
        grid_spec=pltpu.PrefetchScalarGridSpec(
            num_scalar_prefetch=1,
            grid=(ff // tile,),
            in_specs=[
                rows, pl.BlockSpec((up.shape[0], 4, up.shape[2], tile), lambda t, at: (0, 0, 0, t)),
                pl.BlockSpec((tile, width), lambda t, at: (t, 0)), thin, row, row, flat,
            ] + [pl.BlockSpec(b.shape, lambda t, at: (0, 0), pipeline_mode=once) for b in g] + extra,
            out_specs=tuple(out_specs),
            scratch_shapes=scratch,
        ),
        name="feed",
    )(
        jnp.full((1,), at, jnp.int32), x, up, down, zu, bu, an, au, *g, other, *((slope,) if known else ()),
        *((before,) if earlier else ()),
    )


def emit_kernel(earlier, at_ref, active_ref, hidden_ref, down_ref, an_ref, bn_ref, z_in_ref, d_in_ref, *refs):
    if earlier:
        before_ref, gn_ref, gu_ref, z_ref, out_ref = refs
    else:
        gn_ref, gu_ref, z_ref, out_ref = refs

    @pl.when(pl.program_id(0) == 0)
    def _():
        z_ref[...] = dot_nt(active_ref[...], an_ref[...]).astype(BF16)
        gn_ref[...] = dot_tn(d_in_ref[...], active_ref[...]).astype(BF16)
        gu_ref[...] = dot_tn(z_in_ref[...], hidden_ref[...]).astype(BF16)

    total = dot_nn(active_ref[...], down_ref[...]) + dot_nn(z_ref[...], bn_ref[...])
    if earlier:
        total = total + before_ref[...]
    out_ref[...] = total.astype(out_ref.dtype)


def emit(at, active, hidden, down, an, bn, zu, dz, before, kind):
    count, ff = active.shape
    width = down.shape[1]
    tile = min(512, width)
    rank = an.shape[0]
    earlier = before is not None
    once = pl.Buffered(1)
    whole = pl.BlockSpec((count, ff), lambda t, at: (0, 0), pipeline_mode=once)
    flat = pl.BlockSpec((rank, ff), lambda t, at: (0, 0))
    thin = pl.BlockSpec((count, rank), lambda t, at: (at[0], 0))
    return pl.pallas_call(
        functools.partial(emit_kernel, earlier),
        out_shape=(shape((rank, ff)), shape((rank, ff)), shape((count, rank)), shape((count, width), kind)),
        grid_spec=pltpu.PrefetchScalarGridSpec(
            num_scalar_prefetch=1,
            grid=(width // tile,),
            in_specs=[
                whole, whole, pl.BlockSpec((ff, tile), lambda t, at: (0, t)), flat,
                pl.BlockSpec((rank, tile), lambda t, at: (0, t)), thin, thin,
            ] + [pl.BlockSpec((count, tile), lambda t, at: (at[0], t))] * earlier,
            out_specs=(
                flat, flat, pl.BlockSpec((count, rank), lambda t, at: (0, 0)),
                pl.BlockSpec((count, tile), lambda t, at: (0, t)),
            ),
        ),
        name="emit",
    )(jnp.full((1,), at, jnp.int32), active, hidden, down, an, bn, zu, dz, *((before,) if earlier else ()))


def dense_back_kernel(own_ref, far_ref, cot_ref, gain_ref, bd_ref, ad_ref, middle_ref, w0_ref, w1_ref,
                      low_out_ref, dz_ref, *refs):
    outs = refs[:4]
    mid_ref, w_ref, loads = refs[4:]
    count, width = own_ref.shape
    size = outs[0].shape[1]
    pieces, _, thick, _ = w1_ref.shape
    first = pltpu.make_async_copy(middle_ref.at[pl.ds(0, count), :], mid_ref, loads.at[4])
    first.start()
    pltpu.make_async_copy(w0_ref.reshape(pieces, thick, width), w_ref.at[0], loads.at[0]).start()

    def start(r, carry):
        pltpu.make_async_copy(w1_ref.at[:, r + 3], w_ref.at[r], loads.at[r]).start()
        return carry

    lax.fori_loop(1, 4, start, 0)
    first.wait()
    chunk = min(64, count)

    def norm(i, carry):
        part = pl.ds(pl.multiple_of(i * chunk, chunk), chunk)
        grad = own_ref[part, :].astype(F32) + far_ref[part, :].astype(F32)
        change = norm_back(grad, mid_ref[part, :].astype(F32), gain_ref[...])
        low_out_ref[part, :] = (cot_ref[part, :].astype(F32) + change).astype(BF16)
        return carry

    lax.fori_loop(0, count // chunk, norm, 0, unroll=4)
    dz_ref[...] = dot_nt(low_out_ref[...], bd_ref[...]).astype(BF16)

    def one(r, carry):
        pltpu.make_async_copy(w1_ref.at[:, 0], w_ref.at[r], loads.at[r]).wait()
        weights = w_ref[r].reshape(size, width)
        cols = pl.ds(pl.multiple_of(r * size, size), size)
        value = (dot_nt(low_out_ref[...], weights) + dot_nn(dz_ref[...], ad_ref[:, cols])).astype(BF16)
        for n, out in enumerate(outs):

            @pl.when(r == n)
            def _(out=out):
                out[...] = value

        return carry

    lax.fori_loop(0, 4, one, 0)


def dense_back(own, far, middle, cot, gain, bd, ad, w_own, w_far):
    count, width = own.shape
    rank = bd.shape[0]
    return pl.pallas_call(
        dense_back_kernel,
        out_shape=(shape((count, width)), shape((count, rank))) + (shape((count, width // 4)),) * 4,
        in_specs=[WHOLE] * 6 + [REMOTE] * 3,
        out_specs=(WHOLE,) * 6,
        scratch_shapes=[
            pltpu.VMEM((count, width), BF16), pltpu.VMEM((4, w_far.shape[0]) + w_far.shape[2:], BF16),
            pltpu.SemaphoreType.DMA((5,)),
        ],
        name="dense_back",
    )(own, far, cot, gain, bd, ad, middle, w_own, w_far)


def project_back_kernel(order, at_ref, aq_ref, bq_ref, d_ref, wq_ref, *refs):
    outs = refs[:len(order)]
    part_ref, w_ref, inner_ref, sems, loads = refs[len(order):]
    count = outs[0].shape[0]
    tiles, _, tile, _ = w_ref.shape

    def columns(t):
        return pl.ds(pl.multiple_of(t * tile, tile), tile)

    def fetch(place):
        rows = pl.ds(pl.multiple_of((at_ref[0] ^ order[place]) * count, count), count)
        here = pl.ds(place * count, count)
        return pltpu.make_async_copy(d_ref.at[:, rows, :], part_ref.at[:, here, :], sems.at[place])

    def load(t):
        return pltpu.make_async_copy(wq_ref.at[:, columns(t), :], w_ref.at[t], loads.at[t])

    def start(t, carry):
        load(t).start()
        return carry

    blocks = [fetch(place) for place in range(len(order))]
    for copy in blocks:
        copy.start()
    lax.fori_loop(0, tiles, start, 0)
    for copy in blocks:
        copy.wait()
    inner_ref[...] = sum(dot_nt(part_ref[i], bq_ref[i]) for i in range(3)).astype(BF16)

    def one(t, carry):
        load(t).wait()
        cols = columns(t)
        total = dot_nn(inner_ref[...], aq_ref[:, cols])
        for i in range(3):
            total = total + dot_nt(part_ref[i], w_ref[t, i])
        for place, out in enumerate(outs):
            out[:, cols] = total[place * count:(place + 1) * count].astype(BF16)
        return carry

    lax.fori_loop(0, tiles, one, 0)


def project_back(at, d_merged, wq, aq, bq, order):
    parts, total, local_width = d_merged.shape
    width = wq.shape[1]
    count = total // 4
    tile = min(512, width)
    rows = len(order) * count
    return pl.pallas_call(
        functools.partial(project_back_kernel, order),
        out_shape=(shape((count, width)),) * len(order),
        in_specs=[pl.BlockSpec(memory_space=pltpu.SMEM)] + [WHOLE] * 2 + [REMOTE] * 2,
        out_specs=(WHOLE,) * len(order),
        scratch_shapes=[
            pltpu.VMEM((parts, rows, local_width), BF16), pltpu.VMEM((width // tile, parts, tile, local_width), BF16),
            pltpu.VMEM((rows, aq.shape[0]), BF16),
            pltpu.SemaphoreType.DMA((len(order),)), pltpu.SemaphoreType.DMA((width // tile,)),
        ],
        name="project_back",
    )(at.reshape(1), aq, bq, d_merged, wq)


def inner_kernel(d_ref, z_ref, n_ref, bq_ref, ga_ref, gb_ref):
    step = pl.program_id(0)

    @pl.when(step == 0)
    def _():
        ga_ref[...] = jnp.zeros_like(ga_ref)
        gb_ref[...] = jnp.zeros_like(gb_ref)

    inner = sum(dot_nt(d_ref[i], bq_ref[i]) for i in range(3)).astype(BF16)
    ga_ref[...] += dot_tn(inner, n_ref[...])
    width = d_ref.shape[2]
    for i in range(3):
        gb_ref[:, i * width:(i + 1) * width] += dot_tn(z_ref[...], d_ref[i])


def inner_grads(d_merged, z_qkv, normed, bq):
    parts, total, local_width = d_merged.shape
    width = normed.shape[1]
    rank = z_qkv.shape[1]
    count = total // 2
    return pl.pallas_call(
        inner_kernel,
        out_shape=(shape((rank, width), F32), shape((rank, parts * local_width), F32)),
        grid=(2,),
        in_specs=[
            pl.BlockSpec((parts, count, local_width), lambda i: (0, i, 0)),
            pl.BlockSpec((count, rank), lambda i: (i, 0)),
            pl.BlockSpec((count, width), lambda i: (i, 0)),
            pl.BlockSpec(bq.shape, lambda i: (0, 0, 0)),
        ],
        out_specs=(
            pl.BlockSpec((rank, width), lambda i: (0, 0)),
            pl.BlockSpec((rank, parts * local_width), lambda i: (0, 0)),
        ),
        name="inner_grads",
    )(d_merged, z_qkv, normed, bq)


def spread_kernel(ids_ref, first_ref, second_ref, *outs):
    step = pl.program_id(0)

    @pl.when(step == 0)
    def _():
        for out in outs:
            out[...] = jnp.zeros_like(out)

    which = ids_ref[step]
    ga_up, gb_down, gb_dense, gb_up, ga_down, ga_dense, ga_qkv, gb_qkv = outs
    at = 0
    for out in (ga_up, gb_down, gb_dense, gb_up, ga_down, ga_dense):
        size = out.shape[2]
        out[which] += first_ref[0, :, at:at + size].astype(F32)
        at += size
    size = ga_qkv.shape[2]
    ga_qkv[which] += second_ref[0, :, :size].astype(F32)
    local_width = gb_qkv.shape[3]
    for i in range(3):
        gb_qkv[which, i] += second_ref[0, :, size + i * local_width:size + (i + 1) * local_width].astype(F32)


def spread(ids, first, second, kinds, width, local_width, local_ff):
    copies, rank, _ = first.shape
    dims = [(kinds, rank, n) for n in (width, width, width, local_ff, local_ff, local_width, width)]
    dims.append((kinds, 3, rank, local_width))
    return pl.pallas_call(
        spread_kernel,
        out_shape=tuple(shape(d, F32) for d in dims),
        grid_spec=pltpu.PrefetchScalarGridSpec(
            num_scalar_prefetch=1,
            grid=(copies,),
            in_specs=[
                pl.BlockSpec((1,) + first.shape[1:], lambda s, _: (s, 0, 0)),
                pl.BlockSpec((1,) + second.shape[1:], lambda s, _: (s, 0, 0)),
            ],
            out_specs=tuple(
                pl.BlockSpec(d, lambda s, _, n=len(d): (0,) * n, pipeline_mode=pl.Buffered(1)) for d in dims
            ),
        ),
        name="spread",
    )(ids, first, second)


def last_kernel(kept_ref, one_ref, two_ref, x_ref, d_ref, gain_ref, out_ref):
    grad = kept_ref[...].astype(F32) + one_ref[...].astype(F32) + two_ref[...].astype(F32)
    change = norm_back(grad, x_ref[...].astype(F32), gain_ref[...])
    out_ref[...] = (d_ref[...].astype(F32) + change).astype(BF16)


def last_norm(kept, one, two, x, d, gain):
    count, width = x.shape
    chunk = min(128, count)
    rows = pl.BlockSpec((chunk, width), lambda i: (i, 0))
    return pl.pallas_call(
        last_kernel,
        out_shape=shape((count, width)),
        grid=(count // chunk,),
        in_specs=[rows] * 5 + [pl.BlockSpec((1, width), lambda i: (0, 0))],
        out_specs=rows,
        name="last_norm",
    )(kept, one, two, x, d, gain)


def turned(factor, which):
    return lax.dynamic_index_in_dim(factor.transpose(1, 2, 0), which, 0, False)


def local(
    layer_in, first_gain, first_bias, w_qkv, a_qkv, b_qkv, w_dense, a_dense, b_dense, second_gain, second_bias,
    w_up, a_up, b_up, w_down, a_down, b_down, segment_ids, adapter_ids, cotangent,
):
    own_rows, width = layer_in.shape
    kinds = a_qkv.shape[1]
    rank = a_qkv.shape[2]
    local_width = w_dense.shape[0]
    local_ff = w_up.shape[1]
    local_heads = local_width // HD
    index = lax.axis_index("mp")
    spot = lax.axis_index("dp")
    copies = lax.axis_size("dp")
    total_rows = 4 * own_rows
    low, high = index & 1, index >> 1
    which = adapter_ids[0]
    seg = segment_ids[0]
    head_ids = (index * local_heads + lax.iota(jnp.int32, local_heads)).astype(F32)
    slopes = jnp.exp2(-8.0 * (head_ids + 1.0) / HEADS)
    first_gain, first_bias, second_gain, second_bias = (
        v[None, :] for v in (first_gain, first_bias, second_gain, second_bias)
    )

    aq, ad, au, an = (turned(a, which) for a in (a_qkv, a_dense, a_up, a_down))
    bq = lax.dynamic_index_in_dim(b_qkv.transpose(0, 2, 1, 3), which, 0, False)
    bd, bu, bn = (lax.dynamic_index_in_dim(b, which, 0, False) for b in (b_dense, b_up, b_down))
    wq = w_qkv.transpose(1, 0, 2)

    def slice_of(weight):
        size = weight.shape[0] // copies
        return lax.dynamic_slice_in_dim(weight, spot * size, size, 0)

    x_one = swap(layer_in, "mp", 1)
    x_two = swap(layer_in, "mp", 2)
    wd_slice = slice_of(w_dense)
    size = wd_slice.shape[0]
    ad_flat = ad.reshape(-1, width)
    last = size + ad_flat.shape[0]
    tail = jnp.concatenate([wd_slice, ad_flat], 0)

    def step_in(r, block, held):
        return project(index ^ r, block, first_gain, first_bias, aq, bq, wq, total_rows, held)

    held = step_in(0, layer_in, ())
    wu_halves = jnp.split(slice_of(w_up), 2, axis=0)
    wn_halves = slice_of(w_down)
    wn_halves = jnp.split(wn_halves, [3 * wn_halves.shape[0] // 4], axis=0)
    cot_halves = jnp.split(cotangent, 2, axis=0)
    pack = jnp.concatenate([tail, bu, an], 0)
    col = jnp.broadcast_to(seg[:, None], (total_rows, 128))
    early = (au, bd, bn, bu, an, first_bias, second_gain, second_bias, tail, pack, col)
    x_one, x_two, held, early, wu_halves, wn_halves, cot_halves = lax.optimization_barrier(
        (x_one, x_two, held, early, wu_halves, wn_halves, cot_halves)
    )
    au, bd, bn, bu, an, first_bias, second_gain, second_bias, tail, pack, col = early

    x_three = swap(x_two, "mp", 1)
    pack_two = swap(pack, "mp", 2)
    wu_first = swap(wu_halves[0], "mp", 2)
    held = step_in(1, x_one, held)
    held = step_in(2, x_two, held)
    x_three, pack_two, wu_first, *held = lax.optimization_barrier((x_three, pack_two, wu_first, *held))

    pack_one = swap(jnp.concatenate([tail, pack_two[:last]], 0), "mp", 1)
    wu_second = swap(after(wu_halves[1], x_three), "mp", 2)
    held = step_in(3, x_three, held)
    merged, normed, z_qkv = held
    other, stat_other = attend(index ^ 2, merged, seg, col, slopes, 2)
    other, pack_one, pack_two, wu_first, wu_second, merged = lax.optimization_barrier(
        (other, pack_one, pack_two, wu_first, wu_second, merged)
    )

    m_two = swap(other, "mp", 2)
    cot_first = swap(after(cot_halves[0], other), "mp", 1)
    bu_far, an_far = pack_two[last:last + rank], pack_two[last + rank:]
    packs = (pack_one[:last], pack_two, pack_one[last:])
    slices = jnp.concatenate([wu_first, wu_second, *(p[:size] for p in packs)], 0)
    shared = lax.all_gather(slices, "dp", axis=0).reshape(copies, 7, size, width)
    ad = jnp.concatenate([ad] + [p[size:last].reshape(rank, local_width) for p in packs], 1)
    mine, stat_mine = attend(index, merged, seg, col, slopes, 2)
    m_two, mine, cot_first = lax.optimization_barrier((m_two, mine, cot_first))

    m_one = swap(mine, "mp", 1)
    m_three = swap(m_two, "mp", 1)
    wn_first = swap(after(wn_halves[0], m_two), "mp", 2)
    m_one, m_three, wn_first = lax.optimization_barrier((m_one, m_three, wn_first))

    m_parts = [mine, m_one, m_two, m_three]
    wn_second = swap(after(wn_halves[1], m_one), "mp", 2)
    cot_second = swap(after(cot_halves[1], wn_second), "mp", 1)
    wn_far = lax.all_gather(jnp.concatenate([wn_first, wn_second], 0), "dp", axis=0, tiled=True)

    middle, second, z_dense, z_up = dense(
        layer_in, x_one, m_parts, ad, bd, second_gain, second_bias, au, w_dense, shared
    )
    second, cot_second = lax.optimization_barrier((second, cot_second))

    cot_parts = (cot_first, cot_second)
    act, dh, dzu, so_far, dz_down = feed(
        0, 2 * own_rows, second, (cotangent, *cot_parts), w_up.reshape(copies, 4, size, width), w_down, z_up, bn, bu, an,
        au, None, F32
    )
    gn_own, gu_own, zn, out_so_far = emit(0, act, dh, w_down, an, bn, z_up, dz_down, None, F32)
    act_a, slope_a = hidden_units(1, own_rows, second, shared, z_up, bu_far)
    out_so_far, so_far, act_a, slope_a = lax.optimization_barrier((out_so_far, so_far, act_a, slope_a))
    far_args = (shared, wn_far, z_up, dz_down, bu_far, an_far, au, so_far)
    dh_a, dzu_a, d_send = feed(1, own_rows, second, cot_parts, *far_args, BF16, slope_a)
    second, d_send = lax.optimization_barrier((second, d_send))

    d_near = swap(d_send, "mp", 1)
    act_b, dh_b, dzu_b, d_own = feed(0, own_rows, second, (cotangent,), *far_args, BF16)
    act_a, d_own = lax.optimization_barrier((act_a, d_own))
    gn_a, gu_a, zn_a, out_send = emit(1, act_a, dh_a, wn_far, an_far, bn, z_up, dz_down, out_so_far, BF16)
    d_near, d_own, out_send = lax.optimization_barrier((d_near, d_own, out_send))

    d_low, dz_dense, *d_mixed = dense_back(
        d_own, d_near, middle, cotangent, second_gain, bd, ad, w_dense, shared
    )
    d_low, dz_dense, act_b, *d_mixed = lax.optimization_barrier((d_low, dz_dense, act_b, *d_mixed))
    g_blocks = [d_mixed[0]] + [swap(d_mixed[r], "mp", r) for r in (1, 2, 3)]
    gn_b, gu_b, zn_b, out_own = emit(0, act_b, dh_b, wn_far, an_far, bn, z_up, dz_down, out_so_far, F32)

    def join(value, own, far):
        return (value.astype(F32) + jnp.concatenate([own, far], 0).astype(F32)).astype(BF16)

    dzu, zn_a = lax.optimization_barrier((dzu, zn_a, d_low))[:2]
    ga_up = dot_tn(join(dzu, dzu_b, dzu_a), second)
    zn = join(zn, zn_b, zn_a)
    gb_down = dot_tn(zn[:own_rows], cotangent) + dot_tn(zn[own_rows:], jnp.concatenate(cot_parts, 0))
    gb_dense = dot_tn(z_dense[:own_rows], d_low)
    gd = [dot_tn(dz_dense, m[(r % 2) * own_rows:(r % 2 + 1) * own_rows]) for r, m in enumerate(m_parts)]
    gu_far, gn_far = ((a.astype(F32) + b.astype(F32)).astype(BF16) for a, b in ((gu_a, gu_b), (gn_a, gn_b)))
    sums = jnp.concatenate([ga_up, gb_down, gb_dense], 1)
    near = swap(jnp.concatenate([sums, gd[1], gd[3]], 1).astype(BF16), "mp", 1)
    *g_blocks, near = lax.optimization_barrier((*g_blocks, near))

    near = near.astype(F32)
    sums = sums + near[:, :3 * width]
    gd_own = gd[0] + near[:, 3 * width:3 * width + local_width]
    gd_far = gd[2] + near[:, 3 * width + local_width:]
    mate = swap(jnp.concatenate([sums.astype(BF16), gu_far, gn_far, gd_far.astype(BF16)], 1), "mp", 2)
    out_near = swap(after(out_send, near), "mp", 1)
    d_merged, send = attend_back(
        index, merged, (mine, other), g_blocks, (stat_mine, stat_other), seg, col, slopes, aq, bq, wq
    )
    send, d_merged, mate, out_near = lax.optimization_barrier((send, d_merged, mate, out_near))

    relay = swap(send, "mp", 1)
    first_pack = jnp.concatenate([sums, gu_own, gn_own, gd_own], 1) + mate.astype(F32)
    first_pack = jnp.concatenate([first_pack.astype(BF16), jnp.full((rank, 128), which, BF16)], 1)
    first_pack = lax.all_gather(first_pack, "dp", axis=0)
    ga_qkv, gb_qkv = inner_grads(d_merged, z_qkv, normed, bq)
    ga_low, d_merged = lax.optimization_barrier((ga_qkv.astype(BF16), d_merged))
    ga_others = [swap(ga_low, "mp", r) for r in (1, 2, 3)]
    send_two, send_one = project_back(index, d_merged, wq, aq, bq, (2, 1))
    relay, send_one, send_two, out_near, *ga_others = lax.optimization_barrier(
        (relay, send_one, send_two, out_near, *ga_others)
    )

    send_two = (send_two.astype(F32) + relay.astype(F32)).astype(BF16)
    d_two = swap(send_two, "mp", 2)
    d_one = swap(after(send_one, send_two), "mp", 1)
    layer_out = (middle[:own_rows].astype(F32) + out_own + out_near.astype(F32)).astype(BF16)
    ga_qkv = ga_qkv + sum(g.astype(F32) for g in ga_others)
    second_pack = jnp.concatenate([ga_qkv, gb_qkv], 1).astype(BF16)
    second_pack = lax.all_gather(second_pack, "dp", axis=0)
    ids = first_pack[:, 0, -1].astype(jnp.int32)
    (kept,) = project_back(after(index, ids), d_merged, wq, aq, bq, (0,))
    ga_up, gb_down, gb_dense, gb_up, ga_down, ga_dense, ga_qkv, gb_qkv = spread(
        ids, first_pack, second_pack, kinds, width, local_width, local_ff
    )
    d_one, d_two = lax.optimization_barrier((d_one, d_two, gb_qkv))[:2]
    input_grad = last_norm(kept, d_one, d_two, layer_in, d_low, first_gain)
    return (
        layer_out,
        input_grad,
        ga_qkv.transpose(2, 0, 1),
        gb_qkv.transpose(0, 2, 1, 3),
        ga_dense.transpose(2, 0, 1),
        gb_dense,
        ga_up.transpose(2, 0, 1),
        gb_up,
        ga_down.transpose(2, 0, 1),
        gb_down,
    )


def solution(mesh):
    return jax.shard_map(
        local,
        mesh=mesh,
        in_specs=(
            P(("dp", "mp"), None), P(), P(), P(None, None, "mp"), P(), P(None, None, None, "mp"), P("mp", None),
            P("mp", None, None), P(), P(), P(), P(None, "mp"), P(), P(None, None, "mp"), P("mp", None),
            P("mp", None, None), P(), P("dp", None), P("dp"), P(("dp", "mp"), None),
        ),
        out_specs=(
            P(("dp", "mp"), None), P(("dp", "mp"), None), P(), P(None, None, None, "mp"), P("mp", None, None), P(),
            P(), P(None, None, "mp"), P("mp", None, None), P(),
        ),
        check_vma=False,
    )
```
